32 devices in a mesh: gossip: 8 (over z, x), fsdp: 4 (over y, core).
Axes of the slice: x: 2, y: 2, z: 4, core: 2. Of those that a mesh axis runs over, the one named last changes fastest.
Arguments:
- series: bfloat16 [8, 2, 512, 768], P('gossip', None, 'fsdp'), may hold values from -6 to 6
- cotangent: bfloat16 [8, 2, 512, 768], P('gossip', None, 'fsdp'), may hold values from -6 to 6
- observed: int32 [8, 2, 512], P('gossip', None, 'fsdp'), may hold values 0 or 1
- depth_kernel: float32 [7, 768], replicated, may hold values from -2.5 to 2.5
- norm_gain: float32 [768], replicated, may hold values from 0.1 to 1.9
- layer_scale: float32 [768], replicated, may hold values from 0.5 to 2
- step_index: int32 [1], replicated, may hold values from 0 to 999
- w_expand: bfloat16 [8, 768, 4096], P('gossip', 'fsdp'), may hold values from -4 to 4
- w_project: bfloat16 [8, 4096, 768], P('gossip', 'fsdp'), may hold values from -4 to 4
- first_expand: float32 [8, 768, 4096], P('gossip', 'fsdp'), may hold values from -3 to 3
- second_expand: float32 [8, 768, 4096], P('gossip', 'fsdp'), may hold values from 0.1 to 2
- first_project: float32 [8, 4096, 768], P('gossip', 'fsdp'), may hold values from -3 to 3
- second_project: float32 [8, 4096, 768], P('gossip', 'fsdp'), may hold values from 0.1 to 2
Outputs:
- shared_expand: bfloat16 [8, 768, 4096], P('gossip', 'fsdp')
- shared_project: bfloat16 [8, 4096, 768], P('gossip', 'fsdp')
- first_expand_next: float32 [8, 768, 4096], P('gossip', 'fsdp')
- second_expand_next: float32 [8, 768, 4096], P('gossip', 'fsdp')
- first_project_next: float32 [8, 4096, 768], P('gossip', 'fsdp')
- second_project_next: float32 [8, 4096, 768], P('gossip', 'fsdp')
- input_grad: bfloat16 [8, 2, 512, 768], P('gossip', None, 'fsdp')
The draws below stay inside these ranges and needn't reach their ends.
All inputs are finite; a program needn't handle non-finite values. No bound on the sum of `observed` on one device may be relied on, other than what follows from the above.
Results may differ from the reference program's by a relative error of at most 0.0095.
Values may be sent and summed in bfloat16 or wider, within the bound.
No kernel may reach another device: no remote copies, remote signals or barrier semaphores. Data moves between devices by JAX's collectives and lax.ppermute only.
A program may use at most 128 MiB of HBM per device.

```python
import math
import jax
import jax.numpy as jnp
from jax import lax

D = 768
FF = 4096
KERNEL = 7
SEQS = 2
LENGTH = 512
N_GOSSIP = 8


def plant(entries, own_key, smallest, largest):
    extent = entries.shape
    place = [jax.random.randint(jax.random.fold_in(own_key, axis), (), 0, extent[axis]) for axis in range(len(extent))]
    entries = entries.at[tuple(place)].set(smallest)
    longest = extent.index(max(extent))
    place[longest] = (place[longest] + 1) % extent[longest]
    return entries.at[tuple(place)].set(largest)


def steps_of(rng, extent, shards, low, high):
    def one(axis_at, shards_of):
        draws = jax.random.uniform(jax.random.fold_in(jax.random.fold_in(rng, 6), axis_at), (shards_of,), jnp.float32, low / len(shards), high / len(shards))
        return jnp.repeat(jnp.exp(draws), extent[axis_at] // shards_of).reshape((-1,) + (1,) * (len(extent) - axis_at - 1))

    gain = one(*shards[0])
    for cut in shards[1:]:
        gain = gain * one(*cut)
    return gain


def noise(key, dims, scale, most, pieces=(), held_as=jnp.bfloat16):
    result = jax.random.normal(key, dims, jnp.float32) * scale
    if len(pieces) > 0:
        result = steps_of(key, dims, pieces, -0.22, 0.18) * result
    return jnp.clip(result, min=-most, max=most).astype(held_as)


def setup_inputs(seed: int = 0) -> dict:
    splits = jax.random.split(jax.random.key(seed), 14)
    return {
        "series": noise(splits[0], (N_GOSSIP, SEQS, LENGTH, D), 1.0, 6.0, ((0, 8), (2, 4))),
        "cotangent": noise(splits[1], (N_GOSSIP, SEQS, LENGTH, D), 1.0, 6.0, ((0, 8), (2, 4))),
        "observed": plant((jax.random.randint(splits[2], (N_GOSSIP, SEQS, LENGTH), 0, 4) < 3).astype(jnp.int32), jax.random.fold_in(splits[2], 1), 0, 1),
        "depth_kernel": noise(splits[3], (KERNEL, D), 0.4, 2.5, (), jnp.float32),
        "norm_gain": jnp.clip(1.0 + 0.18 * jax.random.normal(splits[4], (D,), jnp.float32), 0.1, 1.9),
        "layer_scale": jnp.clip(jnp.exp(jax.random.uniform(splits[5], (D,), jnp.float32, math.log(0.5), math.log(2.0))), 0.5, 2.0),
        "step_index": jax.random.randint(splits[6], (1,), 0, 1000).astype(jnp.int32),
        "w_expand": noise(splits[7], (N_GOSSIP, D, FF), 1.0, 4.0, ((0, 8), (1, 4))),
        "w_project": noise(splits[8], (N_GOSSIP, FF, D), 1.0, 4.0, ((0, 8), (1, 4))),
        "first_expand": noise(splits[9], (N_GOSSIP, D, FF), 0.5, 3.0, ((0, 8), (1, 4)), jnp.float32),
        "second_expand": jnp.clip(jnp.exp(math.log(2.0) - 2.9957323 * jax.random.uniform(splits[10], (N_GOSSIP, D, FF), jnp.float32) ** steps_of(splits[10], (N_GOSSIP, D, FF), ((0, 8), (1, 4)), -0.2, 0.2)), 0.1, 2.0),
        "first_project": noise(splits[11], (N_GOSSIP, FF, D), 0.5, 3.0, ((0, 8), (1, 4)), jnp.float32),
        "second_project": jnp.clip(jnp.exp(math.log(2.0) - 2.9957323 * jax.random.uniform(splits[12], (N_GOSSIP, FF, D), jnp.float32) ** steps_of(splits[12], (N_GOSSIP, FF, D), ((0, 8), (1, 4)), -0.2, 0.2)), 0.1, 2.0),
    }


NORM_EPS = 1e-06
ADAM_EPS = 1e-08
BETA_ONE = 0.9
BETA_TWO = 0.999
LEARN_RATE = 0.02
DECAY_RATE = 0.1
HALF_ROOT = 0.7071067811865476
INV_ROOT_TAU = 0.3989422804014327

def gelu_parts(pre_act):
    cumul = 0.5 * (1.0 + jax.scipy.special.erf(pre_act * HALF_ROOT))
    density = jnp.exp(-0.5 * pre_act * pre_act) * INV_ROOT_TAU
    return (pre_act * cumul, cumul + pre_act * density)

def group_grads(series, cotangent, observed, w_expand, w_project, depth_kernel, norm_gain, layer_scale):
    seqs, length, width = series.shape
    hidden_width = w_expand.shape[1]
    taps = depth_kernel.shape[0]
    reach = taps // 2
    scale_in = 1.0 / math.sqrt(width)
    scale_out = 1.0 / math.sqrt(hidden_width)
    padded = jnp.pad(series.astype(jnp.float32), ((0, 0), (reach, reach), (0, 0)))
    conv_out = jnp.zeros((seqs, length, width), jnp.float32)
    for offset in range(taps):
        conv_out = conv_out + depth_kernel[offset] * padded[:, offset:offset + length, :]
    centred = conv_out - lax.optimization_barrier(jnp.mean(conv_out, axis=-1, keepdims=True))
    inv_std = lax.rsqrt(lax.optimization_barrier(jnp.mean(centred * centred, axis=-1, keepdims=True)) + NORM_EPS)
    unit = centred * inv_std
    normed = (unit * norm_gain).astype(jnp.bfloat16)
    norm_rows = normed.reshape(seqs * length, width)
    pre_act = jnp.dot(norm_rows, w_expand, preferred_element_type=jnp.float32) * scale_in
    act_value, act_slope = gelu_parts(pre_act)
    hidden = act_value.astype(jnp.bfloat16)
    masked_cot = cotangent * observed[..., None].astype(jnp.bfloat16)
    branch_grad = (masked_cot.astype(jnp.float32) * layer_scale).astype(jnp.bfloat16).reshape(seqs * length, width)
    grad_hidden = lax.dot_general(branch_grad, w_project, (((1,), (1,)), ((), ())), preferred_element_type=jnp.float32) * scale_out
    grad_pre = (grad_hidden * act_slope).astype(jnp.bfloat16)
    grad_norm = lax.dot_general(grad_pre, w_expand, (((1,), (1,)), ((), ())), preferred_element_type=jnp.float32) * scale_in
    scaled = grad_norm.reshape(seqs, length, width) * norm_gain
    grad_conv = inv_std * (scaled - lax.optimization_barrier(jnp.mean(scaled, axis=-1, keepdims=True)) - unit * lax.optimization_barrier(jnp.mean(scaled * unit, axis=-1, keepdims=True)))
    grad_padded = jnp.pad(grad_conv, ((0, 0), (reach, reach), (0, 0)))
    conv_back = jnp.zeros((seqs, length, width), jnp.float32)
    for offset in range(taps):
        start_at = 2 * reach - offset
        conv_back = conv_back + depth_kernel[offset] * grad_padded[:, start_at:start_at + length, :]
    input_grad = (masked_cot.astype(jnp.float32) + conv_back).astype(jnp.bfloat16)
    grad_expand = lax.dot_general(norm_rows, grad_pre, (((0,), (0,)), ((), ())), preferred_element_type=jnp.float32) * scale_in
    grad_project = lax.dot_general(hidden, branch_grad, (((0,), (0,)), ((), ())), preferred_element_type=jnp.float32) * scale_out
    return (input_grad, grad_expand, grad_project)

def adam_step(weight, first, second, gradient, timestep):
    first_next = BETA_ONE * first + (1.0 - BETA_ONE) * gradient
    second_next = BETA_TWO * second + (1.0 - BETA_TWO) * gradient * gradient
    correct_one = 1.0 - jnp.power(jnp.float32(BETA_ONE), timestep)
    correct_two = 1.0 - jnp.power(jnp.float32(BETA_TWO), timestep)
    weight_f = weight.astype(jnp.float32)
    direction = first_next / correct_one / (jnp.sqrt(second_next / correct_two) + ADAM_EPS)
    updated = (weight_f - LEARN_RATE * (direction + DECAY_RATE * weight_f)).astype(jnp.bfloat16)
    return (updated, first_next, second_next)

def reference(series, cotangent, observed, depth_kernel, norm_gain, layer_scale, step_index, w_expand, w_project, first_expand, second_expand, first_project, second_project):

    def one_group(items):
        return group_grads(items[0], items[1], items[2], items[3], items[4], depth_kernel, norm_gain, layer_scale)
    input_grad, grad_expand, grad_project = lax.map(one_group, (series, cotangent, observed, w_expand, w_project))
    timestep = (step_index[0] + 1).astype(jnp.float32)
    updated_expand, first_expand_next, second_expand_next = adam_step(w_expand, first_expand, second_expand, grad_expand, timestep)
    updated_project, first_project_next, second_project_next = adam_step(w_project, first_project, second_project, grad_project, timestep)
    levels = N_GOSSIP.bit_length() - 1
    level_index = (step_index[0] % levels).astype(jnp.int32)
    distance = jnp.left_shift(jnp.int32(1), level_index).astype(jnp.int32)
    partner_ids = jnp.bitwise_xor(jnp.arange(N_GOSSIP, dtype=jnp.int32), distance).astype(jnp.int32)
    shared_expand = ((updated_expand.astype(jnp.float32) + updated_expand[partner_ids].astype(jnp.float32)) * 0.5).astype(jnp.bfloat16)
    shared_project = ((updated_project.astype(jnp.float32) + updated_project[partner_ids].astype(jnp.float32)) * 0.5).astype(jnp.bfloat16)
    return (shared_expand, shared_project, first_expand_next, second_expand_next, first_project_next, second_project_next, input_grad)
```

```python
from functools import partial
import math

import jax
import jax.numpy as jnp
from jax import lax
from jax.experimental import pallas as pl
from jax.experimental.pallas import tpu as pltpu
from jax.sharding import PartitionSpec as P

NORM_EPS = 1e-06
ADAM_EPS = 1e-08
BETA_ONE = 0.9
BETA_TWO = 0.999
LEARN_RATE = 0.02
DECAY_RATE = 0.1
HALF_ROOT = 0.7071067811865476
INV_ROOT_TAU = 0.3989422804014327
PAD = 8
CHUNKS = 2
F32 = jnp.float32
BF16 = jnp.bfloat16
MIB = 1 << 20


def dims(lhs, rhs):
    return (((lhs,), (rhs,)), ((), ()))


def dot(lhs, rhs, contract=(1, 0)):
    return lax.dot_general(lhs, rhs, dims(*contract), preferred_element_type=F32)


def whole(array):
    rank = len(array.shape)
    return pl.BlockSpec(array.shape, lambda *ids: (0,) * rank)


def hbm():
    return pl.BlockSpec(memory_space=pl.ANY)


def params(limit):
    return pltpu.CompilerParams(vmem_limit_bytes=limit)


def cost(flops, moved):
    return pl.CostEstimate(flops=int(flops), transcendentals=0, bytes_accessed=int(moved))


def xor_perm(value, off):
    count = lax.axis_size("fsdp")
    return lax.ppermute(value, "fsdp", [(i, i ^ off) for i in range(count)])


def gather_xor(own):
    count = lax.axis_size("fsdp")
    pieces = {0: own}
    bit = count // 2
    while bit:
        for off in list(pieces):
            pieces[off ^ bit] = xor_perm(pieces[off], bit)
        bit //= 2
    return [pieces[off] for off in range(count)]


def swap_gossip(value, level):
    count = lax.axis_size("gossip")
    return lax.ppermute(value, "gossip", [(i, i ^ (1 << level)) for i in range(count)])


def slice_kernel(me_ref, w_ref, *outs, count, chunks):
    here = w_ref.shape[1] // count
    part = here // chunks
    for off in range(count):
        for c in range(chunks):
            start = pl.multiple_of((me_ref[0] ^ off) * here + c * part, 128)
            outs[off * chunks + c][...] = w_ref[:, pl.ds(start, part)]


def slice_weights(me, w, count, chunks):
    rows, full = w.shape
    part = full // count // chunks
    shape = jax.ShapeDtypeStruct((rows, part), w.dtype)
    flat = pl.pallas_call(
        partial(slice_kernel, count=count, chunks=chunks),
        out_shape=[shape] * (count * chunks),
        grid_spec=pltpu.PrefetchScalarGridSpec(
            num_scalar_prefetch=1,
            grid=(1,),
            in_specs=[whole(w)],
            out_specs=[whole(shape)] * (count * chunks),
        ),
        compiler_params=params(16 * MIB),
        cost_estimate=cost(0, 4 * rows * full),
        name="slice_weights",
    )(me, w)
    return [[flat[off * chunks + c] for off in range(count)] for c in range(chunks)]


def norm_kernel(me_ref, taps_ref, gain_ref, *refs, count, tile):
    pieces = refs[:count]
    normed_ref, turned_ref, unit_ref, inv_ref, padded = refs[count:]
    off = pl.program_id(0)
    seqs, steps, width = pieces[0].shape
    taps = taps_ref.shape[0]
    reach = taps // 2
    me = me_ref[0]

    @pl.when(off == 0)
    def _():
        edge = jnp.zeros((seqs, PAD, width), F32)
        padded[:, :PAD] = edge
        padded[:, PAD + count * steps :] = edge
        for other in range(count):
            start = pl.multiple_of((me ^ other) * steps + PAD, 8)
            padded[:, pl.ds(start, steps)] = pieces[other][...].astype(F32)

    for s in range(seqs):
        for r in range(steps // tile):
            base = pl.multiple_of((me ^ off) * steps + r * tile, 8)
            window = padded[s, pl.ds(base, tile + 2 * PAD)]
            conv = jnp.zeros((tile, width), F32)
            for j in range(taps):
                low = PAD + j - reach
                conv = conv + taps_ref[j : j + 1] * window[low : low + tile]
            centred = conv - jnp.mean(conv, axis=-1, keepdims=True)
            inv = lax.rsqrt(jnp.mean(centred * centred, axis=-1, keepdims=True) + NORM_EPS)
            unit = centred * inv
            rows = pl.ds(s * steps + r * tile, tile)
            normed_ref[rows] = (unit * gain_ref[...]).astype(BF16)

            @pl.when(off == 0)
            def _():
                unit_ref[rows] = unit
                inv_ref[rows] = jnp.broadcast_to(inv, (tile, 128))

    turned_ref[...] = normed_ref[...].T


def norm_rows(me, pieces, taps, gain):
    count = len(pieces)
    seqs, steps, width = pieces[0].shape
    rows = seqs * steps
    total = count * rows
    return pl.pallas_call(
        partial(norm_kernel, count=count, tile=32),
        out_shape=[
            jax.ShapeDtypeStruct((total, width), BF16),
            jax.ShapeDtypeStruct((width, total), BF16),
            jax.ShapeDtypeStruct((rows, width), F32),
            jax.ShapeDtypeStruct((rows, 128), F32),
        ],
        grid_spec=pltpu.PrefetchScalarGridSpec(
            num_scalar_prefetch=1,
            grid=(count,),
            in_specs=[whole(taps), whole(gain)] + [whole(p) for p in pieces],
            out_specs=[
                pl.BlockSpec((rows, width), lambda i, m: (i, 0)),
                pl.BlockSpec((width, rows), lambda i, m: (0, i)),
                pl.BlockSpec((rows, width), lambda i, m: (0, 0)),
                pl.BlockSpec((rows, 128), lambda i, m: (0, 0)),
            ],
            scratch_shapes=[pltpu.VMEM((seqs, count * steps + 2 * PAD, width), F32)],
        ),
        compiler_params=params(18 * MIB + 14 * total * width // 2),
        cost_estimate=cost(40 * total * width, 8 * total * width),
        name="norm_rows",
    )(me, taps, gain, *pieces)


def adam(weight, first, second, gradient, inv_one, inv_two):
    first_next = BETA_ONE * first + (1.0 - BETA_ONE) * gradient
    second_next = BETA_TWO * second + (1.0 - BETA_TWO) * gradient * gradient
    weight_f = weight.astype(F32)
    direction = first_next * inv_one / (jnp.sqrt(second_next * inv_two) + ADAM_EPS)
    updated = (weight_f - LEARN_RATE * (direction + DECAY_RATE * weight_f)).astype(BF16)
    return updated, first_next, second_next


def join_rows(me, pieces, joined):
    part = pieces[0].shape[0]
    for off, piece in enumerate(pieces):
        start = pl.multiple_of((me ^ off) * part, 16)
        joined[pl.ds(start, part)] = piece[...]


def hidden_kernel(me_ref, corr_ref, normed_ref, w_ref, m_ref, v_ref, *refs, count, chained):
    grads = refs[:count]
    wide = refs[count : 2 * count]
    rest = refs[2 * count + (2 if chained else 0) :]
    updated_ref, first_ref, second_ref, slope_ref, joined = rest
    join_rows(me_ref[0], wide, joined)
    rows = grads[0].shape[0]
    width = normed_ref.shape[1]
    scale_in = 1.0 / math.sqrt(width)
    scale_out = corr_ref[2]
    total = None
    for off in range(count):
        part = pl.ds(off * rows, rows)
        pre = dot(normed_ref[part], joined[...]) * scale_in
        cumul = 0.5 * (1.0 + lax.erf(pre * HALF_ROOT))
        density = jnp.exp(-0.5 * pre * pre) * INV_ROOT_TAU
        hidden = (pre * cumul).astype(BF16)
        slope_ref[part] = (cumul + pre * density).astype(BF16)
        term = dot(hidden, grads[off][...], (0, 0))
        total = term if total is None else total + term
    updated, first, second = adam(
        w_ref[...], m_ref[...], v_ref[...], total * scale_out, corr_ref[0], corr_ref[1]
    )
    updated_ref[...] = updated
    first_ref[...] = first
    second_ref[...] = second


def hidden_chunk(me, corr, c, chunks, normed, w, m, v, grads, wide, previous, block):
    count = len(grads)
    total, width = normed.shape
    owned = w.shape[0]
    part = owned // chunks
    block = min(block, part)
    grid = part // block
    base = c * grid
    row_block = pl.BlockSpec((block, width), lambda f, *_: (base + f, 0))
    chained = previous is not None
    return pl.pallas_call(
        partial(hidden_kernel, count=count, chained=chained),
        out_shape=[
            jax.ShapeDtypeStruct((part, width), BF16),
            jax.ShapeDtypeStruct(m.shape, F32),
            jax.ShapeDtypeStruct(v.shape, F32),
            jax.ShapeDtypeStruct((total, part), BF16),
        ],
        grid_spec=pltpu.PrefetchScalarGridSpec(
            num_scalar_prefetch=2,
            grid=(grid,),
            in_specs=[whole(normed), row_block, row_block, row_block]
            + [whole(g) for g in grads]
            + [pl.BlockSpec((x.shape[0], block), lambda f, *_: (0, f)) for x in wide]
            + ([hbm(), hbm()] if chained else []),
            out_specs=[
                pl.BlockSpec((block, width), lambda f, *_: (f, 0)),
                row_block,
                row_block,
                pl.BlockSpec((total, block), lambda f, *_: (0, f)),
            ],
            scratch_shapes=[pltpu.VMEM((width, block), BF16)],
        ),
        input_output_aliases=(
            {6 + 2 * count: 1, 7 + 2 * count: 2} if chained else {}
        ),
        compiler_params=params(20 * MIB + 5 * total * width * 2),
        cost_estimate=cost(4 * total * width * part, 20 * part * width + 6 * total * width),
        name=f"hidden_chunk_{c}",
    )(me, corr, normed, w, m, v, *grads, *wide, *(previous or ()))


def expand_kernel(me_ref, corr_ref, turned_ref, w_ref, slope_ref, *refs, count):
    grads = refs[:count]
    outs = refs[count : 2 * count]
    pre_ref, scratch = refs[2 * count :]
    rows = grads[0].shape[0]
    width = turned_ref.shape[0]
    scale_in = 1.0 / math.sqrt(width)
    scale_out = corr_ref[2]
    for off in range(count):
        part = pl.ds(off * rows, rows)
        back = dot(grads[off][...], w_ref[...], (1, 1)) * scale_out
        pre_ref[part] = (back * slope_ref[part].astype(F32)).astype(BF16)
    scratch[...] = (dot(turned_ref[...], pre_ref[...]) * scale_in).astype(BF16)
    piece = width // count
    for off in range(count):
        start = pl.multiple_of((me_ref[0] ^ off) * piece, 16)
        outs[off][...] = scratch[pl.ds(start, piece)]


def expand_chunk(me, corr, c, chunks, turned, w, slope, grads, block):
    count = len(grads)
    width, total = turned.shape
    part = w.shape[0] // chunks
    block = min(block, part)
    grid = part // block
    base = c * grid
    piece = width // count
    return pl.pallas_call(
        partial(expand_kernel, count=count),
        out_shape=[jax.ShapeDtypeStruct((piece, part), BF16)] * count
        + [jax.ShapeDtypeStruct((total, part), BF16)],
        grid_spec=pltpu.PrefetchScalarGridSpec(
            num_scalar_prefetch=2,
            grid=(grid,),
            in_specs=[
                whole(turned),
                pl.BlockSpec((block, width), lambda f, *_: (base + f, 0)),
                pl.BlockSpec((total, block), lambda f, *_: (0, f)),
            ]
            + [whole(g) for g in grads],
            out_specs=[pl.BlockSpec((piece, block), lambda f, *_: (0, f))] * count
            + [pl.BlockSpec((total, block), lambda f, *_: (0, f))],
            scratch_shapes=[pltpu.VMEM((width, block), BF16)],
        ),
        compiler_params=params(20 * MIB + 5 * total * width * 2),
        cost_estimate=cost(4 * total * width * part, 4 * part * width + 6 * total * width),
        name=f"expand_chunk_{c}",
    )(me, corr, turned, w, slope, *grads)


def update_kernel(me_ref, corr_ref, w_ref, m_ref, v_ref, *refs, count, chained):
    pieces = refs[:count]
    updated_ref, first_ref, second_ref = refs[count + (2 if chained else 0) :]
    for off in range(count):

        @pl.when(pl.program_id(0) == off)
        def _():
            updated, first, second = adam(
                w_ref[...],
                m_ref[...],
                v_ref[...],
                pieces[off][...].astype(F32),
                corr_ref[0],
                corr_ref[1],
            )
            updated_ref[0] = updated
            first_ref[...] = first
            second_ref[...] = second


def update_chunk(me, corr, c, chunks, w, m, v, pieces, previous):
    count = len(pieces)
    rows, part = pieces[0].shape
    column = pl.BlockSpec((rows, part), lambda i, me, *_: (0, (me[0] ^ i) * chunks + c))
    chained = previous is not None
    return pl.pallas_call(
        partial(update_kernel, count=count, chained=chained),
        out_shape=[
            jax.ShapeDtypeStruct((count, rows, part), BF16),
            jax.ShapeDtypeStruct(m.shape, F32),
            jax.ShapeDtypeStruct(v.shape, F32),
        ],
        grid_spec=pltpu.PrefetchScalarGridSpec(
            num_scalar_prefetch=2,
            grid=(count,),
            in_specs=[column, column, column]
            + [whole(p) for p in pieces]
            + ([hbm(), hbm()] if chained else []),
            out_specs=[
                pl.BlockSpec((1, rows, part), lambda i, *_: (i, 0, 0)),
                column,
                column,
            ],
        ),
        input_output_aliases={5 + count: 1, 6 + count: 2} if chained else {},
        compiler_params=params(24 * MIB),
        cost_estimate=cost(20 * count * rows * part, 22 * count * rows * part),
        name=f"update_chunk_{c}",
    )(me, corr, w, m, v, *pieces, *(previous or ()))


def mean_kernel(me_ref, own_ref, other_ref, *refs):
    out_ref = refs[-1]
    value = (own_ref[...].astype(F32) + other_ref[...].astype(F32)) * 0.5
    out_ref[...] = value.reshape(out_ref.shape).astype(BF16)


def mean_chunk(me, own, other, shape, grid, in_spec, out_spec, previous, name):
    chained = previous is not None
    return pl.pallas_call(
        mean_kernel,
        out_shape=jax.ShapeDtypeStruct(shape, BF16),
        grid_spec=pltpu.PrefetchScalarGridSpec(
            num_scalar_prefetch=1,
            grid=(grid,),
            in_specs=[in_spec, in_spec] + ([hbm()] if chained else []),
            out_specs=out_spec,
        ),
        input_output_aliases={3: 0} if chained else {},
        compiler_params=params(16 * MIB),
        cost_estimate=cost(own.size, 6 * own.size),
        name=name,
    )(me, own, other, *((previous,) if chained else ()))


def rows_kernel(me_ref, *refs, count, chunks):
    pre = refs[:chunks]
    wide = refs[chunks : chunks + chunks * count]
    out_ref = refs[chunks + chunks * count]
    joined = refs[chunks + chunks * count + 1 :]
    width = out_ref.shape[1]

    @pl.when(pl.program_id(0) == 0)
    def _():
        for c in range(chunks):
            join_rows(me_ref[0], wide[c * count : (c + 1) * count], joined[c])

    total = None
    for c in range(chunks):
        term = dot(pre[c][...], joined[c][...], (1, 1))
        total = term if total is None else total + term
    out_ref[...] = (total * (1.0 / math.sqrt(width))).astype(BF16)


def row_grads(me, pre, wide, width):
    chunks = len(pre)
    count = len(wide[0])
    total, part = pre[0].shape
    rows = total // count
    flat = [piece for chunk in wide for piece in chunk]
    return pl.pallas_call(
        partial(rows_kernel, count=count, chunks=chunks),
        out_shape=jax.ShapeDtypeStruct((total, width), BF16),
        grid_spec=pltpu.PrefetchScalarGridSpec(
            num_scalar_prefetch=1,
            grid=(count,),
            in_specs=[pl.BlockSpec((rows, part), lambda i, m: (i, 0))] * chunks
            + [whole(x) for x in flat],
            out_specs=pl.BlockSpec((rows, width), lambda i, m: (i, 0)),
            scratch_shapes=[pltpu.VMEM((width, part), BF16)] * chunks,
        ),
        compiler_params=params(24 * MIB),
        cost_estimate=cost(2 * total * width * part * chunks, 6 * total * width),
        name="row_grads",
    )(me, *pre, *flat)


def norm_back_kernel(gain_ref, unit_ref, inv_ref, *refs, count, steps):
    pieces = refs[:count]
    conv_ref, first_ref, last_ref = refs[count:]
    total = pieces[0][...].astype(F32)
    for piece in pieces[1:]:
        total = total + piece[...].astype(F32)
    scaled = total * gain_ref[...]
    unit = unit_ref[...]
    inv = inv_ref[:, :1]
    grad = inv * (
        scaled
        - jnp.mean(scaled, axis=-1, keepdims=True)
        - unit * jnp.mean(scaled * unit, axis=-1, keepdims=True)
    )
    grad = grad.reshape(conv_ref.shape)
    conv_ref[...] = grad
    first_ref[...] = grad[:, :PAD].astype(BF16)
    last_ref[...] = grad[:, steps - PAD :].astype(BF16)


def norm_back(gain, unit, inv, pieces, seqs, steps):
    count = len(pieces)
    width = unit.shape[1]
    edge = jax.ShapeDtypeStruct((seqs, PAD, width), BF16)
    full = jax.ShapeDtypeStruct((seqs, steps, width), F32)
    return pl.pallas_call(
        partial(norm_back_kernel, count=count, steps=steps),
        out_shape=[full, edge, edge],
        grid=(1,),
        in_specs=[whole(gain), whole(unit), whole(inv)] + [whole(p) for p in pieces],
        out_specs=[whole(full), whole(edge), whole(edge)],
        compiler_params=params(32 * MIB),
        cost_estimate=cost(20 * unit.size, 12 * unit.size),
        name="norm_back",
    )(gain, unit, inv, *pieces)


def conv_back_kernel(taps_ref, grad_ref, low_ref, high_ref, cot_ref, out_ref, padded, *, tile):
    seqs, steps, width = grad_ref.shape
    taps = taps_ref.shape[0]
    reach = taps // 2
    padded[:, :PAD] = low_ref[...].astype(F32)
    padded[:, PAD : PAD + steps] = grad_ref[...]
    padded[:, PAD + steps :] = high_ref[...].astype(F32)
    for s in range(seqs):
        for r in range(steps // tile):
            window = padded[s, r * tile : r * tile + tile + 2 * PAD]
            back = cot_ref[s, r * tile : (r + 1) * tile].astype(F32)
            for j in range(taps):
                low = PAD + reach - j
                back = back + taps_ref[j : j + 1] * window[low : low + tile]
            out_ref[s, r * tile : (r + 1) * tile] = back.astype(BF16)


def conv_back(taps, grad, low, high, cot):
    seqs, steps, width = grad.shape
    return pl.pallas_call(
        partial(conv_back_kernel, tile=32),
        out_shape=jax.ShapeDtypeStruct(cot.shape, BF16),
        grid=(1,),
        in_specs=[whole(x) for x in (taps, grad, low, high, cot)],
        out_specs=whole(cot),
        scratch_shapes=[pltpu.VMEM((seqs, steps + 2 * PAD, width), F32)],
        compiler_params=params(32 * MIB),
        cost_estimate=cost(20 * grad.size, 12 * grad.size),
        name="conv_back",
    )(taps, grad, low, high, cot)


def step(
    series,
    cotangent,
    observed,
    depth_kernel,
    norm_gain,
    layer_scale,
    step_index,
    w_expand,
    w_project,
    first_expand,
    second_expand,
    first_project,
    second_project,
    level,
):
    count = lax.axis_size("fsdp")
    seqs, steps, width = series.shape[1:]
    rows = seqs * steps
    hidden_width = w_expand.shape[2]
    owned = hidden_width // count
    chunks = CHUNKS
    me = lax.axis_index("fsdp").astype(jnp.int32).reshape(1)
    gain = norm_gain.reshape(1, width)
    we, wp = w_expand[0], w_project[0]
    me_ax, ve_ax = first_expand[0], second_expand[0]
    mp_ax, vp_ax = first_project[0], second_project[0]

    timestep = (step_index[0] + 1).astype(F32)
    corr = jnp.stack(
        [
            1.0 / (1.0 - jnp.power(F32(BETA_ONE), timestep)),
            1.0 / (1.0 - jnp.power(F32(BETA_TWO), timestep)),
            F32(1.0 / math.sqrt(hidden_width)),
        ]
    )

    series_pieces = gather_xor(series[0])
    masked = cotangent[0] * observed[0][..., None].astype(BF16)
    branch = (masked.astype(F32) * layer_scale).astype(BF16).reshape(rows, width)
    grads = gather_xor(branch)
    sliced = slice_weights(me, we, count, chunks)
    wide = [
        [sliced[c][0]] + [xor_perm(sliced[c][off], off) for off in range(1, count)]
        for c in range(chunks)
    ]
    normed, turned, unit, inv = norm_rows(me, series_pieces, depth_kernel, gain)

    project_pairs = []
    expand_pairs = []
    pre = []
    moments = None
    for c in range(chunks):
        updated, first, second, slope = hidden_chunk(
            me, corr, c, chunks, normed, wp, mp_ax, vp_ax, grads, wide[c], moments, 256
        )
        moments = (first, second)
        project_pairs.append((updated, swap_gossip(updated, level)))
        *parts, pre_c = expand_chunk(me, corr, c, chunks, turned, wp, slope, grads, 256)
        pre.append(pre_c)
        expand_pairs.append([parts[0]] + [xor_perm(parts[off], off) for off in range(1, count)])
    first_project_next, second_project_next = moments

    moments = None
    for c in range(chunks):
        updated, first, second = update_chunk(
            me, corr, c, chunks, we, me_ax, ve_ax, expand_pairs[c], moments
        )
        moments = (first, second)
        expand_pairs[c] = (updated, swap_gossip(updated, level))
    first_expand_next, second_expand_next = moments

    back = row_grads(me, pre, wide, width)
    back_pieces = [back[:rows]] + [
        xor_perm(back[off * rows : (off + 1) * rows], off) for off in range(1, count)
    ]
    grad_conv, first_rows, last_rows = norm_back(gain, unit, inv, back_pieces, seqs, steps)
    forward = [(i, i + 1) for i in range(count - 1)]
    backward = [(target, source) for source, target in forward]
    low = lax.ppermute(last_rows, "fsdp", forward)
    high = lax.ppermute(first_rows, "fsdp", backward)
    input_grad = conv_back(depth_kernel, grad_conv, low, high, masked)

    part = owned // chunks
    shared_project = None
    for c, (own, other) in enumerate(project_pairs):
        shared_project = mean_chunk(
            me,
            own,
            other,
            wp.shape,
            1,
            pl.BlockSpec((part, width), lambda i, m: (0, 0)),
            pl.BlockSpec((part, width), lambda i, m, c=c: (c, 0)),
            shared_project,
            f"mean_project_{c}",
        )
    shared_expand = None
    for c, (own, other) in enumerate(expand_pairs):
        shared_expand = mean_chunk(
            me,
            own,
            other,
            we.shape,
            count,
            pl.BlockSpec((1, width // count, part), lambda i, m: (i, 0, 0)),
            pl.BlockSpec(
                (width // count, part), lambda i, m, c=c: (0, (m[0] ^ i) * chunks + c)
            ),
            shared_expand,
            f"mean_expand_{c}",
        )
    return (
        shared_expand[None],
        shared_project[None],
        first_expand_next[None],
        second_expand_next[None],
        first_project_next[None],
        second_project_next[None],
        input_grad[None],
    )


def body(*args):
    step_index = args[6]
    levels = lax.axis_size("gossip").bit_length() - 1
    return lax.switch(
        step_index[0] % levels,
        [lambda *a, level=level: step(*a, level) for level in range(levels)],
        *args,
    )


def solution(mesh):
    rows = P("gossip", "fsdp", None)
    steps = P("gossip", None, "fsdp", None)
    in_specs = (steps, steps, P("gossip", None, "fsdp"), P(), P(), P(), P()) + (rows,) * 6
    out_specs = (rows,) * 6 + (steps,)
    return jax.shard_map(body, mesh=mesh, in_specs=in_specs, out_specs=out_specs, check_vma=False)
```

```python
from functools import partial
import math

import jax
import jax.numpy as jnp
from jax import lax
from jax.experimental import pallas as pl
from jax.experimental.pallas import tpu as pltpu
from jax.sharding import PartitionSpec as P

NORM_EPS = 1e-06
ADAM_EPS = 1e-08
BETA_ONE = 0.9
BETA_TWO = 0.999
LEARN_RATE = 0.02
DECAY_RATE = 0.1
HALF_ROOT = 0.7071067811865476
INV_ROOT_TAU = 0.3989422804014327
PAD = 8
BLOCK = 256
F32 = jnp.float32
BF16 = jnp.bfloat16
MIB = 1 << 20


def dims(lhs, rhs):
    return (((lhs,), (rhs,)), ((), ()))


def dot(lhs, rhs, contract=(1, 0)):
    return lax.dot_general(lhs, rhs, dims(*contract), preferred_element_type=F32)


def whole(array):
    rank = len(array.shape)
    return pl.BlockSpec(array.shape, lambda *ids: (0,) * rank)


def hbm():
    return pl.BlockSpec(memory_space=pl.ANY)


def params(limit):
    return pltpu.CompilerParams(vmem_limit_bytes=limit)


def cost(moved=1):
    return pl.CostEstimate(flops=1, transcendentals=0, bytes_accessed=moved)


def loop(count, body, unroll=False):
    if count > 4 or not unroll:
        lax.fori_loop(0, count, lambda i, carry: (body(i), carry)[1], 0)
    else:
        for i in range(count):
            body(i)


def row_range(i, rows):
    return pl.ds(i * rows if isinstance(i, int) else pl.multiple_of(i * rows, rows), rows)


def ranges(sizes):
    starts = [sum(sizes[:i]) for i in range(len(sizes))]
    return list(zip(starts, sizes))


def plan(owned):
    if owned % 1024 == 0:
        q = owned // 4
        return ranges([2 * q, 2 * q]), ranges([q] * 4), ranges([2 * q, 2 * q])
    half = owned // 2
    return ranges([owned]), ranges([half, half]), ranges([owned])


def xor_perm(value, off):
    count = lax.axis_size("fsdp")
    return lax.ppermute(value, "fsdp", [(i, i ^ off) for i in range(count)])


def gather_xor(own, hold=()):
    count = lax.axis_size("fsdp")
    pieces = {0: own}
    bit = count // 2
    while bit:
        for off in list(pieces):
            value = pieces[off]
            if off and len(hold):
                value = lax.optimization_barrier((value, *hold))[0]
            pieces[off ^ bit] = xor_perm(value, bit)
        bit //= 2
    return [pieces[off] for off in range(count)]


def send_packs(packs):
    return [xor_perm(pack, 2 * h) if h else pack for h, pack in enumerate(packs)]


def relay_packs(packs, hold=()):
    held = []
    for h, pack in enumerate(packs):
        out = lax.optimization_barrier((pack, *hold))[0] if h and len(hold) else pack
        held += [pack, xor_perm(out, 1)]
    return held


def pieces_of(held, base, spans, k):
    return [(array, base + off % 2 * spans + k) for off, array in enumerate(held)]


def swap_blocks(blocks):
    return [block if off == 0 else xor_perm(block, off) for off, block in enumerate(blocks)]


def swap_gossip(value, level):
    count = lax.axis_size("gossip")
    return lax.ppermute(value, "gossip", [(i, i ^ (1 << level)) for i in range(count)])


def token_kernel(*refs):
    refs[-1][...] = jnp.zeros(refs[-1].shape, F32)


def token(value, name):
    shape = jax.ShapeDtypeStruct((8, 128), F32)
    return pl.pallas_call(
        token_kernel,
        out_shape=shape,
        in_specs=[hbm()],
        out_specs=pl.BlockSpec(memory_space=pltpu.VMEM),
        compiler_params=params(MIB),
        cost_estimate=cost(40 * MIB),
        name=name,
    )(value)


def slice_kernel(me_ref, *refs, count):
    outs = refs[-(count // 2) :]
    rows = refs[0].shape[0]
    for off in range(count):
        low = off % 2 * rows
        outs[off // 2][low : low + rows] = refs[off][...]


def slice_specs(rows, full, count, span):
    start, size = span
    ratio = full // count // size
    base = start // size
    return [
        pl.BlockSpec((rows, size), lambda i, me, off=off: (0, (me[0] ^ off) * ratio + base))
        for off in range(count)
    ]


def slice_weights(me, w, count, span):
    rows, full = w.shape
    shape = jax.ShapeDtypeStruct((2 * rows, span[1]), w.dtype)
    return pl.pallas_call(
        partial(slice_kernel, count=count),
        out_shape=[shape] * (count // 2),
        grid_spec=pltpu.PrefetchScalarGridSpec(
            num_scalar_prefetch=1,
            grid=(1,),
            in_specs=slice_specs(rows, full, count, span),
            out_specs=[whole(shape)] * (count // 2),
        ),
        compiler_params=params(16 * MIB),
        cost_estimate=cost(),
        name=f"slice_{span[0]}",
    )(me, *[w] * count)


def pack_kernel(me_ref, cot_ref, seen_ref, scale_ref, *refs, count):
    *outs, masked_ref = refs[-(count // 2) - 1 :]
    blocks = refs[: -(count // 2) - 1]
    spans = len(blocks) // count
    rows, width = cot_ref.shape
    part, size = blocks[0].shape
    panels = width // size
    masked = (cot_ref[...].astype(F32) * seen_ref[...]).astype(BF16)
    masked_ref[...] = masked
    branch = (masked.astype(F32) * scale_ref[...]).astype(BF16)
    for out in outs:
        for p in range(panels):
            out[p * rows : (p + 1) * rows] = branch[:, p * size : (p + 1) * size]
    for off in range(count):
        for k in range(spans):
            low = panels * rows + (off % 2 * spans + k) * part
            outs[off // 2][low : low + part] = blocks[k * count + off][...]


def pack_first(me, cot, seen, scale, w, count, spans):
    rows, width = cot.shape
    part, full = w.shape
    size = spans[0][1]
    shape = jax.ShapeDtypeStruct((width // size * rows + 2 * len(spans) * part, size), BF16)
    *packs, masked = pl.pallas_call(
        partial(pack_kernel, count=count),
        out_shape=[shape] * (count // 2) + [jax.ShapeDtypeStruct(cot.shape, BF16)],
        grid_spec=pltpu.PrefetchScalarGridSpec(
            num_scalar_prefetch=1,
            grid=(1,),
            in_specs=[whole(cot), whole(seen), whole(scale)]
            + [spec for span in spans for spec in slice_specs(part, full, count, span)],
            out_specs=[whole(shape)] * (count // 2) + [whole(cot)],
        ),
        compiler_params=params(24 * MIB),
        cost_estimate=cost(),
        name="pack_first",
    )(me, cot, seen, scale, *[w] * (count * len(spans)))
    return packs, masked


def norm_kernel(me_ref, taps_ref, gain_ref, *refs, count, tile):
    pieces = refs[:count]
    normed_ref, turned_ref, unit_ref, inv_ref, padded = refs[-5:]
    off = pl.program_id(0)
    seqs, steps, width = pieces[0].shape
    taps = taps_ref.shape[0]
    reach = taps // 2
    me = me_ref[0]

    @pl.when(off == 0)
    def _():
        edge = jnp.zeros((seqs, PAD, width), F32)
        padded[:, :PAD] = edge
        padded[:, PAD + count * steps :] = edge
        for other in range(count):
            start = pl.multiple_of((me ^ other) * steps + PAD, 8)
            padded[:, pl.ds(start, steps)] = pieces[other][...].astype(F32)

    def body(i, carry):
        s = i // (steps // tile)
        r = i % (steps // tile)
        base = pl.multiple_of((me ^ off) * steps + r * tile, 8)
        window = padded.at[s, pl.ds(base, tile + 2 * PAD)]
        conv = jnp.zeros((tile, width), F32)
        for j in range(taps):
            low = PAD + j - reach
            conv = conv + taps_ref[j : j + 1] * window[low : low + tile]
        centred = conv - jnp.mean(conv, axis=-1, keepdims=True)
        inv = lax.rsqrt(jnp.mean(centred * centred, axis=-1, keepdims=True) + NORM_EPS)
        unit = centred * inv
        rows = pl.ds(pl.multiple_of(i * tile, tile), tile)
        normed_ref[rows] = (unit * gain_ref[...]).astype(BF16)

        @pl.when(off == 0)
        def _():
            unit_ref[rows] = unit
            inv_ref[rows] = jnp.broadcast_to(inv, (tile, 128))

        return carry

    lax.fori_loop(0, seqs * steps // tile, body, 0)
    turned_ref[...] = normed_ref[...].T


def norm_rows(me, pieces, taps, gain, after):
    count = len(pieces)
    seqs, steps, width = pieces[0].shape
    rows = seqs * steps
    total = count * rows
    return pl.pallas_call(
        partial(norm_kernel, count=count, tile=math.gcd(steps, 128)),
        out_shape=[
            jax.ShapeDtypeStruct((total, width), BF16),
            jax.ShapeDtypeStruct((width, total), BF16),
            jax.ShapeDtypeStruct((rows, width), F32),
            jax.ShapeDtypeStruct((rows, 128), F32),
        ],
        grid_spec=pltpu.PrefetchScalarGridSpec(
            num_scalar_prefetch=1,
            grid=(count,),
            in_specs=[whole(taps), whole(gain)]
            + [whole(p) for p in pieces]
            + [hbm()] * len(after),
            out_specs=[
                pl.BlockSpec((rows, width), lambda i, m: (i, 0)),
                pl.BlockSpec((width, rows), lambda i, m: (0, i)),
                pl.BlockSpec((rows, width), lambda i, m: (0, 0)),
                pl.BlockSpec((rows, 128), lambda i, m: (0, 0)),
            ],
            scratch_shapes=[pltpu.VMEM((seqs, count * steps + 2 * PAD, width), F32)],
        ),
        compiler_params=params(18 * MIB + 14 * total * width // 2),
        cost_estimate=cost(40 * MIB),
        name="norm_rows",
    )(me, taps, gain, *pieces, *after)


def adam(weight, first, second, gradient, inv_one, inv_two):
    first_next = BETA_ONE * first + (1.0 - BETA_ONE) * gradient
    second_next = BETA_TWO * second + (1.0 - BETA_TWO) * gradient * gradient
    weight_f = weight.astype(F32)
    direction = first_next * inv_one / (jnp.sqrt(second_next * inv_two) + ADAM_EPS)
    updated = (weight_f - LEARN_RATE * (direction + DECAY_RATE * weight_f)).astype(BF16)
    return updated, first_next, second_next


def adam_tiles(w_ref, m_ref, v_ref, gradient, corr_ref, updated_ref, first_ref, second_ref, tile):
    def body(i, carry):
        rows = pl.ds(pl.multiple_of(i * tile, tile), tile)
        updated, first, second = adam(
            w_ref[rows], m_ref[rows], v_ref[rows], gradient(rows), corr_ref[0], corr_ref[1]
        )
        updated_ref[rows] = updated
        first_ref[rows] = first
        second_ref[rows] = second
        return carry

    lax.fori_loop(0, w_ref.shape[0] // tile, body, 0)


def join_rows(me, pieces, joined, columns=slice(None)):
    part = pieces[0].shape[0]
    for off, piece in enumerate(pieces):
        start = pl.multiple_of((me ^ off) * part, 16)
        joined[pl.ds(start, part), columns] = piece[...]


def hidden_kernel(me_ref, corr_ref, normed_ref, w_ref, m_ref, v_ref, *refs, count, first):
    wide = refs[:count]
    if first:
        packs = refs[count : 2 * count]
        updated_ref, first_ref, second_ref, slope_ref, grads_ref, joined, total = refs[-7:]
    else:
        grads_ref = refs[count]
        updated_ref, first_ref, second_ref, slope_ref, joined, total = refs[-6:]
    join_rows(me_ref[0], wide, joined)
    width = normed_ref.shape[1]
    rows = normed_ref.shape[0] // count
    scale_in = 1.0 / math.sqrt(width)
    if first:
        size = packs[0].shape[1]
        for off in range(count):
            for p in range(width // size):
                grads_ref[off * rows : (off + 1) * rows, p * size : (p + 1) * size] = packs[off][
                    p * rows : (p + 1) * rows
                ]
    total[...] = jnp.zeros(total.shape, F32)

    def body(off):
        part = row_range(off, rows)
        pre = dot(normed_ref[part], joined[...]) * scale_in
        cumul = 0.5 * (1.0 + lax.erf(pre * HALF_ROOT))
        density = jnp.exp(-0.5 * pre * pre) * INV_ROOT_TAU
        hidden = (pre * cumul).astype(BF16)
        slope_ref[part] = (cumul + pre * density).astype(BF16)
        total[...] += dot(hidden, grads_ref[part], (0, 0))

    loop(count, body, first)
    adam_tiles(
        w_ref,
        m_ref,
        v_ref,
        lambda rows: total[rows] * corr_ref[2],
        corr_ref,
        updated_ref,
        first_ref,
        second_ref,
        32,
    )


def hidden_chunk(me, corr, span, normed, grads, w, m, v, wide, low, previous, after):
    count = len(wide)
    total, width = normed.shape
    owned, part = w.shape[0], width // count
    start, size = span
    block = min(BLOCK, size)
    base = start // block
    rows = total // count
    row_block = pl.BlockSpec((block, width), lambda f, *_: (base + f, 0))
    arrays = [array for array, _ in wide]
    wide_specs = [
        pl.BlockSpec((part, block), lambda f, *_, lead=lead: (lead, low // block + f))
        for _, lead in wide
    ]
    if grads is None:
        spread = width // size * rows
        more = [pl.BlockSpec((spread, size), lambda f, *_: (0, 0))] * count
        extra = arrays
        out_grads = [jax.ShapeDtypeStruct((total, width), BF16)]
    else:
        more = [whole(grads)]
        extra = [grads]
        out_grads = []
    chained = previous is not None
    last = 6 + count + len(extra)
    return pl.pallas_call(
        partial(hidden_kernel, count=count, first=grads is None),
        out_shape=[
            jax.ShapeDtypeStruct((size, width), BF16),
            jax.ShapeDtypeStruct(m.shape, F32),
            jax.ShapeDtypeStruct(v.shape, F32),
            jax.ShapeDtypeStruct((total, owned), BF16),
        ]
        + out_grads,
        grid_spec=pltpu.PrefetchScalarGridSpec(
            num_scalar_prefetch=2,
            grid=(size // block,),
            in_specs=[whole(normed), row_block, row_block, row_block]
            + wide_specs
            + more
            + ([hbm()] * 3 if chained else [])
            + [hbm()] * len(after),
            out_specs=[
                pl.BlockSpec((block, width), lambda f, *_: (f, 0)),
                row_block,
                row_block,
                pl.BlockSpec((total, block), lambda f, *_: (0, base + f)),
            ]
            + [whole(g) for g in out_grads],
            scratch_shapes=[pltpu.VMEM((width, block), BF16), pltpu.VMEM((block, width), F32)],
        ),
        input_output_aliases={last: 1, last + 1: 2, last + 2: 3} if chained else {},
        compiler_params=params(20 * MIB + 5 * total * width * 2),
        cost_estimate=cost(),
        name=f"hidden_{start}",
    )(me, corr, normed, w, m, v, *arrays, *extra, *(previous or ()), *after)


def expand_kernel(me_ref, corr_ref, turned_ref, grads_ref, w_ref, slope_ref, *refs, count):
    *outs, pre_ref, scratch = refs[-count - 2 :]
    width = turned_ref.shape[0]
    rows = grads_ref.shape[0] // count
    scale_in = 1.0 / math.sqrt(width)

    def body(off):
        part = row_range(off, rows)
        back = dot(grads_ref[part], w_ref[...], (1, 1)) * corr_ref[2]
        pre_ref[part] = (back * slope_ref[part].astype(F32)).astype(BF16)

    loop(count, body)
    scratch[...] = (dot(turned_ref[...], pre_ref[...]) * scale_in).astype(BF16)
    piece = width // count
    for off in range(count):
        start = pl.multiple_of((me_ref[0] ^ off) * piece, 16)
        outs[off][...] = scratch[pl.ds(start, piece)]


def expand_chunk(me, corr, span, turned, grads, w, slope, count, after):
    width, total = turned.shape
    start, size = span
    block = min(BLOCK, size)
    base = start // block
    piece = width // count
    return pl.pallas_call(
        partial(expand_kernel, count=count),
        out_shape=[jax.ShapeDtypeStruct((piece, size), BF16)] * count
        + [jax.ShapeDtypeStruct((total, size), BF16)],
        grid_spec=pltpu.PrefetchScalarGridSpec(
            num_scalar_prefetch=2,
            grid=(size // block,),
            in_specs=[
                whole(turned),
                whole(grads),
                pl.BlockSpec((block, width), lambda f, *_: (base + f, 0)),
                pl.BlockSpec((total, block), lambda f, *_: (0, base + f)),
            ]
            + [hbm()] * len(after),
            out_specs=[pl.BlockSpec((piece, block), lambda f, *_: (0, f))] * count
            + [pl.BlockSpec((total, block), lambda f, *_: (0, f))],
            scratch_shapes=[pltpu.VMEM((width, block), BF16)],
        ),
        compiler_params=params(20 * MIB + 5 * total * width * 2),
        cost_estimate=cost(),
        name=f"expand_{start}",
    )(me, corr, turned, grads, w, slope, *after)


def update_kernel(me_ref, corr_ref, w_ref, m_ref, v_ref, *refs, count):
    pieces = refs[:count]
    updated_ref, first_ref, second_ref, held = refs[-4:]
    for off in range(count):

        @pl.when(pl.program_id(0) == off)
        def _():
            held[...] = pieces[off][...]

    adam_tiles(
        w_ref,
        m_ref,
        v_ref,
        lambda rows: held[rows].astype(F32),
        corr_ref,
        updated_ref.at[0],
        first_ref,
        second_ref,
        48,
    )


def update_chunk(me, corr, span, w, m, v, pieces, previous, after):
    count = len(pieces)
    rows, size = pieces[0].shape
    start, _ = span
    ratio = w.shape[1] // count // size
    base = start // size
    column = pl.BlockSpec((rows, size), lambda i, me, *_: (0, (me[0] ^ i) * ratio + base))
    chained = previous is not None
    last = 5 + count
    return pl.pallas_call(
        partial(update_kernel, count=count),
        out_shape=[
            jax.ShapeDtypeStruct((count, rows, size), BF16),
            jax.ShapeDtypeStruct(m.shape, F32),
            jax.ShapeDtypeStruct(v.shape, F32),
        ],
        grid_spec=pltpu.PrefetchScalarGridSpec(
            num_scalar_prefetch=2,
            grid=(count,),
            in_specs=[column, column, column]
            + [whole(p) for p in pieces]
            + ([hbm()] * 2 if chained else [])
            + [hbm()] * len(after),
            out_specs=[
                pl.BlockSpec((1, rows, size), lambda i, *_: (i, 0, 0)),
                column,
                column,
            ],
            scratch_shapes=[pltpu.VMEM((rows, size), BF16)],
        ),
        input_output_aliases={last: 1, last + 1: 2} if chained else {},
        compiler_params=params(24 * MIB),
        cost_estimate=cost(),
        name=f"update_{start}",
    )(me, corr, w, m, v, *pieces, *(previous or ()), *after)


def mean_tiles(own_ref, other_ref, out_ref):
    rows = out_ref.shape[0]
    tile = math.gcd(rows, 64)

    def body(i, carry):
        part = pl.ds(pl.multiple_of(i * tile, tile), tile)
        value = (own_ref[part].astype(F32) + other_ref[part].astype(F32)) * 0.5
        out_ref[part] = value.astype(BF16)
        return carry

    lax.fori_loop(0, rows // tile, body, 0)


def mean_project_kernel(*refs, parts):
    out_ref = refs[-1]
    for i, (start, size) in enumerate(parts):
        mean_tiles(refs[2 * i], refs[2 * i + 1], out_ref.at[pl.ds(start, size)])


def mean_project(pairs, parts):
    flat = [x for pair in pairs for x in pair]
    shape = jax.ShapeDtypeStruct((sum(p[0].shape[0] for p in pairs), flat[0].shape[1]), BF16)
    return pl.pallas_call(
        partial(mean_project_kernel, parts=parts),
        out_shape=shape,
        grid=(1,),
        in_specs=[whole(x) for x in flat],
        out_specs=whole(shape),
        compiler_params=params(24 * MIB),
        cost_estimate=cost(),
        name="mean_project",
    )(*flat)


def mean_expand_kernel(me_ref, own_ref, other_ref, *refs):
    mean_tiles(own_ref.at[0], other_ref.at[0], refs[-1])


def mean_expand(me, span, own, other, full, previous, after):
    count, rows, size = own.shape
    ratio = full // count // size
    base = span[0] // size
    in_spec = pl.BlockSpec((1, rows, size), lambda i, m: (i, 0, 0))
    chained = previous is not None
    return pl.pallas_call(
        mean_expand_kernel,
        out_shape=pltpu.HBM((rows, full), BF16),
        grid_spec=pltpu.PrefetchScalarGridSpec(
            num_scalar_prefetch=1,
            grid=(count,),
            in_specs=[in_spec, in_spec] + [hbm()] * (chained + len(after)),
            out_specs=pl.BlockSpec((rows, size), lambda i, m: (0, (m[0] ^ i) * ratio + base)),
        ),
        input_output_aliases={3: 0} if chained else {},
        compiler_params=params(16 * MIB),
        cost_estimate=cost(),
        name=f"mean_expand_{span[0]}",
    )(me, own, other, *((previous,) if chained else ()), *after)


def rows_kernel(me_ref, *refs, count, groups, parts):
    pre = refs[:groups]
    wide = refs[groups : groups + len(parts) * count]
    *outs, joined = refs[-count - 1 :]
    width = joined.shape[0]

    @pl.when(pl.program_id(0) == 0)
    def _():
        for i, (start, size) in enumerate(parts):
            pieces = wide[i * count : (i + 1) * count]
            join_rows(me_ref[0], pieces, joined, slice(start, start + size))

    total = None
    low = 0
    for piece in pre:
        size = piece.shape[1]
        term = dot(piece[...], joined[:, low : low + size], (1, 1))
        total = term if total is None else total + term
        low += size
    total = (total * (1.0 / math.sqrt(width))).astype(BF16)
    for off in range(count):

        @pl.when(pl.program_id(0) == off)
        def _():
            outs[off][...] = total


def row_grads(me, pre, wide, parts, width, after):
    count = len(wide[0])
    total = pre[0].shape[0]
    rows = total // count
    owned = sum(p.shape[1] for p in pre)
    flat = [piece for chunk in wide for piece in chunk]
    shapes = [jax.ShapeDtypeStruct((rows, width), BF16)] * count
    return pl.pallas_call(
        partial(rows_kernel, count=count, groups=len(pre), parts=parts),
        out_shape=shapes,
        grid_spec=pltpu.PrefetchScalarGridSpec(
            num_scalar_prefetch=1,
            grid=(count,),
            in_specs=[pl.BlockSpec((rows, p.shape[1]), lambda i, m: (i, 0)) for p in pre]
            + [
                pl.BlockSpec((width // count, x.shape[1]), lambda i, m, lead=lead: (lead, 0))
                for x, lead in flat
            ]
            + [hbm()] * len(after),
            out_specs=[whole(x) for x in shapes],
            scratch_shapes=[pltpu.VMEM((width, owned), BF16)],
        ),
        compiler_params=params(24 * MIB),
        cost_estimate=cost(),
        name="row_grads",
    )(me, *pre, *[x for x, _ in flat], *after)


def norm_back_kernel(gain_ref, unit_ref, inv_ref, *refs, count, steps, tile):
    pieces = refs[:count]
    conv_ref, first_ref, last_ref = refs[-3:]

    def body(i, carry):
        rows = pl.ds(pl.multiple_of(i * tile, tile), tile)
        total = pieces[0][rows].astype(F32)
        for piece in pieces[1:]:
            total = total + piece[rows].astype(F32)
        scaled = total * gain_ref[...]
        unit = unit_ref[rows]
        conv_ref[rows] = inv_ref[rows, :1] * (
            scaled
            - jnp.mean(scaled, axis=-1, keepdims=True)
            - unit * jnp.mean(scaled * unit, axis=-1, keepdims=True)
        )
        return carry

    lax.fori_loop(0, conv_ref.shape[0] // tile, body, 0)
    for s in range(first_ref.shape[0]):
        first_ref[s] = conv_ref[s * steps : s * steps + PAD].astype(BF16)
        last_ref[s] = conv_ref[(s + 1) * steps - PAD : (s + 1) * steps].astype(BF16)


def norm_back(gain, unit, inv, pieces, seqs, steps, after):
    count = len(pieces)
    width = unit.shape[1]
    edge = jax.ShapeDtypeStruct((seqs, PAD, width), BF16)
    full = jax.ShapeDtypeStruct((seqs * steps, width), F32)
    return pl.pallas_call(
        partial(norm_back_kernel, count=count, steps=steps, tile=32),
        out_shape=[full, edge, edge],
        grid=(1,),
        in_specs=[whole(gain), whole(unit), whole(inv)]
        + [whole(p) for p in pieces]
        + [hbm()] * len(after),
        out_specs=[whole(full), whole(edge), whole(edge)],
        compiler_params=params(32 * MIB),
        cost_estimate=cost(),
        name="norm_back",
    )(gain, unit, inv, *pieces, *after)


def conv_back_kernel(taps_ref, grad_ref, low_ref, high_ref, cot_ref, out_ref, padded, *, tile):
    seqs, steps, width = out_ref.shape
    taps = taps_ref.shape[0]
    reach = taps // 2
    for s in range(seqs):
        padded[s, :PAD] = low_ref[s].astype(F32)
        padded[s, PAD + steps :] = high_ref[s].astype(F32)

    def fill(i, carry):
        s = i // (steps // tile)
        r = i % (steps // tile)
        rows = pl.ds(pl.multiple_of(i * tile, tile), tile)
        padded[s, pl.ds(pl.multiple_of(r * tile + PAD, 8), tile)] = grad_ref[rows]
        return carry

    def body(i, carry):
        s = i // (steps // tile)
        r = i % (steps // tile)
        rows = pl.ds(pl.multiple_of(r * tile, tile), tile)
        window = padded.at[s, pl.ds(pl.multiple_of(r * tile, 8), tile + 2 * PAD)]
        back = cot_ref[pl.ds(pl.multiple_of(i * tile, tile), tile)].astype(F32)
        for j in range(taps):
            low = PAD + reach - j
            back = back + taps_ref[j : j + 1] * window[low : low + tile]
        out_ref[s, rows] = back.astype(BF16)
        return carry

    lax.fori_loop(0, seqs * steps // tile, fill, 0)
    lax.fori_loop(0, seqs * steps // tile, body, 0)


def conv_back(taps, grad, low, high, cot, seqs):
    total, width = cot.shape
    steps = total // seqs
    shape = jax.ShapeDtypeStruct((seqs, steps, width), BF16)
    return pl.pallas_call(
        partial(conv_back_kernel, tile=32),
        out_shape=shape,
        grid=(1,),
        in_specs=[whole(x) for x in (taps, grad, low, high, cot)],
        out_specs=whole(shape),
        scratch_shapes=[pltpu.VMEM((seqs, steps + 2 * PAD, width), F32)],
        compiler_params=params(32 * MIB),
        cost_estimate=cost(),
        name="conv_back",
    )(taps, grad, low, high, cot)


def step(
    series,
    cotangent,
    observed,
    depth_kernel,
    norm_gain,
    layer_scale,
    step_index,
    w_expand,
    w_project,
    first_expand,
    second_expand,
    first_project,
    second_project,
    level,
):
    count = lax.axis_size("fsdp")
    seqs, steps, width = series.shape[1:]
    rows = seqs * steps
    hidden_width = w_expand.shape[2]
    owned = hidden_width // count
    sent, parts, groups = plan(owned)
    me = lax.axis_index("fsdp").astype(jnp.int32).reshape(1)
    gain = norm_gain.reshape(1, width)
    we, wp = w_expand[0], w_project[0]
    me_ax, ve_ax = first_expand[0], second_expand[0]
    mp_ax, vp_ax = first_project[0], second_project[0]

    timestep = (step_index[0] + 1).astype(F32)
    corr = jnp.stack(
        [
            1.0 / (1.0 - jnp.power(F32(BETA_ONE), timestep)),
            1.0 / (1.0 - jnp.power(F32(BETA_TWO), timestep)),
            F32(1.0 / math.sqrt(hidden_width)),
        ]
    )

    part = width // count
    first_spans = [span for span in parts if sum(span) <= sum(sent[0])]
    spans = first_spans + list(sent[1:])
    seen = observed[0].reshape(rows, 1).astype(F32)
    cot = cotangent[0].reshape(rows, width)
    packs, masked = pack_first(
        me, cot, seen, layer_scale.reshape(1, width), we, count, first_spans
    )
    series_pieces = gather_xor(series[0], (packs[0],))
    normed, turned, unit, inv = norm_rows(me, series_pieces, depth_kernel, gain, ())
    base = width // parts[0][1] * rows // part
    held = relay_packs(send_packs(packs), (normed,))
    wide = [pieces_of(held, base, len(first_spans), k) for k in range(len(first_spans))]
    received = [send_packs(slice_weights(me, we, count, span)) for span in sent[1:]]

    project_pairs = []
    expand_pairs = []
    pre = []
    carried = None
    grads = None
    done = 0
    pending = list(groups)
    for i, (start, size) in enumerate(parts):
        if i == 0:
            after = ()
        elif i == 2:
            after = (token(project_pairs[0][1], "first_arrived"), *pre)
        else:
            after = ()
        at = max(j for j, (low, _) in enumerate(spans) if low <= start)
        low = start - spans[at][0]
        updated, *carried = hidden_chunk(
            me, corr, (start, size), normed, grads, wp, mp_ax, vp_ax, wide[at], low, carried, after
        )
        if i == 0:
            grads = carried.pop()
        if i == 1:
            wide += [pieces_of(relay_packs(packs, (updated,)), 0, 1, 0) for packs in received]
        project_pairs.append((updated, swap_gossip(updated, level)))
        done = start + size
        while pending and sum(pending[0]) <= done:
            after = (project_pairs[1][1], expand_pairs[0][-1]) if len(pre) else ()
            *blocks, pre_g = expand_chunk(
                me, corr, pending.pop(0), turned, grads, wp, carried[2], count, after
            )
            pre.append(pre_g)
            expand_pairs.append(swap_blocks(blocks))
    first_project_next, second_project_next, _ = carried

    moments = None
    for i, span in enumerate(groups):
        last = i + 1 == len(groups)
        if last:
            back = row_grads(me, pre, wide, spans, width, tuple(u for u, _ in expand_pairs[:i]))
            after = (*(other for _, other in project_pairs[2:]), back[0])
        else:
            after = ()
        updated, *moments = update_chunk(
            me, corr, span, we, me_ax, ve_ax, expand_pairs[i], moments, after
        )
        expand_pairs[i] = (updated, swap_gossip(updated, level))
    first_expand_next, second_expand_next = moments

    back_pieces = swap_blocks(back)

    after = tuple(other for _, other in expand_pairs[:-1])
    grad_conv, first_rows, last_rows = norm_back(
        gain, unit, inv, back_pieces, seqs, steps, after
    )
    forward = [(i, i + 1) for i in range(count - 1)]
    backward = [(target, source) for source, target in forward]
    low = lax.ppermute(last_rows, "fsdp", forward)
    high = lax.ppermute(first_rows, "fsdp", backward)
    input_grad = conv_back(depth_kernel, grad_conv, low, high, masked, seqs)

    shared_project = mean_project(project_pairs, parts)
    shared_expand = None
    for span, pair in zip(groups, expand_pairs):
        after = (input_grad, shared_project) if shared_expand is None else ()
        shared_expand = mean_expand(me, span, *pair, hidden_width, shared_expand, after)
    return (
        shared_expand[None],
        shared_project[None],
        first_expand_next[None],
        second_expand_next[None],
        first_project_next[None],
        second_project_next[None],
        input_grad[None],
    )


def body(*args):
    step_index = args[6]
    levels = lax.axis_size("gossip").bit_length() - 1
    return lax.switch(
        step_index[0] % levels,
        [lambda *a, level=level: step(*a, level) for level in range(levels)],
        *args,
    )


def solution(mesh):
    rows = P("gossip", "fsdp", None)
    steps = P("gossip", None, "fsdp", None)
    in_specs = (steps, steps, P("gossip", None, "fsdp"), P(), P(), P(), P()) + (rows,) * 6
    out_specs = (rows,) * 6 + (steps,)
    return jax.shard_map(body, mesh=mesh, in_specs=in_specs, out_specs=out_specs, check_vma=False)
```

```python
from functools import partial
import math

import jax
import jax.numpy as jnp
from jax import lax
from jax.experimental import pallas as pl
from jax.experimental.pallas import tpu as pltpu
from jax.sharding import PartitionSpec as P

NORM_EPS = 1e-06
ADAM_EPS = 1e-08
BETA_ONE = 0.9
BETA_TWO = 0.999
LEARN_RATE = 0.02
DECAY_RATE = 0.1
HALF_ROOT = 0.7071067811865476
INV_ROOT_TAU = 0.3989422804014327
PAD = 8
BLOCK = 256
EXPAND_UNROLL = False
F32 = jnp.float32
BF16 = jnp.bfloat16
MIB = 1 << 20


def dims(lhs, rhs):
    return (((lhs,), (rhs,)), ((), ()))


def dot(lhs, rhs, contract=(1, 0)):
    return lax.dot_general(lhs, rhs, dims(*contract), preferred_element_type=F32)


def whole(array):
    rank = len(array.shape)
    return pl.BlockSpec(array.shape, lambda *ids: (0,) * rank)


def hbm():
    return pl.BlockSpec(memory_space=pl.ANY)


def params(limit):
    return pltpu.CompilerParams(vmem_limit_bytes=limit)


def cost(moved=1):
    return pl.CostEstimate(flops=1, transcendentals=0, bytes_accessed=moved)


def loop(count, body, unroll=False):
    if count > 4 or not unroll:
        lax.fori_loop(0, count, lambda i, carry: (body(i), carry)[1], 0)
    else:
        for i in range(count):
            body(i)


def row_range(i, rows):
    return pl.ds(i * rows if isinstance(i, int) else pl.multiple_of(i * rows, rows), rows)


def ranges(sizes):
    starts = [sum(sizes[:i]) for i in range(len(sizes))]
    return list(zip(starts, sizes))


def plan(owned):
    if owned % 1024 == 0:
        q = owned // 4
        return ranges([2 * q, 2 * q]), ranges([q, q, 2 * q]), ranges([2 * q, 2 * q])
    half = owned // 2
    return ranges([owned]), ranges([half, half]), ranges([owned])


def xor_perm(value, off):
    count = lax.axis_size("fsdp")
    return lax.ppermute(value, "fsdp", [(i, i ^ off) for i in range(count)])


def gather_xor(own, hold=()):
    count = lax.axis_size("fsdp")
    pieces = {0: own}
    bit = count // 2
    while bit:
        for off in list(pieces):
            value = pieces[off]
            if off and len(hold):
                value = lax.optimization_barrier((value, *hold))[0]
            pieces[off ^ bit] = xor_perm(value, bit)
        bit //= 2
    return [pieces[off] for off in range(count)]


def send_packs(packs):
    return [xor_perm(pack, 2 * h) if h else pack for h, pack in enumerate(packs)]


def relay_packs(packs, hold=()):
    held = []
    for h, pack in enumerate(packs):
        out = lax.optimization_barrier((pack, *hold))[0] if h and len(hold) else pack
        held += [pack, xor_perm(out, 1)]
    return held


def pieces_of(held, base, spans, k):
    return [(array, base + off % 2 * spans + k) for off, array in enumerate(held)]


def swap_blocks(blocks):
    return [block if off == 0 else xor_perm(block, off) for off, block in enumerate(blocks)]


def swap_gossip(value, level):
    count = lax.axis_size("gossip")
    return lax.ppermute(value, "gossip", [(i, i ^ (1 << level)) for i in range(count)])


def token_kernel(*refs):
    refs[-1][...] = jnp.zeros(refs[-1].shape, F32)


def token(values, name):
    shape = jax.ShapeDtypeStruct((8, 128), F32)
    return pl.pallas_call(
        token_kernel,
        out_shape=shape,
        in_specs=[hbm()] * len(values),
        out_specs=pl.BlockSpec(memory_space=pltpu.VMEM),
        compiler_params=params(MIB),
        cost_estimate=cost(40 * MIB),
        name=name,
    )(*values)


def slice_kernel(me_ref, *refs, count):
    outs = refs[-(count // 2) :]
    rows = refs[0].shape[0]
    for off in range(count):
        low = off % 2 * rows
        outs[off // 2][low : low + rows] = refs[off][...]


def slice_specs(rows, full, count, span):
    start, size = span
    ratio = full // count // size
    base = start // size
    return [
        pl.BlockSpec((rows, size), lambda i, me, off=off: (0, (me[0] ^ off) * ratio + base))
        for off in range(count)
    ]


def slice_weights(me, w, count, span):
    rows, full = w.shape
    shape = jax.ShapeDtypeStruct((2 * rows, span[1]), w.dtype)
    return pl.pallas_call(
        partial(slice_kernel, count=count),
        out_shape=[shape] * (count // 2),
        grid_spec=pltpu.PrefetchScalarGridSpec(
            num_scalar_prefetch=1,
            grid=(1,),
            in_specs=slice_specs(rows, full, count, span),
            out_specs=[whole(shape)] * (count // 2),
        ),
        compiler_params=params(16 * MIB),
        cost_estimate=cost(),
        name=f"slice_{span[0]}",
    )(me, *[w] * count)


def pack_kernel(me_ref, cot_ref, seen_ref, scale_ref, *refs, count):
    *outs, masked_ref = refs[-(count // 2) - 1 :]
    blocks = refs[: -(count // 2) - 1]
    spans = len(blocks) // count
    rows, width = cot_ref.shape
    part, size = blocks[0].shape
    panels = width // size
    tile = 64

    def body(i, carry):
        here = pl.ds(pl.multiple_of(i * tile, tile), tile)
        masked = (cot_ref[here].astype(F32) * seen_ref[here]).astype(BF16)
        masked_ref[here] = masked
        branch = (masked.astype(F32) * scale_ref[...]).astype(BF16)
        for out in outs:
            for p in range(panels):
                there = pl.ds(pl.multiple_of(p * rows + i * tile, tile), tile)
                out[there] = branch[:, p * size : (p + 1) * size]
        return carry

    lax.fori_loop(0, rows // tile, body, 0)
    for off in range(count):
        for k in range(spans):
            low = panels * rows + (off % 2 * spans + k) * part
            outs[off // 2][low : low + part] = blocks[k * count + off][...]


def pack_first(me, cot, seen, scale, w, count, spans):
    rows, width = cot.shape
    part, full = w.shape
    size = spans[0][1]
    shape = jax.ShapeDtypeStruct((width // size * rows + 2 * len(spans) * part, size), BF16)
    *packs, masked = pl.pallas_call(
        partial(pack_kernel, count=count),
        out_shape=[shape] * (count // 2) + [jax.ShapeDtypeStruct(cot.shape, BF16)],
        grid_spec=pltpu.PrefetchScalarGridSpec(
            num_scalar_prefetch=1,
            grid=(1,),
            in_specs=[whole(cot), whole(seen), whole(scale)]
            + [spec for span in spans for spec in slice_specs(part, full, count, span)],
            out_specs=[whole(shape)] * (count // 2) + [whole(cot)],
        ),
        compiler_params=params(24 * MIB),
        cost_estimate=cost(),
        name="pack_first",
    )(me, cot, seen, scale, *[w] * (count * len(spans)))
    return packs, masked


def norm_kernel(me_ref, taps_ref, gain_ref, *refs, count, tile):
    pieces = refs[:count]
    normed_ref, turned_ref, unit_ref, inv_ref, padded = refs[-5:]
    off = pl.program_id(0)
    seqs, steps, width = pieces[0].shape
    taps = taps_ref.shape[0]
    reach = taps // 2
    me = me_ref[0]

    @pl.when(off == 0)
    def _():
        edge = jnp.zeros((seqs, PAD, width), F32)
        padded[:, :PAD] = edge
        padded[:, PAD + count * steps :] = edge
        for other in range(count):
            start = pl.multiple_of((me ^ other) * steps + PAD, 8)
            padded[:, pl.ds(start, steps)] = pieces[other][...].astype(F32)

    def body(i, carry):
        s = i // (steps // tile)
        r = i % (steps // tile)
        base = pl.multiple_of((me ^ off) * steps + r * tile, 8)
        window = padded.at[s, pl.ds(base, tile + 2 * PAD)]
        conv = jnp.zeros((tile, width), F32)
        for j in range(taps):
            low = PAD + j - reach
            conv = conv + taps_ref[j : j + 1] * window[low : low + tile]
        centred = conv - jnp.mean(conv, axis=-1, keepdims=True)
        inv = lax.rsqrt(jnp.mean(centred * centred, axis=-1, keepdims=True) + NORM_EPS)
        unit = centred * inv
        rows = pl.ds(pl.multiple_of(i * tile, tile), tile)
        normed_ref[rows] = (unit * gain_ref[...]).astype(BF16)

        @pl.when(off == 0)
        def _():
            unit_ref[rows] = unit
            inv_ref[rows] = jnp.broadcast_to(inv, (tile, 128))

        return carry

    lax.fori_loop(0, seqs * steps // tile, body, 0)
    turned_ref[...] = normed_ref[...].T


def norm_rows(me, pieces, taps, gain, after):
    count = len(pieces)
    seqs, steps, width = pieces[0].shape
    rows = seqs * steps
    total = count * rows
    return pl.pallas_call(
        partial(norm_kernel, count=count, tile=math.gcd(steps, 64)),
        out_shape=[
            jax.ShapeDtypeStruct((total, width), BF16),
            jax.ShapeDtypeStruct((width, total), BF16),
            jax.ShapeDtypeStruct((rows, width), F32),
            jax.ShapeDtypeStruct((rows, 128), F32),
        ],
        grid_spec=pltpu.PrefetchScalarGridSpec(
            num_scalar_prefetch=1,
            grid=(count,),
            in_specs=[whole(taps), whole(gain)]
            + [whole(p) for p in pieces]
            + [hbm()] * len(after),
            out_specs=[
                pl.BlockSpec((rows, width), lambda i, m: (i, 0)),
                pl.BlockSpec((width, rows), lambda i, m: (0, i)),
                pl.BlockSpec((rows, width), lambda i, m: (0, 0)),
                pl.BlockSpec((rows, 128), lambda i, m: (0, 0)),
            ],
            scratch_shapes=[pltpu.VMEM((seqs, count * steps + 2 * PAD, width), F32)],
        ),
        compiler_params=params(18 * MIB + 14 * total * width // 2),
        cost_estimate=cost(40 * MIB),
        name="norm_rows",
    )(me, taps, gain, *pieces, *after)


def adam(weight, first, second, gradient, inv_one, inv_two):
    first_next = BETA_ONE * first + (1.0 - BETA_ONE) * gradient
    second_next = BETA_TWO * second + (1.0 - BETA_TWO) * gradient * gradient
    weight_f = weight.astype(F32)
    direction = first_next * inv_one / (jnp.sqrt(second_next * inv_two) + ADAM_EPS)
    updated = (weight_f - LEARN_RATE * (direction + DECAY_RATE * weight_f)).astype(BF16)
    return updated, first_next, second_next


def adam_tiles(w_ref, m_ref, v_ref, gradient, corr_ref, updated_ref, first_ref, second_ref, tile):
    def body(i, carry):
        rows = pl.ds(pl.multiple_of(i * tile, tile), tile)
        updated, first, second = adam(
            w_ref[rows], m_ref[rows], v_ref[rows], gradient(rows), corr_ref[0], corr_ref[1]
        )
        updated_ref[rows] = updated
        first_ref[rows] = first
        second_ref[rows] = second
        return carry

    lax.fori_loop(0, w_ref.shape[0] // tile, body, 0)


def join_rows(me, pieces, joined, columns=slice(None)):
    part = pieces[0].shape[0]
    for off, piece in enumerate(pieces):
        start = pl.multiple_of((me ^ off) * part, 16)
        joined[pl.ds(start, part), columns] = piece[...]


def hidden_kernel(
    me_ref, corr_ref, normed_ref, w_ref, m_ref, v_ref, *refs, count, first, splits
):
    wide = refs[:count]
    if first:
        packs = refs[count : 2 * count]
        *outs, first_ref, second_ref, slope_ref, grads_ref = refs[-splits - 7 : -3]
    else:
        grads_ref = refs[count]
        *outs, first_ref, second_ref, slope_ref = refs[-splits - 6 : -3]
    joined, total, updated = refs[-3:]
    join_rows(me_ref[0], wide, joined)
    width = normed_ref.shape[1]
    rows = normed_ref.shape[0] // count
    scale_in = 1.0 / math.sqrt(width)
    if first:
        size = packs[0].shape[1]
        for off in range(count):
            for p in range(width // size):
                grads_ref[off * rows : (off + 1) * rows, p * size : (p + 1) * size] = packs[off][
                    p * rows : (p + 1) * rows
                ]
    total[...] = jnp.zeros(total.shape, F32)

    def body(off):
        part = row_range(off, rows)
        pre = dot(normed_ref[part], joined[...]) * scale_in
        cumul = 0.5 * (1.0 + lax.erf(pre * HALF_ROOT))
        density = jnp.exp(-0.5 * pre * pre) * INV_ROOT_TAU
        hidden = (pre * cumul).astype(BF16)
        slope_ref[part] = (cumul + pre * density).astype(BF16)
        total[...] += dot(hidden, grads_ref[part], (0, 0))

    loop(count, body, True)
    adam_tiles(
        w_ref,
        m_ref,
        v_ref,
        lambda rows: total[rows] * corr_ref[2],
        corr_ref,
        updated if splits > 1 else outs[0],
        first_ref,
        second_ref,
        32,
    )
    for k in range(splits if splits > 1 else 0):

        @pl.when(pl.program_id(0) == k)
        def _():
            outs[k][...] = updated[...]


def hidden_chunk(me, corr, span, normed, grads, w, m, v, wide, low, previous, after):
    count = len(wide)
    total, width = normed.shape
    owned, part = w.shape[0], width // count
    start, size = span
    block = min(BLOCK, size)
    base = start // block
    splits = size // block
    rows = total // count
    row_block = pl.BlockSpec((block, width), lambda f, *_: (base + f, 0))
    arrays = [array for array, _ in wide]
    wide_specs = [
        pl.BlockSpec((part, block), lambda f, *_, lead=lead: (lead, low // block + f))
        for _, lead in wide
    ]
    if grads is None:
        spread = width // size * rows
        more = [pl.BlockSpec((spread, size), lambda f, *_: (0, 0))] * count
        extra = arrays
        out_grads = [jax.ShapeDtypeStruct((total, width), BF16)]
    else:
        more = [whole(grads)]
        extra = [grads]
        out_grads = []
    chained = previous is not None
    last = 6 + count + len(extra)
    return pl.pallas_call(
        partial(hidden_kernel, count=count, first=grads is None, splits=splits),
        out_shape=[jax.ShapeDtypeStruct((block, width), BF16)] * splits
        + [
            jax.ShapeDtypeStruct(m.shape, F32),
            jax.ShapeDtypeStruct(v.shape, F32),
            jax.ShapeDtypeStruct((total, owned), BF16),
        ]
        + out_grads,
        grid_spec=pltpu.PrefetchScalarGridSpec(
            num_scalar_prefetch=2,
            grid=(splits,),
            in_specs=[whole(normed), row_block, row_block, row_block]
            + wide_specs
            + more
            + ([hbm()] * 3 if chained else [])
            + [hbm()] * len(after),
            out_specs=[pl.BlockSpec((block, width), lambda f, *_: (0, 0))] * splits
            + [
                row_block,
                row_block,
                pl.BlockSpec((total, block), lambda f, *_: (0, base + f)),
            ]
            + [whole(g) for g in out_grads],
            scratch_shapes=[
                pltpu.VMEM((width, block), BF16),
                pltpu.VMEM((block, width), F32),
                pltpu.VMEM((block, width), BF16),
            ],
        ),
        input_output_aliases=(
            {last + j: splits + j for j in range(3)} if chained else {}
        ),
        compiler_params=params(20 * MIB + 5 * total * width * 2),
        cost_estimate=cost(),
        name=f"hidden_{start}",
    )(me, corr, normed, w, m, v, *arrays, *extra, *(previous or ()), *after)


def expand_kernel(me_ref, corr_ref, turned_ref, grads_ref, w_ref, slope_ref, *refs, count):
    *outs, pre_ref, scratch = refs[-count - 2 :]
    width = turned_ref.shape[0]
    rows = grads_ref.shape[0] // count
    scale_in = 1.0 / math.sqrt(width)

    def body(off):
        part = row_range(off, rows)
        back = dot(grads_ref[part], w_ref[...], (1, 1)) * corr_ref[2]
        pre_ref[part] = (back * slope_ref[part].astype(F32)).astype(BF16)

    loop(count, body, EXPAND_UNROLL)
    scratch[...] = (dot(turned_ref[...], pre_ref[...]) * scale_in).astype(BF16)
    piece = width // count
    for off in range(count):
        start = pl.multiple_of((me_ref[0] ^ off) * piece, 16)
        outs[off][...] = scratch[pl.ds(start, piece)]


def expand_chunk(me, corr, span, turned, grads, w, slope, count, after):
    width, total = turned.shape
    start, size = span
    block = min(BLOCK, size)
    base = start // block
    piece = width // count
    return pl.pallas_call(
        partial(expand_kernel, count=count),
        out_shape=[jax.ShapeDtypeStruct((piece, size), BF16)] * count
        + [jax.ShapeDtypeStruct((total, size), BF16)],
        grid_spec=pltpu.PrefetchScalarGridSpec(
            num_scalar_prefetch=2,
            grid=(size // block,),
            in_specs=[
                whole(turned),
                whole(grads),
                pl.BlockSpec((block, width), lambda f, *_: (base + f, 0)),
                pl.BlockSpec((total, block), lambda f, *_: (0, base + f)),
            ]
            + [hbm()] * len(after),
            out_specs=[pl.BlockSpec((piece, block), lambda f, *_: (0, f))] * count
            + [pl.BlockSpec((total, block), lambda f, *_: (0, f))],
            scratch_shapes=[pltpu.VMEM((width, block), BF16)],
        ),
        compiler_params=params(20 * MIB + 5 * total * width * 2),
        cost_estimate=cost(),
        name=f"expand_{start}",
    )(me, corr, turned, grads, w, slope, *after)


def update_kernel(me_ref, corr_ref, w_ref, m_ref, v_ref, *refs, count, splits):
    pieces = refs[:count]
    *outs, first_ref, second_ref, held, updated = refs[-splits - 4 :]
    for off in range(count):

        @pl.when(pl.program_id(0) == off)
        def _():
            held[...] = pieces[off][...]

    adam_tiles(
        w_ref,
        m_ref,
        v_ref,
        lambda rows: held[rows].astype(F32),
        corr_ref,
        updated,
        first_ref,
        second_ref,
        48,
    )
    for h in range(splits):

        @pl.when(pl.program_id(0) // (count // splits) == h)
        def _():
            outs[h][0] = updated[...]


def update_chunk(me, corr, span, w, m, v, pieces, splits, previous, after):
    count = len(pieces)
    half = count // splits
    rows, size = pieces[0].shape
    start, _ = span
    ratio = w.shape[1] // count // size
    base = start // size
    column = pl.BlockSpec((rows, size), lambda i, me, *_: (0, (me[0] ^ i) * ratio + base))
    chained = previous is not None
    last = 5 + count
    return pl.pallas_call(
        partial(update_kernel, count=count, splits=splits),
        out_shape=[jax.ShapeDtypeStruct((half, rows, size), BF16)] * splits
        + [jax.ShapeDtypeStruct(m.shape, F32), jax.ShapeDtypeStruct(v.shape, F32)],
        grid_spec=pltpu.PrefetchScalarGridSpec(
            num_scalar_prefetch=2,
            grid=(count,),
            in_specs=[column, column, column]
            + [whole(p) for p in pieces]
            + ([hbm()] * 2 if chained else [])
            + [hbm()] * len(after),
            out_specs=[
                pl.BlockSpec(
                    (1, rows, size),
                    lambda i, *_, h=h: (jnp.clip(i - h * half, 0, half - 1).astype(jnp.int32), 0, 0),
                )
                for h in range(splits)
            ]
            + [column, column],
            scratch_shapes=[pltpu.VMEM((rows, size), BF16)] * 2,
        ),
        input_output_aliases={last: splits, last + 1: splits + 1} if chained else {},
        compiler_params=params(24 * MIB),
        cost_estimate=cost(),
        name=f"update_{start}",
    )(me, corr, w, m, v, *pieces, *(previous or ()), *after)


def mean_tiles(own_ref, other_ref, out_ref):
    rows = out_ref.shape[0]
    tile = math.gcd(rows, 64)

    def body(i, carry):
        part = pl.ds(pl.multiple_of(i * tile, tile), tile)
        value = (own_ref[part].astype(F32) + other_ref[part].astype(F32)) * 0.5
        out_ref[part] = value.astype(BF16)
        return carry

    lax.fori_loop(0, rows // tile, body, 0)


def mean_project_kernel(*refs, parts):
    out_ref = refs[-1]
    for i, (start, size) in enumerate(parts):
        mean_tiles(refs[2 * i], refs[2 * i + 1], out_ref.at[pl.ds(start, size)])


def mean_project(pairs, parts):
    flat = [x for pair in pairs for x in pair]
    shape = jax.ShapeDtypeStruct((sum(p[0].shape[0] for p in pairs), flat[0].shape[1]), BF16)
    return pl.pallas_call(
        partial(mean_project_kernel, parts=parts),
        out_shape=shape,
        grid=(1,),
        in_specs=[whole(x) for x in flat],
        out_specs=whole(shape),
        compiler_params=params(24 * MIB),
        cost_estimate=cost(),
        name="mean_project",
    )(*flat)


def mean_expand_kernel(me_ref, own_ref, other_ref, *refs):
    mean_tiles(own_ref.at[0], other_ref.at[0], refs[-1])


def mean_expand(me, span, lead, own, other, full, owned, previous, after):
    count, rows, size = own.shape
    ratio = owned // size
    base = span[0] // size
    in_spec = pl.BlockSpec((1, rows, size), lambda i, m: (i, 0, 0))
    chained = previous is not None
    return pl.pallas_call(
        mean_expand_kernel,
        out_shape=pltpu.HBM((rows, full), BF16),
        grid_spec=pltpu.PrefetchScalarGridSpec(
            num_scalar_prefetch=1,
            grid=(count,),
            in_specs=[in_spec, in_spec] + [hbm()] * (chained + len(after)),
            out_specs=pl.BlockSpec((rows, size), lambda i, m: (0, (m[0] ^ (i + lead)) * ratio + base)),
        ),
        input_output_aliases={3: 0} if chained else {},
        compiler_params=params(16 * MIB),
        cost_estimate=cost(),
        name=f"mean_expand_{span[0]}_{lead}",
    )(me, own, other, *((previous,) if chained else ()), *after)


def rows_kernel(me_ref, *refs, count, groups, parts):
    pre = refs[:groups]
    wide = refs[groups : groups + len(parts) * count]
    *outs, joined = refs[-count - 1 :]
    width = joined.shape[0]

    @pl.when(pl.program_id(0) == 0)
    def _():
        for i, (start, size) in enumerate(parts):
            pieces = wide[i * count : (i + 1) * count]
            join_rows(me_ref[0], pieces, joined, slice(start, start + size))

    total = None
    low = 0
    for piece in pre:
        size = piece.shape[1]
        term = dot(piece[...], joined[:, low : low + size], (1, 1))
        total = term if total is None else total + term
        low += size
    total = (total * (1.0 / math.sqrt(width))).astype(BF16)
    for off in range(count):

        @pl.when(pl.program_id(0) == off)
        def _():
            outs[off][...] = total


def row_grads(me, pre, wide, parts, width, after):
    count = len(wide[0])
    total = pre[0].shape[0]
    rows = total // count
    owned = sum(p.shape[1] for p in pre)
    flat = [piece for chunk in wide for piece in chunk]
    shapes = [jax.ShapeDtypeStruct((rows, width), BF16)] * count
    return pl.pallas_call(
        partial(rows_kernel, count=count, groups=len(pre), parts=parts),
        out_shape=shapes,
        grid_spec=pltpu.PrefetchScalarGridSpec(
            num_scalar_prefetch=1,
            grid=(count,),
            in_specs=[pl.BlockSpec((rows, p.shape[1]), lambda i, m: (i, 0)) for p in pre]
            + [
                pl.BlockSpec((width // count, x.shape[1]), lambda i, m, lead=lead: (lead, 0))
                for x, lead in flat
            ]
            + [hbm()] * len(after),
            out_specs=[whole(x) for x in shapes],
            scratch_shapes=[pltpu.VMEM((width, owned), BF16)],
        ),
        compiler_params=params(24 * MIB),
        cost_estimate=cost(),
        name="row_grads",
    )(me, *pre, *[x for x, _ in flat], *after)


def norm_back_kernel(gain_ref, unit_ref, inv_ref, *refs, count, steps, tile):
    pieces = refs[:count]
    conv_ref, first_ref, last_ref = refs[-3:]

    def body(i, carry):
        rows = pl.ds(pl.multiple_of(i * tile, tile), tile)
        total = pieces[0][rows].astype(F32)
        for piece in pieces[1:]:
            total = total + piece[rows].astype(F32)
        scaled = total * gain_ref[...]
        unit = unit_ref[rows]
        conv_ref[rows] = inv_ref[rows, :1] * (
            scaled
            - jnp.mean(scaled, axis=-1, keepdims=True)
            - unit * jnp.mean(scaled * unit, axis=-1, keepdims=True)
        )
        return carry

    lax.fori_loop(0, conv_ref.shape[0] // tile, body, 0)
    for s in range(first_ref.shape[0]):
        first_ref[s] = conv_ref[s * steps : s * steps + PAD].astype(BF16)
        last_ref[s] = conv_ref[(s + 1) * steps - PAD : (s + 1) * steps].astype(BF16)


def norm_back(gain, unit, inv, pieces, seqs, steps, after):
    count = len(pieces)
    width = unit.shape[1]
    edge = jax.ShapeDtypeStruct((seqs, PAD, width), BF16)
    full = jax.ShapeDtypeStruct((seqs * steps, width), F32)
    return pl.pallas_call(
        partial(norm_back_kernel, count=count, steps=steps, tile=32),
        out_shape=[full, edge, edge],
        grid=(1,),
        in_specs=[whole(gain), whole(unit), whole(inv)]
        + [whole(p) for p in pieces]
        + [hbm()] * len(after),
        out_specs=[whole(full), whole(edge), whole(edge)],
        compiler_params=params(32 * MIB),
        cost_estimate=cost(),
        name="norm_back",
    )(gain, unit, inv, *pieces, *after)


def conv_back_kernel(taps_ref, grad_ref, low_ref, high_ref, cot_ref, out_ref, padded, *, tile):
    seqs, steps, width = out_ref.shape
    taps = taps_ref.shape[0]
    reach = taps // 2
    for s in range(seqs):
        padded[s, :PAD] = low_ref[s].astype(F32)
        padded[s, PAD + steps :] = high_ref[s].astype(F32)

    def fill(i, carry):
        s = i // (steps // tile)
        r = i % (steps // tile)
        rows = pl.ds(pl.multiple_of(i * tile, tile), tile)
        padded[s, pl.ds(pl.multiple_of(r * tile + PAD, 8), tile)] = grad_ref[rows]
        return carry

    def body(i, carry):
        s = i // (steps // tile)
        r = i % (steps // tile)
        rows = pl.ds(pl.multiple_of(r * tile, tile), tile)
        window = padded.at[s, pl.ds(pl.multiple_of(r * tile, 8), tile + 2 * PAD)]
        back = cot_ref[pl.ds(pl.multiple_of(i * tile, tile), tile)].astype(F32)
        for j in range(taps):
            low = PAD + reach - j
            back = back + taps_ref[j : j + 1] * window[low : low + tile]
        out_ref[s, rows] = back.astype(BF16)
        return carry

    lax.fori_loop(0, seqs * steps // tile, fill, 0)
    lax.fori_loop(0, seqs * steps // tile, body, 0)


def conv_back(taps, grad, low, high, cot, seqs):
    total, width = cot.shape
    steps = total // seqs
    shape = jax.ShapeDtypeStruct((seqs, steps, width), BF16)
    return pl.pallas_call(
        partial(conv_back_kernel, tile=32),
        out_shape=shape,
        grid=(1,),
        in_specs=[whole(x) for x in (taps, grad, low, high, cot)],
        out_specs=whole(shape),
        scratch_shapes=[pltpu.VMEM((seqs, steps + 2 * PAD, width), F32)],
        compiler_params=params(32 * MIB),
        cost_estimate=cost(),
        name="conv_back",
    )(taps, grad, low, high, cot)


def step(
    series,
    cotangent,
    observed,
    depth_kernel,
    norm_gain,
    layer_scale,
    step_index,
    w_expand,
    w_project,
    first_expand,
    second_expand,
    first_project,
    second_project,
    level,
):
    count = lax.axis_size("fsdp")
    seqs, steps, width = series.shape[1:]
    rows = seqs * steps
    hidden_width = w_expand.shape[2]
    owned = hidden_width // count
    sent, parts, groups = plan(owned)
    me = lax.axis_index("fsdp").astype(jnp.int32).reshape(1)
    gain = norm_gain.reshape(1, width)
    we, wp = w_expand[0], w_project[0]
    me_ax, ve_ax = first_expand[0], second_expand[0]
    mp_ax, vp_ax = first_project[0], second_project[0]

    timestep = (step_index[0] + 1).astype(F32)
    corr = jnp.stack(
        [
            1.0 / (1.0 - jnp.power(F32(BETA_ONE), timestep)),
            1.0 / (1.0 - jnp.power(F32(BETA_TWO), timestep)),
            F32(1.0 / math.sqrt(hidden_width)),
        ]
    )

    part = width // count
    first_spans = [span for span in parts if sum(span) <= sum(sent[0])]
    spans = first_spans + list(sent[1:])
    seen = observed[0].reshape(rows, 1).astype(F32)
    cot = cotangent[0].reshape(rows, width)
    packs, masked = pack_first(
        me, cot, seen, layer_scale.reshape(1, width), we, count, first_spans
    )
    series_pieces = gather_xor(series[0], (packs[0],))
    normed, turned, unit, inv = norm_rows(me, series_pieces, depth_kernel, gain, ())
    base = width // parts[0][1] * rows // part
    held = relay_packs(send_packs(packs), (normed,))
    wide = [pieces_of(held, base, len(first_spans), k) for k in range(len(first_spans))]
    received = [send_packs(slice_weights(me, we, count, span)) for span in sent[1:]]

    project_pairs = []
    expand_pairs = []
    pre = []
    carried = None
    grads = None
    done = 0
    pending = list(groups)
    for i, (start, size) in enumerate(parts):
        if i == 0:
            after = ()
        elif i == 2:
            after = (token([project_pairs[0][1]], "first_arrived"), *pre)
        else:
            after = ()
        at = max(j for j, (low, _) in enumerate(spans) if low <= start)
        low = start - spans[at][0]
        outs = hidden_chunk(
            me, corr, (start, size), normed, grads, wp, mp_ax, vp_ax, wide[at], low, carried, after
        )
        splits = max(1, size // BLOCK)
        updates, carried = outs[:splits], list(outs[splits:])
        if i == 0:
            grads = carried.pop()
        if i == 1:
            wide += [pieces_of(relay_packs(packs, (updates[0],)), 0, 1, 0) for packs in received]
        project_pairs += [(updated, swap_gossip(updated, level)) for updated in updates]
        done = start + size
        while pending and sum(pending[0]) <= done:
            after = (project_pairs[1][1], expand_pairs[0][-1]) if len(pre) else ()
            *blocks, pre_g = expand_chunk(
                me, corr, pending.pop(0), turned, grads, wp, carried[2], count, after
            )
            pre.append(pre_g)
            expand_pairs.append(swap_blocks(blocks))
    first_project_next, second_project_next, _ = carried

    moments = None
    for i, span in enumerate(groups):
        last = i + 1 == len(groups)
        if last:
            done = tuple(pairs[0][0] for pairs in expand_pairs[:i])
            back = row_grads(me, pre, wide, spans, width, done)
            after = (project_pairs[-1][1], back[0])
        else:
            after = (project_pairs[2][1],)
        splits = 2 if last else 1
        last_blocks = expand_pairs[i][1:]
        outs = update_chunk(
            me, corr, span, we, me_ax, ve_ax, expand_pairs[i], splits, moments, after
        )
        moments = outs[splits:]
        expand_pairs[i] = [(updated, swap_gossip(updated, level)) for updated in outs[:splits]]
    first_expand_next, second_expand_next = moments

    back = list(back)
    back[1] = lax.optimization_barrier((back[1], expand_pairs[-1][-1][0]))[0]
    back[2:] = lax.optimization_barrier((*back[2:], *last_blocks))[: count - 2]
    back_pieces = swap_blocks(back)

    shared_project = mean_project(project_pairs, ranges([p[0].shape[0] for p in project_pairs]))
    shared_expand = None
    for span, pairs in zip(groups[:-1], expand_pairs):
        for own, other in pairs:
            shared_expand = mean_expand(
                me, span, 0, own, other, hidden_width, owned, shared_expand, ()
            )
    lead = 0
    after = (shared_project,) if shared_expand is None else (shared_project, shared_expand)
    grad_conv, first_rows, last_rows = norm_back(
        gain, unit, inv, back_pieces, seqs, steps, after
    )
    forward = [(i, i + 1) for i in range(count - 1)]
    backward = [(target, source) for source, target in forward]
    low = lax.ppermute(last_rows, "fsdp", forward)
    high = lax.ppermute(first_rows, "fsdp", backward)
    input_grad = conv_back(depth_kernel, grad_conv, low, high, masked, seqs)

    for own, other in expand_pairs[-1]:
        shared_expand = mean_expand(
            me, groups[-1], lead, own, other, hidden_width, owned, shared_expand, (input_grad,)
        )
        lead += own.shape[0]
    return (
        shared_expand[None],
        shared_project[None],
        first_expand_next[None],
        second_expand_next[None],
        first_project_next[None],
        second_project_next[None],
        input_grad[None],
    )


def body(*args):
    step_index = args[6]
    levels = lax.axis_size("gossip").bit_length() - 1
    return lax.switch(
        step_index[0] % levels,
        [lambda *a, level=level: step(*a, level) for level in range(levels)],
        *args,
    )


def solution(mesh):
    rows = P("gossip", "fsdp", None)
    steps = P("gossip", None, "fsdp", None)
    in_specs = (steps, steps, P("gossip", None, "fsdp"), P(), P(), P(), P()) + (rows,) * 6
    out_specs = (rows,) * 6 + (steps,)
    return jax.shard_map(body, mesh=mesh, in_specs=in_specs, out_specs=out_specs, check_vma=False)
```

```python
from functools import partial
import math

import jax
import jax.numpy as jnp
from jax import lax
from jax.experimental import pallas as pl
from jax.experimental.pallas import tpu as pltpu
from jax.sharding import PartitionSpec as P

NORM_EPS = 1e-06
ADAM_EPS = 1e-08
BETA_ONE = 0.9
BETA_TWO = 0.999
LEARN_RATE = 0.02
DECAY_RATE = 0.1
HALF_ROOT = 0.7071067811865476
INV_ROOT_TAU = 0.3989422804014327
PAD = 8
BLOCK = 256
EXPAND_UNROLL = False
F32 = jnp.float32
BF16 = jnp.bfloat16
MIB = 1 << 20


def dims(lhs, rhs):
    return (((lhs,), (rhs,)), ((), ()))


def dot(lhs, rhs, contract=(1, 0)):
    return lax.dot_general(lhs, rhs, dims(*contract), preferred_element_type=F32)


def whole(array):
    rank = len(array.shape)
    return pl.BlockSpec(array.shape, lambda *ids: (0,) * rank)


def hbm():
    return pl.BlockSpec(memory_space=pl.ANY)


def params(limit):
    return pltpu.CompilerParams(vmem_limit_bytes=limit)


def cost(moved=1):
    return pl.CostEstimate(flops=1, transcendentals=0, bytes_accessed=moved)


def loop(count, body, unroll=False):
    if count > 4 or not unroll:
        lax.fori_loop(0, count, lambda i, carry: (body(i), carry)[1], 0)
    else:
        for i in range(count):
            body(i)


def row_range(i, rows):
    return pl.ds(i * rows if isinstance(i, int) else pl.multiple_of(i * rows, rows), rows)


def ranges(sizes):
    starts = [sum(sizes[:i]) for i in range(len(sizes))]
    return list(zip(starts, sizes))


def plan(owned):
    if owned % 1024 == 0:
        q = owned // 4
        return ranges([2 * q, 2 * q]), ranges([q, q, 2 * q]), ranges([2 * q, 2 * q])
    half = owned // 2
    return ranges([owned]), ranges([half, half]), ranges([owned])


def xor_perm(value, off):
    count = lax.axis_size("fsdp")
    return lax.ppermute(value, "fsdp", [(i, i ^ off) for i in range(count)])


def gather_xor(own, hold=()):
    count = lax.axis_size("fsdp")
    pieces = {0: own}
    bit = count // 2
    while bit:
        for off in list(pieces):
            value = pieces[off]
            if off and len(hold):
                value = lax.optimization_barrier((value, *hold))[0]
            pieces[off ^ bit] = xor_perm(value, bit)
        bit //= 2
    return [pieces[off] for off in range(count)]


def send_packs(packs):
    return [xor_perm(pack, 2 * h) if h else pack for h, pack in enumerate(packs)]


def relay_packs(packs, hold=()):
    held = []
    for h, pack in enumerate(packs):
        out = lax.optimization_barrier((pack, *hold))[0] if h and len(hold) else pack
        held += [pack, xor_perm(out, 1)]
    return held


def pieces_of(held, base, spans, k):
    return [(array, base + off % 2 * spans + k) for off, array in enumerate(held)]


def swap_blocks(blocks):
    return [block if off == 0 else xor_perm(block, off) for off, block in enumerate(blocks)]


def swap_gossip(value, level):
    count = lax.axis_size("gossip")
    return lax.ppermute(value, "gossip", [(i, i ^ (1 << level)) for i in range(count)])


def token_kernel(*refs):
    refs[-1][...] = jnp.zeros(refs[-1].shape, F32)


def token(values, name):
    shape = jax.ShapeDtypeStruct((8, 128), F32)
    return pl.pallas_call(
        token_kernel,
        out_shape=shape,
        in_specs=[hbm()] * len(values),
        out_specs=pl.BlockSpec(memory_space=pltpu.VMEM),
        compiler_params=params(MIB),
        cost_estimate=cost(40 * MIB),
        name=name,
    )(*values)


def slice_kernel(me_ref, *refs, count):
    outs = refs[-(count // 2) :]
    rows = refs[0].shape[0]
    for off in range(count):
        low = off % 2 * rows
        outs[off // 2][low : low + rows] = refs[off][...]


def slice_specs(rows, full, count, span):
    start, size = span
    ratio = full // count // size
    base = start // size
    return [
        pl.BlockSpec((rows, size), lambda i, me, off=off: (0, (me[0] ^ off) * ratio + base))
        for off in range(count)
    ]


def slice_weights(me, w, count, span):
    rows, full = w.shape
    shape = jax.ShapeDtypeStruct((2 * rows, span[1]), w.dtype)
    return pl.pallas_call(
        partial(slice_kernel, count=count),
        out_shape=[shape] * (count // 2),
        grid_spec=pltpu.PrefetchScalarGridSpec(
            num_scalar_prefetch=1,
            grid=(1,),
            in_specs=slice_specs(rows, full, count, span),
            out_specs=[whole(shape)] * (count // 2),
        ),
        compiler_params=params(16 * MIB),
        cost_estimate=cost(),
        name=f"slice_{span[0]}",
    )(me, *[w] * count)


def pack_kernel(me_ref, cot_ref, seen_ref, scale_ref, *refs, count):
    *outs, masked_ref = refs[-(count // 2) - 1 :]
    blocks = refs[: -(count // 2) - 1]
    spans = len(blocks) // count
    rows, width = cot_ref.shape
    part, size = blocks[0].shape
    panels = width // size
    tile = 64

    def body(i, carry):
        here = pl.ds(pl.multiple_of(i * tile, tile), tile)
        masked = (cot_ref[here].astype(F32) * seen_ref[here]).astype(BF16)
        masked_ref[here] = masked
        branch = (masked.astype(F32) * scale_ref[...]).astype(BF16)
        for out in outs:
            for p in range(panels):
                there = pl.ds(pl.multiple_of(p * rows + i * tile, tile), tile)
                out[there] = branch[:, p * size : (p + 1) * size]
        return carry

    lax.fori_loop(0, rows // tile, body, 0)
    for off in range(count):
        for k in range(spans):
            low = panels * rows + (off % 2 * spans + k) * part
            outs[off // 2][low : low + part] = blocks[k * count + off][...]


def pack_first(me, cot, seen, scale, w, count, spans):
    rows, width = cot.shape
    part, full = w.shape
    size = spans[0][1]
    shape = jax.ShapeDtypeStruct((width // size * rows + 2 * len(spans) * part, size), BF16)
    *packs, masked = pl.pallas_call(
        partial(pack_kernel, count=count),
        out_shape=[shape] * (count // 2) + [jax.ShapeDtypeStruct(cot.shape, BF16)],
        grid_spec=pltpu.PrefetchScalarGridSpec(
            num_scalar_prefetch=1,
            grid=(1,),
            in_specs=[whole(cot), whole(seen), whole(scale)]
            + [spec for span in spans for spec in slice_specs(part, full, count, span)],
            out_specs=[whole(shape)] * (count // 2) + [whole(cot)],
        ),
        compiler_params=params(24 * MIB),
        cost_estimate=cost(),
        name="pack_first",
    )(me, cot, seen, scale, *[w] * (count * len(spans)))
    return packs, masked


def norm_kernel(me_ref, taps_ref, gain_ref, *refs, count, tile):
    pieces = refs[:count]
    normed_ref, turned_ref, unit_ref, inv_ref, padded = refs[-5:]
    off = pl.program_id(0)
    seqs, steps, width = pieces[0].shape
    taps = taps_ref.shape[0]
    reach = taps // 2
    me = me_ref[0]

    @pl.when(off == 0)
    def _():
        edge = jnp.zeros((seqs, PAD, width), F32)
        padded[:, :PAD] = edge
        padded[:, PAD + count * steps :] = edge
        for other in range(count):
            start = pl.multiple_of((me ^ other) * steps + PAD, 8)
            padded[:, pl.ds(start, steps)] = pieces[other][...].astype(F32)

    def body(i, carry):
        s = i // (steps // tile)
        r = i % (steps // tile)
        base = pl.multiple_of((me ^ off) * steps + r * tile, 8)
        window = padded.at[s, pl.ds(base, tile + 2 * PAD)]
        conv = jnp.zeros((tile, width), F32)
        for j in range(taps):
            low = PAD + j - reach
            conv = conv + taps_ref[j : j + 1] * window[low : low + tile]
        centred = conv - jnp.mean(conv, axis=-1, keepdims=True)
        inv = lax.rsqrt(jnp.mean(centred * centred, axis=-1, keepdims=True) + NORM_EPS)
        unit = centred * inv
        rows = pl.ds(pl.multiple_of(i * tile, tile), tile)
        normed_ref[rows] = (unit * gain_ref[...]).astype(BF16)

        @pl.when(off == 0)
        def _():
            unit_ref[rows] = unit
            inv_ref[rows] = jnp.broadcast_to(inv, (tile, 128))

        return carry

    lax.fori_loop(0, seqs * steps // tile, body, 0)
    turned_ref[...] = normed_ref[...].T


def norm_rows(me, pieces, taps, gain, after):
    count = len(pieces)
    seqs, steps, width = pieces[0].shape
    rows = seqs * steps
    total = count * rows
    return pl.pallas_call(
        partial(norm_kernel, count=count, tile=math.gcd(steps, 64)),
        out_shape=[
            jax.ShapeDtypeStruct((total, width), BF16),
            jax.ShapeDtypeStruct((width, total), BF16),
            jax.ShapeDtypeStruct((rows, width), F32),
            jax.ShapeDtypeStruct((rows, 128), F32),
        ],
        grid_spec=pltpu.PrefetchScalarGridSpec(
            num_scalar_prefetch=1,
            grid=(count,),
            in_specs=[whole(taps), whole(gain)]
            + [whole(p) for p in pieces]
            + [hbm()] * len(after),
            out_specs=[
                pl.BlockSpec((rows, width), lambda i, m: (i, 0)),
                pl.BlockSpec((width, rows), lambda i, m: (0, i)),
                pl.BlockSpec((rows, width), lambda i, m: (0, 0)),
                pl.BlockSpec((rows, 128), lambda i, m: (0, 0)),
            ],
            scratch_shapes=[pltpu.VMEM((seqs, count * steps + 2 * PAD, width), F32)],
        ),
        compiler_params=params(18 * MIB + 14 * total * width // 2),
        cost_estimate=cost(40 * MIB),
        name="norm_rows",
    )(me, taps, gain, *pieces, *after)


def adam(weight, first, second, gradient, inv_one, inv_two):
    first_next = BETA_ONE * first + (1.0 - BETA_ONE) * gradient
    second_next = BETA_TWO * second + (1.0 - BETA_TWO) * gradient * gradient
    weight_f = weight.astype(F32)
    direction = first_next * inv_one / (jnp.sqrt(second_next * inv_two) + ADAM_EPS)
    updated = (weight_f - LEARN_RATE * (direction + DECAY_RATE * weight_f)).astype(BF16)
    return updated, first_next, second_next


def adam_tiles(w_ref, m_ref, v_ref, gradient, corr_ref, updated_ref, first_ref, second_ref, tile):
    def body(i, carry):
        rows = pl.ds(pl.multiple_of(i * tile, tile), tile)
        updated, first, second = adam(
            w_ref[rows], m_ref[rows], v_ref[rows], gradient(rows), corr_ref[0], corr_ref[1]
        )
        updated_ref[rows] = updated
        first_ref[rows] = first
        second_ref[rows] = second
        return carry

    lax.fori_loop(0, w_ref.shape[0] // tile, body, 0)


def join_rows(me, pieces, joined, columns=slice(None)):
    part = pieces[0].shape[0]
    for off, piece in enumerate(pieces):
        start = pl.multiple_of((me ^ off) * part, 16)
        joined[pl.ds(start, part), columns] = piece[...]


def hidden_kernel(
    me_ref, corr_ref, normed_ref, w_ref, m_ref, v_ref, *refs, count, first, splits
):
    wide = refs[:count]
    if first:
        packs = refs[count : 2 * count]
        *outs, first_ref, second_ref, slope_ref, grads_ref = refs[-splits - 7 : -3]
    else:
        grads_ref = refs[count]
        *outs, first_ref, second_ref, slope_ref = refs[-splits - 6 : -3]
    joined, total, updated = refs[-3:]
    join_rows(me_ref[0], wide, joined)
    width = normed_ref.shape[1]
    rows = normed_ref.shape[0] // count
    scale_in = 1.0 / math.sqrt(width)
    if first:
        size = packs[0].shape[1]
        for off in range(count):
            for p in range(width // size):
                grads_ref[off * rows : (off + 1) * rows, p * size : (p + 1) * size] = packs[off][
                    p * rows : (p + 1) * rows
                ]
    total[...] = jnp.zeros(total.shape, F32)

    def body(off):
        part = row_range(off, rows)
        pre = dot(normed_ref[part], joined[...]) * scale_in
        cumul = 0.5 * (1.0 + lax.erf(pre * HALF_ROOT))
        density = jnp.exp(-0.5 * pre * pre) * INV_ROOT_TAU
        hidden = (pre * cumul).astype(BF16)
        slope_ref[part] = (cumul + pre * density).astype(BF16)
        total[...] += dot(hidden, grads_ref[part], (0, 0))

    loop(count, body, True)
    adam_tiles(
        w_ref,
        m_ref,
        v_ref,
        lambda rows: total[rows] * corr_ref[2],
        corr_ref,
        updated if splits > 1 else outs[0],
        first_ref,
        second_ref,
        32,
    )
    for k in range(splits if splits > 1 else 0):

        @pl.when(pl.program_id(0) == k)
        def _():
            outs[k][...] = updated[...]


def hidden_chunk(me, corr, span, normed, grads, w, m, v, wide, low, previous, after):
    count = len(wide)
    total, width = normed.shape
    owned, part = w.shape[0], width // count
    start, size = span
    block = min(BLOCK, size)
    base = start // block
    splits = size // block
    rows = total // count
    row_block = pl.BlockSpec((block, width), lambda f, *_: (base + f, 0))
    arrays = [array for array, _ in wide]
    wide_specs = [
        pl.BlockSpec((part, block), lambda f, *_, lead=lead: (lead, low // block + f))
        for _, lead in wide
    ]
    if grads is None:
        spread = width // size * rows
        more = [pl.BlockSpec((spread, size), lambda f, *_: (0, 0))] * count
        extra = arrays
        out_grads = [jax.ShapeDtypeStruct((total, width), BF16)]
    else:
        more = [whole(grads)]
        extra = [grads]
        out_grads = []
    chained = previous is not None
    last = 6 + count + len(extra)
    return pl.pallas_call(
        partial(hidden_kernel, count=count, first=grads is None, splits=splits),
        out_shape=[jax.ShapeDtypeStruct((block, width), BF16)] * splits
        + [
            jax.ShapeDtypeStruct(m.shape, F32),
            jax.ShapeDtypeStruct(v.shape, F32),
            jax.ShapeDtypeStruct((total, owned), BF16),
        ]
        + out_grads,
        grid_spec=pltpu.PrefetchScalarGridSpec(
            num_scalar_prefetch=2,
            grid=(splits,),
            in_specs=[whole(normed), row_block, row_block, row_block]
            + wide_specs
            + more
            + ([hbm()] * 3 if chained else [])
            + [hbm()] * len(after),
            out_specs=[pl.BlockSpec((block, width), lambda f, *_: (0, 0))] * splits
            + [
                row_block,
                row_block,
                pl.BlockSpec((total, block), lambda f, *_: (0, base + f)),
            ]
            + [whole(g) for g in out_grads],
            scratch_shapes=[
                pltpu.VMEM((width, block), BF16),
                pltpu.VMEM((block, width), F32),
                pltpu.VMEM((block, width), BF16),
            ],
        ),
        input_output_aliases=(
            {last + j: splits + j for j in range(3)} if chained else {}
        ),
        compiler_params=params(20 * MIB + 5 * total * width * 2),
        cost_estimate=cost(),
        name=f"hidden_{start}",
    )(me, corr, normed, w, m, v, *arrays, *extra, *(previous or ()), *after)


def expand_kernel(me_ref, corr_ref, turned_ref, grads_ref, w_ref, slope_ref, *refs, count):
    *outs, pre_ref, scratch = refs[-count - 2 :]
    width = turned_ref.shape[0]
    rows = grads_ref.shape[0] // count
    scale_in = 1.0 / math.sqrt(width)

    def body(off):
        part = row_range(off, rows)
        back = dot(grads_ref[part], w_ref[...], (1, 1)) * corr_ref[2]
        pre_ref[part] = (back * slope_ref[part].astype(F32)).astype(BF16)

    loop(count, body, EXPAND_UNROLL)
    scratch[...] = (dot(turned_ref[...], pre_ref[...]) * scale_in).astype(BF16)
    piece = width // count
    for off in range(count):
        start = pl.multiple_of((me_ref[0] ^ off) * piece, 16)
        outs[off][...] = scratch[pl.ds(start, piece)]


def expand_chunk(me, corr, span, turned, grads, w, slope, count, after):
    width, total = turned.shape
    start, size = span
    block = min(BLOCK, size)
    base = start // block
    piece = width // count
    return pl.pallas_call(
        partial(expand_kernel, count=count),
        out_shape=[jax.ShapeDtypeStruct((piece, size), BF16)] * count
        + [jax.ShapeDtypeStruct((total, size), BF16)],
        grid_spec=pltpu.PrefetchScalarGridSpec(
            num_scalar_prefetch=2,
            grid=(size // block,),
            in_specs=[
                whole(turned),
                whole(grads),
                pl.BlockSpec((block, width), lambda f, *_: (base + f, 0)),
                pl.BlockSpec((total, block), lambda f, *_: (0, base + f)),
            ]
            + [hbm()] * len(after),
            out_specs=[pl.BlockSpec((piece, block), lambda f, *_: (0, f))] * count
            + [pl.BlockSpec((total, block), lambda f, *_: (0, f))],
            scratch_shapes=[pltpu.VMEM((width, block), BF16)],
        ),
        compiler_params=params(20 * MIB + 5 * total * width * 2),
        cost_estimate=cost(),
        name=f"expand_{start}",
    )(me, corr, turned, grads, w, slope, *after)


def update_kernel(me_ref, corr_ref, w_ref, m_ref, v_ref, *refs, count, splits):
    pieces = refs[:count]
    *outs, first_ref, second_ref, held, updated = refs[-splits - 4 :]
    for off in range(count):

        @pl.when(pl.program_id(0) == off)
        def _():
            held[...] = pieces[off][...]

    adam_tiles(
        w_ref,
        m_ref,
        v_ref,
        lambda rows: held[rows].astype(F32),
        corr_ref,
        updated,
        first_ref,
        second_ref,
        48,
    )
    for h in range(splits):

        @pl.when(pl.program_id(0) // (count // splits) == h)
        def _():
            outs[h][0] = updated[...]


def update_chunk(me, corr, span, w, m, v, pieces, splits, previous, after):
    count = len(pieces)
    half = count // splits
    rows, size = pieces[0].shape
    start, _ = span
    ratio = w.shape[1] // count // size
    base = start // size
    column = pl.BlockSpec((rows, size), lambda i, me, *_: (0, (me[0] ^ i) * ratio + base))
    chained = previous is not None
    last = 5 + count
    return pl.pallas_call(
        partial(update_kernel, count=count, splits=splits),
        out_shape=[jax.ShapeDtypeStruct((half, rows, size), BF16)] * splits
        + [jax.ShapeDtypeStruct(m.shape, F32), jax.ShapeDtypeStruct(v.shape, F32)],
        grid_spec=pltpu.PrefetchScalarGridSpec(
            num_scalar_prefetch=2,
            grid=(count,),
            in_specs=[column, column, column]
            + [whole(p) for p in pieces]
            + ([hbm()] * 2 if chained else [])
            + [hbm()] * len(after),
            out_specs=[
                pl.BlockSpec(
                    (1, rows, size),
                    lambda i, *_, h=h: (jnp.clip(i - h * half, 0, half - 1).astype(jnp.int32), 0, 0),
                )
                for h in range(splits)
            ]
            + [column, column],
            scratch_shapes=[pltpu.VMEM((rows, size), BF16)] * 2,
        ),
        input_output_aliases={last: splits, last + 1: splits + 1} if chained else {},
        compiler_params=params(24 * MIB),
        cost_estimate=cost(),
        name=f"update_{start}",
    )(me, corr, w, m, v, *pieces, *(previous or ()), *after)


def mean_tiles(own_ref, other_ref, out_ref):
    rows = out_ref.shape[0]
    tile = math.gcd(rows, 64)

    def body(i, carry):
        part = pl.ds(pl.multiple_of(i * tile, tile), tile)
        value = (own_ref[part].astype(F32) + other_ref[part].astype(F32)) * 0.5
        out_ref[part] = value.astype(BF16)
        return carry

    lax.fori_loop(0, rows // tile, body, 0)


def mean_project_kernel(*refs, parts):
    out_ref = refs[-1]
    for i, (start, size) in enumerate(parts):
        mean_tiles(refs[2 * i], refs[2 * i + 1], out_ref.at[pl.ds(start, size)])


def mean_project(pairs, parts):
    flat = [x for pair in pairs for x in pair]
    shape = jax.ShapeDtypeStruct((sum(p[0].shape[0] for p in pairs), flat[0].shape[1]), BF16)
    return pl.pallas_call(
        partial(mean_project_kernel, parts=parts),
        out_shape=shape,
        grid=(1,),
        in_specs=[whole(x) for x in flat],
        out_specs=whole(shape),
        compiler_params=params(24 * MIB),
        cost_estimate=cost(),
        name="mean_project",
    )(*flat)


def mean_expand_kernel(me_ref, own_ref, other_ref, *refs):
    mean_tiles(own_ref.at[0], other_ref.at[0], refs[-1])


def mean_expand(me, span, lead, own, other, full, owned, previous, after):
    count, rows, size = own.shape
    ratio = owned // size
    base = span[0] // size
    in_spec = pl.BlockSpec((1, rows, size), lambda i, m: (i, 0, 0))
    chained = previous is not None
    return pl.pallas_call(
        mean_expand_kernel,
        out_shape=pltpu.HBM((rows, full), BF16),
        grid_spec=pltpu.PrefetchScalarGridSpec(
            num_scalar_prefetch=1,
            grid=(count,),
            in_specs=[in_spec, in_spec] + [hbm()] * (chained + len(after)),
            out_specs=pl.BlockSpec((rows, size), lambda i, m: (0, (m[0] ^ (i + lead)) * ratio + base)),
        ),
        input_output_aliases={3: 0} if chained else {},
        compiler_params=params(16 * MIB),
        cost_estimate=cost(),
        name=f"mean_expand_{span[0]}_{lead}",
    )(me, own, other, *((previous,) if chained else ()), *after)


def rows_kernel(me_ref, *refs, count, groups, parts):
    pre = refs[:groups]
    wide = refs[groups : groups + len(parts) * count]
    *outs, joined = refs[-count - 1 :]
    width = joined.shape[0]

    @pl.when(pl.program_id(0) == 0)
    def _():
        for i, (start, size) in enumerate(parts):
            pieces = wide[i * count : (i + 1) * count]
            join_rows(me_ref[0], pieces, joined, slice(start, start + size))

    total = None
    low = 0
    for piece in pre:
        size = piece.shape[1]
        term = dot(piece[...], joined[:, low : low + size], (1, 1))
        total = term if total is None else total + term
        low += size
    total = (total * (1.0 / math.sqrt(width))).astype(BF16)
    for off in range(count):

        @pl.when(pl.program_id(0) == off)
        def _():
            outs[off][...] = total


def row_grads(me, pre, wide, parts, width, after):
    count = len(wide[0])
    total = pre[0].shape[0]
    rows = total // count
    owned = sum(p.shape[1] for p in pre)
    flat = [piece for chunk in wide for piece in chunk]
    shapes = [jax.ShapeDtypeStruct((rows, width), BF16)] * count
    return pl.pallas_call(
        partial(rows_kernel, count=count, groups=len(pre), parts=parts),
        out_shape=shapes,
        grid_spec=pltpu.PrefetchScalarGridSpec(
            num_scalar_prefetch=1,
            grid=(count,),
            in_specs=[pl.BlockSpec((rows, p.shape[1]), lambda i, m: (i, 0)) for p in pre]
            + [
                pl.BlockSpec((width // count, x.shape[1]), lambda i, m, lead=lead: (lead, 0))
                for x, lead in flat
            ]
            + [hbm()] * len(after),
            out_specs=[whole(x) for x in shapes],
            scratch_shapes=[pltpu.VMEM((width, owned), BF16)],
        ),
        compiler_params=params(24 * MIB),
        cost_estimate=cost(),
        name="row_grads",
    )(me, *pre, *[x for x, _ in flat], *after)


def norm_back_kernel(gain_ref, unit_ref, inv_ref, *refs, count, steps, tile):
    pieces = refs[:count]
    conv_ref, first_ref, last_ref = refs[-3:]

    def body(i, carry):
        rows = pl.ds(pl.multiple_of(i * tile, tile), tile)
        total = pieces[0][rows].astype(F32)
        for piece in pieces[1:]:
            total = total + piece[rows].astype(F32)
        scaled = total * gain_ref[...]
        unit = unit_ref[rows]
        conv_ref[rows] = inv_ref[rows, :1] * (
            scaled
            - jnp.mean(scaled, axis=-1, keepdims=True)
            - unit * jnp.mean(scaled * unit, axis=-1, keepdims=True)
        )
        return carry

    lax.fori_loop(0, conv_ref.shape[0] // tile, body, 0)
    for s in range(first_ref.shape[0]):
        first_ref[s] = conv_ref[s * steps : s * steps + PAD].astype(BF16)
        last_ref[s] = conv_ref[(s + 1) * steps - PAD : (s + 1) * steps].astype(BF16)


def norm_back(gain, unit, inv, pieces, seqs, steps, after):
    count = len(pieces)
    width = unit.shape[1]
    edge = jax.ShapeDtypeStruct((seqs, PAD, width), BF16)
    full = jax.ShapeDtypeStruct((seqs * steps, width), F32)
    return pl.pallas_call(
        partial(norm_back_kernel, count=count, steps=steps, tile=32),
        out_shape=[full, edge, edge],
        grid=(1,),
        in_specs=[whole(gain), whole(unit), whole(inv)]
        + [whole(p) for p in pieces]
        + [hbm()] * len(after),
        out_specs=[whole(full), whole(edge), whole(edge)],
        compiler_params=params(32 * MIB),
        cost_estimate=cost(),
        name="norm_back",
    )(gain, unit, inv, *pieces, *after)


def conv_back_kernel(taps_ref, grad_ref, low_ref, high_ref, cot_ref, *refs, tile):
    out_ref, padded = refs[-2:]
    seqs, steps, width = out_ref.shape
    taps = taps_ref.shape[0]
    reach = taps // 2
    for s in range(seqs):
        padded[s, :PAD] = low_ref[s].astype(F32)
        padded[s, PAD + steps :] = high_ref[s].astype(F32)

    def fill(i, carry):
        s = i // (steps // tile)
        r = i % (steps // tile)
        rows = pl.ds(pl.multiple_of(i * tile, tile), tile)
        padded[s, pl.ds(pl.multiple_of(r * tile + PAD, 8), tile)] = grad_ref[rows]
        return carry

    def body(i, carry):
        s = i // (steps // tile)
        r = i % (steps // tile)
        rows = pl.ds(pl.multiple_of(r * tile, tile), tile)
        window = padded.at[s, pl.ds(pl.multiple_of(r * tile, 8), tile + 2 * PAD)]
        back = cot_ref[pl.ds(pl.multiple_of(i * tile, tile), tile)].astype(F32)
        for j in range(taps):
            low = PAD + reach - j
            back = back + taps_ref[j : j + 1] * window[low : low + tile]
        out_ref[s, rows] = back.astype(BF16)
        return carry

    lax.fori_loop(0, seqs * steps // tile, fill, 0)
    lax.fori_loop(0, seqs * steps // tile, body, 0)


def conv_back(taps, grad, low, high, cot, seqs, after):
    total, width = cot.shape
    steps = total // seqs
    shape = jax.ShapeDtypeStruct((seqs, steps, width), BF16)
    return pl.pallas_call(
        partial(conv_back_kernel, tile=32),
        out_shape=shape,
        grid=(1,),
        in_specs=[whole(x) for x in (taps, grad, low, high, cot)] + [hbm()] * len(after),
        out_specs=whole(shape),
        scratch_shapes=[pltpu.VMEM((seqs, steps + 2 * PAD, width), F32)],
        compiler_params=params(32 * MIB),
        cost_estimate=cost(),
        name="conv_back",
    )(taps, grad, low, high, cot, *after)


def step(
    series,
    cotangent,
    observed,
    depth_kernel,
    norm_gain,
    layer_scale,
    step_index,
    w_expand,
    w_project,
    first_expand,
    second_expand,
    first_project,
    second_project,
    level,
):
    count = lax.axis_size("fsdp")
    seqs, steps, width = series.shape[1:]
    rows = seqs * steps
    hidden_width = w_expand.shape[2]
    owned = hidden_width // count
    sent, parts, groups = plan(owned)
    me = lax.axis_index("fsdp").astype(jnp.int32).reshape(1)
    gain = norm_gain.reshape(1, width)
    we, wp = w_expand[0], w_project[0]
    me_ax, ve_ax = first_expand[0], second_expand[0]
    mp_ax, vp_ax = first_project[0], second_project[0]

    timestep = (step_index[0] + 1).astype(F32)
    corr = jnp.stack(
        [
            1.0 / (1.0 - jnp.power(F32(BETA_ONE), timestep)),
            1.0 / (1.0 - jnp.power(F32(BETA_TWO), timestep)),
            F32(1.0 / math.sqrt(hidden_width)),
        ]
    )

    part = width // count
    first_spans = [span for span in parts if sum(span) <= sum(sent[0])]
    spans = first_spans + list(sent[1:])
    seen = observed[0].reshape(rows, 1).astype(F32)
    cot = cotangent[0].reshape(rows, width)
    packs, masked = pack_first(
        me, cot, seen, layer_scale.reshape(1, width), we, count, first_spans
    )
    series_pieces = gather_xor(series[0], (packs[0],))
    normed, turned, unit, inv = norm_rows(me, series_pieces, depth_kernel, gain, ())
    base = width // parts[0][1] * rows // part
    held = relay_packs(send_packs(packs), (normed,))
    wide = [pieces_of(held, base, len(first_spans), k) for k in range(len(first_spans))]
    received = [send_packs(slice_weights(me, we, count, span)) for span in sent[1:]]

    project_pairs = []
    expand_pairs = []
    pre = []
    carried = None
    grads = None
    done = 0
    pending = list(groups)
    for i, (start, size) in enumerate(parts):
        if i == 0:
            after = ()
        elif i == 2:
            after = (token([project_pairs[0][1]], "first_arrived"), *pre)
        else:
            after = ()
        at = max(j for j, (low, _) in enumerate(spans) if low <= start)
        low = start - spans[at][0]
        outs = hidden_chunk(
            me, corr, (start, size), normed, grads, wp, mp_ax, vp_ax, wide[at], low, carried, after
        )
        splits = max(1, size // BLOCK)
        updates, carried = outs[:splits], list(outs[splits:])
        if i == 0:
            grads = carried.pop()
        if i == 1:
            wide += [pieces_of(relay_packs(packs, (updates[0],)), 0, 1, 0) for packs in received]
        project_pairs += [(updated, swap_gossip(updated, level)) for updated in updates]
        done = start + size
        while pending and sum(pending[0]) <= done:
            after = (project_pairs[1][1], expand_pairs[0][-1]) if len(pre) else ()
            *blocks, pre_g = expand_chunk(
                me, corr, pending.pop(0), turned, grads, wp, carried[2], count, after
            )
            pre.append(pre_g)
            expand_pairs.append(swap_blocks(blocks))
    first_project_next, second_project_next, _ = carried

    moments = None
    for i, span in enumerate(groups):
        last = i + 1 == len(groups)
        if last:
            done = tuple(pairs[0][0] for pairs in expand_pairs[:i])
            back = row_grads(me, pre, wide, spans, width, done)
            after = (project_pairs[-1][1], back[0])
        else:
            after = (project_pairs[2][1],)
        splits = 2 if last else 1
        last_blocks = expand_pairs[i][1:]
        outs = update_chunk(
            me, corr, span, we, me_ax, ve_ax, expand_pairs[i], splits, moments, after
        )
        moments = outs[splits:]
        expand_pairs[i] = [(updated, swap_gossip(updated, level)) for updated in outs[:splits]]
    first_expand_next, second_expand_next = moments

    back = list(back)
    back[1] = lax.optimization_barrier((back[1], expand_pairs[-1][-1][0]))[0]
    back[2:] = lax.optimization_barrier((*back[2:], *last_blocks))[: count - 2]
    back_pieces = swap_blocks(back)

    after = tuple(other for pairs in expand_pairs[:-1] for _, other in pairs)
    grad_conv, first_rows, last_rows = norm_back(
        gain, unit, inv, back_pieces, seqs, steps, after
    )
    forward = [(i, i + 1) for i in range(count - 1)]
    backward = [(target, source) for source, target in forward]
    low = lax.ppermute(last_rows, "fsdp", forward)
    high = lax.ppermute(first_rows, "fsdp", backward)
    shared_project = mean_project(project_pairs, ranges([p[0].shape[0] for p in project_pairs]))
    shared_expand = None
    for span, pairs in zip(groups[:-1], expand_pairs):
        for own, other in pairs:
            shared_expand = mean_expand(
                me, span, 0, own, other, hidden_width, owned, shared_expand, (grad_conv,)
            )
    after = (shared_project,) if shared_expand is None else (shared_project, shared_expand)
    input_grad = conv_back(depth_kernel, grad_conv, low, high, masked, seqs, after)
    lead = 0
    for own, other in expand_pairs[-1]:
        shared_expand = mean_expand(
            me, groups[-1], lead, own, other, hidden_width, owned, shared_expand, (input_grad,)
        )
        lead += own.shape[0]
    return (
        shared_expand[None],
        shared_project[None],
        first_expand_next[None],
        second_expand_next[None],
        first_project_next[None],
        second_project_next[None],
        input_grad[None],
    )


def body(*args):
    step_index = args[6]
    levels = lax.axis_size("gossip").bit_length() - 1
    return lax.switch(
        step_index[0] % levels,
        [lambda *a, level=level: step(*a, level) for level in range(levels)],
        *args,
    )


def solution(mesh):
    rows = P("gossip", "fsdp", None)
    steps = P("gossip", None, "fsdp", None)
    in_specs = (steps, steps, P("gossip", None, "fsdp"), P(), P(), P(), P()) + (rows,) * 6
    out_specs = (rows,) * 6 + (steps,)
    return jax.shard_map(body, mesh=mesh, in_specs=in_specs, out_specs=out_specs, check_vma=False)
```

```python
from functools import partial
import math

import jax
import jax.numpy as jnp
from jax import lax
from jax.experimental import pallas as pl
from jax.experimental.pallas import tpu as pltpu
from jax.sharding import PartitionSpec as P

NORM_EPS = 1e-06
ADAM_EPS = 1e-08
BETA_ONE = 0.9
BETA_TWO = 0.999
LEARN_RATE = 0.02
DECAY_RATE = 0.1
HALF_ROOT = 0.7071067811865476
INV_ROOT_TAU = 0.3989422804014327
PAD = 8
BLOCK = 256
EXPAND_UNROLL = False
F32 = jnp.float32
BF16 = jnp.bfloat16
MIB = 1 << 20


def dims(lhs, rhs):
    return (((lhs,), (rhs,)), ((), ()))


def dot(lhs, rhs, contract=(1, 0)):
    return lax.dot_general(lhs, rhs, dims(*contract), preferred_element_type=F32)


def whole(array):
    rank = len(array.shape)
    return pl.BlockSpec(array.shape, lambda *ids: (0,) * rank)


def hbm():
    return pl.BlockSpec(memory_space=pl.ANY)


def params(limit):
    return pltpu.CompilerParams(vmem_limit_bytes=limit)


def cost(moved=1):
    return pl.CostEstimate(flops=1, transcendentals=0, bytes_accessed=moved)


def loop(count, body, unroll=False):
    if count > 4 or not unroll:
        lax.fori_loop(0, count, lambda i, carry: (body(i), carry)[1], 0)
    else:
        for i in range(count):
            body(i)


def row_range(i, rows):
    return pl.ds(i * rows if isinstance(i, int) else pl.multiple_of(i * rows, rows), rows)


def ranges(sizes):
    starts = [sum(sizes[:i]) for i in range(len(sizes))]
    return list(zip(starts, sizes))


def plan(owned):
    if owned % 1024 == 0:
        q = owned // 4
        return ranges([q, q, 2 * q]), ranges([q, q, 2 * q]), ranges([2 * q, 2 * q])
    half = owned // 2
    return ranges([owned]), ranges([half, half]), ranges([owned])


def xor_perm(value, off):
    count = lax.axis_size("fsdp")
    return lax.ppermute(value, "fsdp", [(i, i ^ off) for i in range(count)])


def gather_xor(own, hold=()):
    count = lax.axis_size("fsdp")
    pieces = {0: own}
    bit = count // 2
    while bit:
        for off in list(pieces):
            value = pieces[off]
            if off and len(hold):
                value = lax.optimization_barrier((value, *hold))[0]
            pieces[off ^ bit] = xor_perm(value, bit)
        bit //= 2
    return [pieces[off] for off in range(count)]


def send_packs(packs):
    return [xor_perm(pack, 2 * h) if h else pack for h, pack in enumerate(packs)]


def relay_packs(packs, hold=()):
    held = []
    for h, pack in enumerate(packs):
        out = lax.optimization_barrier((pack, *hold))[0] if h and len(hold) else pack
        held += [pack, xor_perm(out, 1)]
    return held


def pieces_of(held, base, spans, k):
    return [(array, base + off % 2 * spans + k) for off, array in enumerate(held)]


def swap_blocks(blocks):
    return [block if off == 0 else xor_perm(block, off) for off, block in enumerate(blocks)]


def swap_gossip(value, level):
    count = lax.axis_size("gossip")
    return lax.ppermute(value, "gossip", [(i, i ^ (1 << level)) for i in range(count)])


def token_kernel(*refs):
    refs[-1][...] = jnp.zeros(refs[-1].shape, F32)


def token(values, name):
    shape = jax.ShapeDtypeStruct((8, 128), F32)
    return pl.pallas_call(
        token_kernel,
        out_shape=shape,
        in_specs=[hbm()] * len(values),
        out_specs=pl.BlockSpec(memory_space=pltpu.VMEM),
        compiler_params=params(MIB),
        cost_estimate=cost(40 * MIB),
        name=name,
    )(*values)


def slice_kernel(me_ref, *refs, count):
    outs = refs[-(count // 2) :]
    rows = refs[0].shape[0]
    for off in range(count):
        low = off % 2 * rows
        outs[off // 2][low : low + rows] = refs[off][...]


def slice_specs(rows, full, count, span):
    start, size = span
    ratio = full // count // size
    base = start // size
    return [
        pl.BlockSpec((rows, size), lambda i, me, off=off: (0, (me[0] ^ off) * ratio + base))
        for off in range(count)
    ]


def slice_weights(me, w, count, span):
    rows, full = w.shape
    shape = jax.ShapeDtypeStruct((2 * rows, span[1]), w.dtype)
    return pl.pallas_call(
        partial(slice_kernel, count=count),
        out_shape=[shape] * (count // 2),
        grid_spec=pltpu.PrefetchScalarGridSpec(
            num_scalar_prefetch=1,
            grid=(1,),
            in_specs=slice_specs(rows, full, count, span),
            out_specs=[whole(shape)] * (count // 2),
        ),
        compiler_params=params(16 * MIB),
        cost_estimate=cost(),
        name=f"slice_{span[0]}",
    )(me, *[w] * count)


def pack_kernel(me_ref, cot_ref, seen_ref, scale_ref, *refs, count):
    *outs, masked_ref = refs[-(count // 2) - 1 :]
    blocks = refs[: -(count // 2) - 1]
    spans = len(blocks) // count
    rows, width = cot_ref.shape
    part, size = blocks[0].shape
    panels = width // size
    tile = 32

    def body(i, carry):
        here = pl.ds(pl.multiple_of(i * tile, tile), tile)
        masked = (cot_ref[here].astype(F32) * seen_ref[here]).astype(BF16)
        masked_ref[here] = masked
        branch = (masked.astype(F32) * scale_ref[...]).astype(BF16)
        for out in outs:
            for p in range(panels):
                there = pl.ds(pl.multiple_of(p * rows + i * tile, tile), tile)
                out[there] = branch[:, p * size : (p + 1) * size]
        return carry

    lax.fori_loop(0, rows // tile, body, 0)
    for off in range(count):
        for k in range(spans):
            low = panels * rows + (off % 2 * spans + k) * part
            outs[off // 2][low : low + part] = blocks[k * count + off][...]


def pack_first(me, cot, seen, scale, w, count, spans):
    rows, width = cot.shape
    part, full = w.shape
    size = spans[0][1]
    shape = jax.ShapeDtypeStruct((width // size * rows + 2 * len(spans) * part, size), BF16)
    *packs, masked = pl.pallas_call(
        partial(pack_kernel, count=count),
        out_shape=[shape] * (count // 2) + [jax.ShapeDtypeStruct(cot.shape, BF16)],
        grid_spec=pltpu.PrefetchScalarGridSpec(
            num_scalar_prefetch=1,
            grid=(1,),
            in_specs=[whole(cot), whole(seen), whole(scale)]
            + [spec for span in spans for spec in slice_specs(part, full, count, span)],
            out_specs=[whole(shape)] * (count // 2) + [whole(cot)],
        ),
        compiler_params=params(24 * MIB),
        cost_estimate=cost(),
        name="pack_first",
    )(me, cot, seen, scale, *[w] * (count * len(spans)))
    return packs, masked


def norm_kernel(me_ref, taps_ref, gain_ref, *refs, count, tile):
    pieces = refs[:count]
    normed_ref, turned_ref, unit_ref, inv_ref, padded = refs[-5:]
    off = pl.program_id(0)
    seqs, steps, width = pieces[0].shape
    taps = taps_ref.shape[0]
    reach = taps // 2
    me = me_ref[0]

    @pl.when(off == 0)
    def _():
        edge = jnp.zeros((seqs, PAD, width), F32)
        padded[:, :PAD] = edge
        padded[:, PAD + count * steps :] = edge
        for other in range(count):
            start = pl.multiple_of((me ^ other) * steps + PAD, 8)
            padded[:, pl.ds(start, steps)] = pieces[other][...].astype(F32)

    def body(i, carry):
        s = i // (steps // tile)
        r = i % (steps // tile)
        base = pl.multiple_of((me ^ off) * steps + r * tile, 8)
        window = padded.at[s, pl.ds(base, tile + 2 * PAD)]
        conv = jnp.zeros((tile, width), F32)
        for j in range(taps):
            low = PAD + j - reach
            conv = conv + taps_ref[j : j + 1] * window[low : low + tile]
        centred = conv - jnp.mean(conv, axis=-1, keepdims=True)
        inv = lax.rsqrt(jnp.mean(centred * centred, axis=-1, keepdims=True) + NORM_EPS)
        unit = centred * inv
        rows = pl.ds(pl.multiple_of(i * tile, tile), tile)
        normed_ref[rows] = (unit * gain_ref[...]).astype(BF16)

        @pl.when(off == 0)
        def _():
            unit_ref[rows] = unit
            inv_ref[rows] = jnp.broadcast_to(inv, (tile, 128))

        return carry

    lax.fori_loop(0, seqs * steps // tile, body, 0)
    turned_ref[...] = normed_ref[...].T


def norm_rows(me, pieces, taps, gain, after):
    count = len(pieces)
    seqs, steps, width = pieces[0].shape
    rows = seqs * steps
    total = count * rows
    return pl.pallas_call(
        partial(norm_kernel, count=count, tile=math.gcd(steps, 64)),
        out_shape=[
            jax.ShapeDtypeStruct((total, width), BF16),
            jax.ShapeDtypeStruct((width, total), BF16),
            jax.ShapeDtypeStruct((rows, width), F32),
            jax.ShapeDtypeStruct((rows, 128), F32),
        ],
        grid_spec=pltpu.PrefetchScalarGridSpec(
            num_scalar_prefetch=1,
            grid=(count,),
            in_specs=[whole(taps), whole(gain)]
            + [whole(p) for p in pieces]
            + [hbm()] * len(after),
            out_specs=[
                pl.BlockSpec((rows, width), lambda i, m: (i, 0)),
                pl.BlockSpec((width, rows), lambda i, m: (0, i)),
                pl.BlockSpec((rows, width), lambda i, m: (0, 0)),
                pl.BlockSpec((rows, 128), lambda i, m: (0, 0)),
            ],
            scratch_shapes=[pltpu.VMEM((seqs, count * steps + 2 * PAD, width), F32)],
        ),
        compiler_params=params(18 * MIB + 14 * total * width // 2),
        cost_estimate=cost(40 * MIB),
        name="norm_rows",
    )(me, taps, gain, *pieces, *after)


def adam(weight, first, second, gradient, inv_one, inv_two):
    first_next = BETA_ONE * first + (1.0 - BETA_ONE) * gradient
    second_next = BETA_TWO * second + (1.0 - BETA_TWO) * gradient * gradient
    weight_f = weight.astype(F32)
    direction = first_next * inv_one / (jnp.sqrt(second_next * inv_two) + ADAM_EPS)
    updated = (weight_f - LEARN_RATE * (direction + DECAY_RATE * weight_f)).astype(BF16)
    return updated, first_next, second_next


def adam_tiles(w_ref, m_ref, v_ref, gradient, corr_ref, updated_ref, first_ref, second_ref, tile):
    def body(i, carry):
        rows = pl.ds(pl.multiple_of(i * tile, tile), tile)
        updated, first, second = adam(
            w_ref[rows], m_ref[rows], v_ref[rows], gradient(rows), corr_ref[0], corr_ref[1]
        )
        updated_ref[rows] = updated
        first_ref[rows] = first
        second_ref[rows] = second
        return carry

    lax.fori_loop(0, w_ref.shape[0] // tile, body, 0)


def join_rows(me, pieces, joined, columns=slice(None)):
    part = pieces[0].shape[0]
    for off, piece in enumerate(pieces):
        start = pl.multiple_of((me ^ off) * part, 16)
        joined[pl.ds(start, part), columns] = piece[...]


def hidden_kernel(
    me_ref, corr_ref, normed_ref, w_ref, m_ref, v_ref, *refs, count, first, splits
):
    wide = refs[:count]
    if first:
        packs = refs[count : 2 * count]
        *outs, first_ref, second_ref, slope_ref, grads_ref = refs[-splits - 7 : -3]
    else:
        grads_ref = refs[count]
        *outs, first_ref, second_ref, slope_ref = refs[-splits - 6 : -3]
    joined, total, updated = refs[-3:]
    join_rows(me_ref[0], wide, joined)
    width = normed_ref.shape[1]
    rows = normed_ref.shape[0] // count
    scale_in = 1.0 / math.sqrt(width)
    if first:
        size = packs[0].shape[1]
        for off in range(count):
            for p in range(width // size):
                grads_ref[off * rows : (off + 1) * rows, p * size : (p + 1) * size] = packs[off][
                    p * rows : (p + 1) * rows
                ]
    total[...] = jnp.zeros(total.shape, F32)

    def body(off):
        part = row_range(off, rows)
        pre = dot(normed_ref[part], joined[...]) * scale_in
        cumul = 0.5 * (1.0 + lax.erf(pre * HALF_ROOT))
        density = jnp.exp(-0.5 * pre * pre) * INV_ROOT_TAU
        hidden = (pre * cumul).astype(BF16)
        slope_ref[part] = (cumul + pre * density).astype(BF16)
        total[...] += dot(hidden, grads_ref[part], (0, 0))

    loop(count, body, True)
    adam_tiles(
        w_ref,
        m_ref,
        v_ref,
        lambda rows: total[rows] * corr_ref[2],
        corr_ref,
        updated if splits > 1 else outs[0],
        first_ref,
        second_ref,
        32,
    )
    for k in range(splits if splits > 1 else 0):

        @pl.when(pl.program_id(0) == k)
        def _():
            outs[k][...] = updated[...]


def hidden_chunk(me, corr, span, normed, grads, w, m, v, wide, low, previous, after):
    count = len(wide)
    total, width = normed.shape
    owned, part = w.shape[0], width // count
    start, size = span
    block = min(BLOCK, size)
    base = start // block
    splits = size // block
    rows = total // count
    row_block = pl.BlockSpec((block, width), lambda f, *_: (base + f, 0))
    arrays = [array for array, _ in wide]
    wide_specs = [
        pl.BlockSpec((part, block), lambda f, *_, lead=lead: (lead, low // block + f))
        for _, lead in wide
    ]
    if grads is None:
        spread = width // size * rows
        more = [pl.BlockSpec((spread, size), lambda f, *_: (0, 0))] * count
        extra = arrays
        out_grads = [jax.ShapeDtypeStruct((total, width), BF16)]
    else:
        more = [whole(grads)]
        extra = [grads]
        out_grads = []
    chained = previous is not None
    last = 6 + count + len(extra)
    return pl.pallas_call(
        partial(hidden_kernel, count=count, first=grads is None, splits=splits),
        out_shape=[jax.ShapeDtypeStruct((block, width), BF16)] * splits
        + [
            jax.ShapeDtypeStruct(m.shape, F32),
            jax.ShapeDtypeStruct(v.shape, F32),
            jax.ShapeDtypeStruct((total, owned), BF16),
        ]
        + out_grads,
        grid_spec=pltpu.PrefetchScalarGridSpec(
            num_scalar_prefetch=2,
            grid=(splits,),
            in_specs=[whole(normed), row_block, row_block, row_block]
            + wide_specs
            + more
            + ([hbm()] * 3 if chained else [])
            + [hbm()] * len(after),
            out_specs=[pl.BlockSpec((block, width), lambda f, *_: (0, 0))] * splits
            + [
                row_block,
                row_block,
                pl.BlockSpec((total, block), lambda f, *_: (0, base + f)),
            ]
            + [whole(g) for g in out_grads],
            scratch_shapes=[
                pltpu.VMEM((width, block), BF16),
                pltpu.VMEM((block, width), F32),
                pltpu.VMEM((block, width), BF16),
            ],
        ),
        input_output_aliases=(
            {last + j: splits + j for j in range(3)} if chained else {}
        ),
        compiler_params=params(20 * MIB + 5 * total * width * 2),
        cost_estimate=cost(),
        name=f"hidden_{start}",
    )(me, corr, normed, w, m, v, *arrays, *extra, *(previous or ()), *after)


def expand_kernel(me_ref, corr_ref, turned_ref, grads_ref, w_ref, slope_ref, *refs, count):
    *outs, pre_ref, scratch = refs[-count - 2 :]
    width = turned_ref.shape[0]
    rows = grads_ref.shape[0] // count
    scale_in = 1.0 / math.sqrt(width)

    def body(off):
        part = row_range(off, rows)
        back = dot(grads_ref[part], w_ref[...], (1, 1)) * corr_ref[2]
        pre_ref[part] = (back * slope_ref[part].astype(F32)).astype(BF16)

    loop(count, body, EXPAND_UNROLL)
    scratch[...] = (dot(turned_ref[...], pre_ref[...]) * scale_in).astype(BF16)
    piece = width // count
    for off in range(count):
        start = pl.multiple_of((me_ref[0] ^ off) * piece, 16)
        outs[off][...] = scratch[pl.ds(start, piece)]


def expand_chunk(me, corr, span, turned, grads, w, slope, count, after):
    width, total = turned.shape
    start, size = span
    block = min(BLOCK, size)
    base = start // block
    piece = width // count
    return pl.pallas_call(
        partial(expand_kernel, count=count),
        out_shape=[jax.ShapeDtypeStruct((piece, size), BF16)] * count
        + [jax.ShapeDtypeStruct((total, size), BF16)],
        grid_spec=pltpu.PrefetchScalarGridSpec(
            num_scalar_prefetch=2,
            grid=(size // block,),
            in_specs=[
                whole(turned),
                whole(grads),
                pl.BlockSpec((block, width), lambda f, *_: (base + f, 0)),
                pl.BlockSpec((total, block), lambda f, *_: (0, base + f)),
            ]
            + [hbm()] * len(after),
            out_specs=[pl.BlockSpec((piece, block), lambda f, *_: (0, f))] * count
            + [pl.BlockSpec((total, block), lambda f, *_: (0, f))],
            scratch_shapes=[pltpu.VMEM((width, block), BF16)],
        ),
        compiler_params=params(20 * MIB + 5 * total * width * 2),
        cost_estimate=cost(),
        name=f"expand_{start}",
    )(me, corr, turned, grads, w, slope, *after)


def update_kernel(me_ref, corr_ref, w_ref, m_ref, v_ref, *refs, count, splits):
    pieces = refs[:count]
    *outs, first_ref, second_ref, held, updated = refs[-splits - 4 :]
    for off in range(count):

        @pl.when(pl.program_id(0) == off)
        def _():
            held[...] = pieces[off][...]

    adam_tiles(
        w_ref,
        m_ref,
        v_ref,
        lambda rows: held[rows].astype(F32),
        corr_ref,
        updated,
        first_ref,
        second_ref,
        48,
    )
    for h in range(splits):

        @pl.when(pl.program_id(0) // (count // splits) == h)
        def _():
            outs[h][0] = updated[...]


def update_chunk(me, corr, span, w, m, v, pieces, splits, previous, after):
    count = len(pieces)
    half = count // splits
    rows, size = pieces[0].shape
    start, _ = span
    ratio = w.shape[1] // count // size
    base = start // size
    column = pl.BlockSpec((rows, size), lambda i, me, *_: (0, (me[0] ^ i) * ratio + base))
    chained = previous is not None
    last = 5 + count
    return pl.pallas_call(
        partial(update_kernel, count=count, splits=splits),
        out_shape=[jax.ShapeDtypeStruct((half, rows, size), BF16)] * splits
        + [jax.ShapeDtypeStruct(m.shape, F32), jax.ShapeDtypeStruct(v.shape, F32)],
        grid_spec=pltpu.PrefetchScalarGridSpec(
            num_scalar_prefetch=2,
            grid=(count,),
            in_specs=[column, column, column]
            + [whole(p) for p in pieces]
            + ([hbm()] * 2 if chained else [])
            + [hbm()] * len(after),
            out_specs=[
                pl.BlockSpec(
                    (1, rows, size),
                    lambda i, *_, h=h: (jnp.clip(i - h * half, 0, half - 1).astype(jnp.int32), 0, 0),
                )
                for h in range(splits)
            ]
            + [column, column],
            scratch_shapes=[pltpu.VMEM((rows, size), BF16)] * 2,
        ),
        input_output_aliases={last: splits, last + 1: splits + 1} if chained else {},
        compiler_params=params(24 * MIB),
        cost_estimate=cost(),
        name=f"update_{start}",
    )(me, corr, w, m, v, *pieces, *(previous or ()), *after)


def mean_tiles(own_ref, other_ref, out_ref):
    rows = out_ref.shape[0]
    tile = math.gcd(rows, 32)

    def body(i, carry):
        part = pl.ds(pl.multiple_of(i * tile, tile), tile)
        value = (own_ref[part].astype(F32) + other_ref[part].astype(F32)) * 0.5
        out_ref[part] = value.astype(BF16)
        return carry

    lax.fori_loop(0, rows // tile, body, 0)


def mean_project_kernel(*refs, parts):
    out_ref = refs[-1]
    for i, (start, size) in enumerate(parts):
        mean_tiles(refs[2 * i], refs[2 * i + 1], out_ref.at[pl.ds(start, size)])


def mean_project(pairs, parts):
    flat = [x for pair in pairs for x in pair]
    shape = jax.ShapeDtypeStruct((sum(p[0].shape[0] for p in pairs), flat[0].shape[1]), BF16)
    return pl.pallas_call(
        partial(mean_project_kernel, parts=parts),
        out_shape=shape,
        grid=(1,),
        in_specs=[whole(x) for x in flat],
        out_specs=whole(shape),
        compiler_params=params(24 * MIB),
        cost_estimate=cost(),
        name="mean_project",
    )(*flat)


def mean_expand_kernel(me_ref, own_ref, other_ref, *refs):
    mean_tiles(own_ref.at[0], other_ref.at[0], refs[-1])


def mean_expand(me, span, lead, own, other, full, owned, previous, after):
    count, rows, size = own.shape
    ratio = owned // size
    base = span[0] // size
    in_spec = pl.BlockSpec((1, rows, size), lambda i, m: (i, 0, 0))
    chained = previous is not None
    return pl.pallas_call(
        mean_expand_kernel,
        out_shape=pltpu.HBM((rows, full), BF16),
        grid_spec=pltpu.PrefetchScalarGridSpec(
            num_scalar_prefetch=1,
            grid=(count,),
            in_specs=[in_spec, in_spec] + [hbm()] * (chained + len(after)),
            out_specs=pl.BlockSpec((rows, size), lambda i, m: (0, (m[0] ^ (i + lead)) * ratio + base)),
        ),
        input_output_aliases={3: 0} if chained else {},
        compiler_params=params(16 * MIB),
        cost_estimate=cost(),
        name=f"mean_expand_{span[0]}_{lead}",
    )(me, own, other, *((previous,) if chained else ()), *after)


def rows_kernel(me_ref, *refs, count, groups, parts):
    pre = refs[:groups]
    wide = refs[groups : groups + len(parts) * count]
    *outs, joined = refs[-count - 1 :]
    width = joined.shape[0]

    @pl.when(pl.program_id(0) == 0)
    def _():
        for i, (start, size) in enumerate(parts):
            pieces = wide[i * count : (i + 1) * count]
            join_rows(me_ref[0], pieces, joined, slice(start, start + size))

    total = None
    low = 0
    for piece in pre:
        size = piece.shape[1]
        term = dot(piece[...], joined[:, low : low + size], (1, 1))
        total = term if total is None else total + term
        low += size
    total = (total * (1.0 / math.sqrt(width))).astype(BF16)
    for off in range(count):

        @pl.when(pl.program_id(0) == off)
        def _():
            outs[off][...] = total


def row_grads(me, pre, wide, parts, width, after):
    count = len(wide[0])
    total = pre[0].shape[0]
    rows = total // count
    owned = sum(p.shape[1] for p in pre)
    flat = [piece for chunk in wide for piece in chunk]
    shapes = [jax.ShapeDtypeStruct((rows, width), BF16)] * count
    return pl.pallas_call(
        partial(rows_kernel, count=count, groups=len(pre), parts=parts),
        out_shape=shapes,
        grid_spec=pltpu.PrefetchScalarGridSpec(
            num_scalar_prefetch=1,
            grid=(count,),
            in_specs=[pl.BlockSpec((rows, p.shape[1]), lambda i, m: (i, 0)) for p in pre]
            + [
                pl.BlockSpec((width // count, x.shape[1]), lambda i, m, lead=lead: (lead, 0))
                for x, lead in flat
            ]
            + [hbm()] * len(after),
            out_specs=[whole(x) for x in shapes],
            scratch_shapes=[pltpu.VMEM((width, owned), BF16)],
        ),
        compiler_params=params(24 * MIB),
        cost_estimate=cost(),
        name="row_grads",
    )(me, *pre, *[x for x, _ in flat], *after)


def norm_back_kernel(gain_ref, unit_ref, inv_ref, *refs, count, steps, tile):
    pieces = refs[:count]
    conv_ref, first_ref, last_ref = refs[-3:]

    def body(i, carry):
        rows = pl.ds(pl.multiple_of(i * tile, tile), tile)
        total = pieces[0][rows].astype(F32)
        for piece in pieces[1:]:
            total = total + piece[rows].astype(F32)
        scaled = total * gain_ref[...]
        unit = unit_ref[rows]
        conv_ref[rows] = inv_ref[rows, :1] * (
            scaled
            - jnp.mean(scaled, axis=-1, keepdims=True)
            - unit * jnp.mean(scaled * unit, axis=-1, keepdims=True)
        )
        return carry

    lax.fori_loop(0, conv_ref.shape[0] // tile, body, 0)
    for s in range(first_ref.shape[0]):
        first_ref[s] = conv_ref[s * steps : s * steps + PAD].astype(BF16)
        last_ref[s] = conv_ref[(s + 1) * steps - PAD : (s + 1) * steps].astype(BF16)


def norm_back(gain, unit, inv, pieces, seqs, steps, after):
    count = len(pieces)
    width = unit.shape[1]
    edge = jax.ShapeDtypeStruct((seqs, PAD, width), BF16)
    full = jax.ShapeDtypeStruct((seqs * steps, width), F32)
    return pl.pallas_call(
        partial(norm_back_kernel, count=count, steps=steps, tile=32),
        out_shape=[full, edge, edge],
        grid=(1,),
        in_specs=[whole(gain), whole(unit), whole(inv)]
        + [whole(p) for p in pieces]
        + [hbm()] * len(after),
        out_specs=[whole(full), whole(edge), whole(edge)],
        compiler_params=params(32 * MIB),
        cost_estimate=cost(),
        name="norm_back",
    )(gain, unit, inv, *pieces, *after)


def conv_back_kernel(taps_ref, grad_ref, low_ref, high_ref, cot_ref, *refs, tile):
    out_ref, padded = refs[-2:]
    seqs, steps, width = out_ref.shape
    taps = taps_ref.shape[0]
    reach = taps // 2
    for s in range(seqs):
        padded[s, :PAD] = low_ref[s].astype(F32)
        padded[s, PAD + steps :] = high_ref[s].astype(F32)

    def fill(i, carry):
        s = i // (steps // tile)
        r = i % (steps // tile)
        rows = pl.ds(pl.multiple_of(i * tile, tile), tile)
        padded[s, pl.ds(pl.multiple_of(r * tile + PAD, 8), tile)] = grad_ref[rows]
        return carry

    def body(i, carry):
        s = i // (steps // tile)
        r = i % (steps // tile)
        rows = pl.ds(pl.multiple_of(r * tile, tile), tile)
        window = padded.at[s, pl.ds(pl.multiple_of(r * tile, 8), tile + 2 * PAD)]
        back = cot_ref[pl.ds(pl.multiple_of(i * tile, tile), tile)].astype(F32)
        for j in range(taps):
            low = PAD + reach - j
            back = back + taps_ref[j : j + 1] * window[low : low + tile]
        out_ref[s, rows] = back.astype(BF16)
        return carry

    lax.fori_loop(0, seqs * steps // tile, fill, 0)
    lax.fori_loop(0, seqs * steps // tile, body, 0)


def conv_back(taps, grad, low, high, cot, seqs, after):
    total, width = cot.shape
    steps = total // seqs
    shape = jax.ShapeDtypeStruct((seqs, steps, width), BF16)
    return pl.pallas_call(
        partial(conv_back_kernel, tile=32),
        out_shape=shape,
        grid=(1,),
        in_specs=[whole(x) for x in (taps, grad, low, high, cot)] + [hbm()] * len(after),
        out_specs=whole(shape),
        scratch_shapes=[pltpu.VMEM((seqs, steps + 2 * PAD, width), F32)],
        compiler_params=params(32 * MIB),
        cost_estimate=cost(),
        name="conv_back",
    )(taps, grad, low, high, cot, *after)


def step(
    series,
    cotangent,
    observed,
    depth_kernel,
    norm_gain,
    layer_scale,
    step_index,
    w_expand,
    w_project,
    first_expand,
    second_expand,
    first_project,
    second_project,
    level,
):
    count = lax.axis_size("fsdp")
    seqs, steps, width = series.shape[1:]
    rows = seqs * steps
    hidden_width = w_expand.shape[2]
    owned = hidden_width // count
    sent, parts, groups = plan(owned)
    me = lax.axis_index("fsdp").astype(jnp.int32).reshape(1)
    gain = norm_gain.reshape(1, width)
    we, wp = w_expand[0], w_project[0]
    me_ax, ve_ax = first_expand[0], second_expand[0]
    mp_ax, vp_ax = first_project[0], second_project[0]

    timestep = (step_index[0] + 1).astype(F32)
    corr = jnp.stack(
        [
            1.0 / (1.0 - jnp.power(F32(BETA_ONE), timestep)),
            1.0 / (1.0 - jnp.power(F32(BETA_TWO), timestep)),
            F32(1.0 / math.sqrt(hidden_width)),
        ]
    )

    part = width // count
    first_spans = [span for span in parts if sum(span) <= sum(sent[0])]
    spans = first_spans + list(sent[1:])
    seen = observed[0].reshape(rows, 1).astype(F32)
    cot = cotangent[0].reshape(rows, width)
    packs, masked = pack_first(
        me, cot, seen, layer_scale.reshape(1, width), we, count, first_spans
    )
    series_pieces = gather_xor(series[0], (packs[0],))
    normed, turned, unit, inv = norm_rows(me, series_pieces, depth_kernel, gain, ())
    base = width // parts[0][1] * rows // part
    held = relay_packs(send_packs(packs), (normed,))
    wide = [pieces_of(held, base, len(first_spans), k) for k in range(len(first_spans))]
    received = [send_packs(slice_weights(me, we, count, span)) for span in sent[1:]]

    project_pairs = []
    expand_pairs = []
    pre = []
    carried = None
    grads = None
    done = 0
    pending = list(groups)
    for i, (start, size) in enumerate(parts):
        if i == 0:
            after = ()
        elif i == 2:
            after = (token([project_pairs[0][1]], "first_arrived"), *pre)
        else:
            after = ()
        if i == len(wide):
            hold = (pre[-1] if pre else updates[0],)
            wide.append(pieces_of(relay_packs(received[i - len(first_spans)], hold), 0, 1, 0))
        at = max(j for j, (low, _) in enumerate(spans) if low <= start)
        low = start - spans[at][0]
        outs = hidden_chunk(
            me, corr, (start, size), normed, grads, wp, mp_ax, vp_ax, wide[at], low, carried, after
        )
        splits = max(1, size // BLOCK)
        updates, carried = outs[:splits], list(outs[splits:])
        if i == 0:
            grads = carried.pop()
        project_pairs += [(updated, swap_gossip(updated, level)) for updated in updates]
        done = start + size
        while pending and sum(pending[0]) <= done:
            after = (project_pairs[1][1], expand_pairs[0][-1]) if len(pre) else ()
            *blocks, pre_g = expand_chunk(
                me, corr, pending.pop(0), turned, grads, wp, carried[2], count, after
            )
            pre.append(pre_g)
            expand_pairs.append(swap_blocks(blocks))
    first_project_next, second_project_next, _ = carried

    moments = None
    for i, span in enumerate(groups):
        last = i + 1 == len(groups)
        if last:
            done = tuple(pairs[0][0] for pairs in expand_pairs[:i])
            back = row_grads(me, pre, wide, spans, width, done)
            after = (project_pairs[-1][1], back[0])
        else:
            after = (project_pairs[2][1],)
        splits = 2 if last else 1
        last_blocks = expand_pairs[i][1:]
        outs = update_chunk(
            me, corr, span, we, me_ax, ve_ax, expand_pairs[i], splits, moments, after
        )
        moments = outs[splits:]
        expand_pairs[i] = [(updated, swap_gossip(updated, level)) for updated in outs[:splits]]
    first_expand_next, second_expand_next = moments

    back = list(back)
    back[1] = lax.optimization_barrier((back[1], expand_pairs[-1][-1][0]))[0]
    back[2:] = lax.optimization_barrier((*back[2:], *last_blocks))[: count - 2]
    back_pieces = swap_blocks(back)

    after = tuple(other for pairs in expand_pairs[:-1] for _, other in pairs)
    grad_conv, first_rows, last_rows = norm_back(
        gain, unit, inv, back_pieces, seqs, steps, after
    )
    forward = [(i, i + 1) for i in range(count - 1)]
    backward = [(target, source) for source, target in forward]
    low = lax.ppermute(last_rows, "fsdp", forward)
    high = lax.ppermute(first_rows, "fsdp", backward)
    shared_project = mean_project(project_pairs, ranges([p[0].shape[0] for p in project_pairs]))
    shared_expand = None
    for span, pairs in zip(groups[:-1], expand_pairs):
        for own, other in pairs:
            shared_expand = mean_expand(
                me, span, 0, own, other, hidden_width, owned, shared_expand, (grad_conv,)
            )
    after = (shared_project,) if shared_expand is None else (shared_project, shared_expand)
    input_grad = conv_back(depth_kernel, grad_conv, low, high, masked, seqs, after)
    lead = 0
    for own, other in expand_pairs[-1]:
        shared_expand = mean_expand(
            me, groups[-1], lead, own, other, hidden_width, owned, shared_expand, (input_grad,)
        )
        lead += own.shape[0]
    return (
        shared_expand[None],
        shared_project[None],
        first_expand_next[None],
        second_expand_next[None],
        first_project_next[None],
        second_project_next[None],
        input_grad[None],
    )


def body(*args):
    step_index = args[6]
    levels = lax.axis_size("gossip").bit_length() - 1
    return lax.switch(
        step_index[0] % levels,
        [lambda *a, level=level: step(*a, level) for level in range(levels)],
        *args,
    )


def solution(mesh):
    rows = P("gossip", "fsdp", None)
    steps = P("gossip", None, "fsdp", None)
    in_specs = (steps, steps, P("gossip", None, "fsdp"), P(), P(), P(), P()) + (rows,) * 6
    out_specs = (rows,) * 6 + (steps,)
    return jax.shard_map(body, mesh=mesh, in_specs=in_specs, out_specs=out_specs, check_vma=False)
```

```python
from functools import partial
import math

import jax
import jax.numpy as jnp
from jax import lax
from jax.experimental import pallas as pl
from jax.experimental.pallas import tpu as pltpu
from jax.sharding import PartitionSpec as P

NORM_EPS = 1e-06
ADAM_EPS = 1e-08
BETA_ONE = 0.9
BETA_TWO = 0.999
LEARN_RATE = 0.02
DECAY_RATE = 0.1
HALF_ROOT = 0.7071067811865476
INV_ROOT_TAU = 0.3989422804014327
PAD = 8
BLOCK = 256
EXPAND_UNROLL = True
F32 = jnp.float32
BF16 = jnp.bfloat16
MIB = 1 << 20


def dims(lhs, rhs):
    return (((lhs,), (rhs,)), ((), ()))


def dot(lhs, rhs, contract=(1, 0)):
    return lax.dot_general(lhs, rhs, dims(*contract), preferred_element_type=F32)


def whole(array):
    rank = len(array.shape)
    return pl.BlockSpec(array.shape, lambda *ids: (0,) * rank)


def hbm():
    return pl.BlockSpec(memory_space=pl.ANY)


def params(limit):
    return pltpu.CompilerParams(vmem_limit_bytes=limit)


def cost(moved=1):
    return pl.CostEstimate(flops=1, transcendentals=0, bytes_accessed=moved)


def loop(count, body, unroll=False):
    if count > 4 or not unroll:
        lax.fori_loop(0, count, lambda i, carry: (body(i), carry)[1], 0)
    else:
        for i in range(count):
            body(i)


def row_range(i, rows):
    return pl.ds(i * rows if isinstance(i, int) else pl.multiple_of(i * rows, rows), rows)


def ranges(sizes):
    starts = [sum(sizes[:i]) for i in range(len(sizes))]
    return list(zip(starts, sizes))


def plan(owned):
    if owned % 1024 == 0:
        q = owned // 4
        return ranges([q, q, 2 * q]), ranges([q, q, 2 * q]), ranges([2 * q, 2 * q])
    half = owned // 2
    return ranges([owned]), ranges([half, half]), ranges([owned])


def xor_perm(value, off):
    count = lax.axis_size("fsdp")
    return lax.ppermute(value, "fsdp", [(i, i ^ off) for i in range(count)])


def gather_xor(own, hold=()):
    count = lax.axis_size("fsdp")
    pieces = {0: own}
    bit = count // 2
    while bit:
        for off in list(pieces):
            value = pieces[off]
            if off and len(hold):
                value = lax.optimization_barrier((value, *hold))[0]
            pieces[off ^ bit] = xor_perm(value, bit)
        bit //= 2
    return [pieces[off] for off in range(count)]


def send_packs(packs):
    return [xor_perm(pack, 2 * h) if h else pack for h, pack in enumerate(packs)]


def relay_packs(packs, hold=()):
    held = []
    for h, pack in enumerate(packs):
        out = lax.optimization_barrier((pack, *hold))[0] if h and len(hold) else pack
        held += [pack, xor_perm(out, 1)]
    return held


def pieces_of(held, base, spans, k):
    return [(array, base + off % 2 * spans + k) for off, array in enumerate(held)]


def swap_blocks(blocks):
    return [block if off == 0 else xor_perm(block, off) for off, block in enumerate(blocks)]


def swap_gossip(value, level):
    count = lax.axis_size("gossip")
    return lax.ppermute(value, "gossip", [(i, i ^ (1 << level)) for i in range(count)])


def token_kernel(*refs):
    refs[-1][...] = jnp.zeros(refs[-1].shape, F32)


def token(values, name):
    shape = jax.ShapeDtypeStruct((8, 128), F32)
    return pl.pallas_call(
        token_kernel,
        out_shape=shape,
        in_specs=[hbm()] * len(values),
        out_specs=pl.BlockSpec(memory_space=pltpu.VMEM),
        compiler_params=params(MIB),
        cost_estimate=cost(40 * MIB),
        name=name,
    )(*values)


def slice_kernel(me_ref, *refs, count):
    outs = refs[-(count // 2) :]
    rows = refs[0].shape[0]
    for off in range(count):
        low = off % 2 * rows
        outs[off // 2][low : low + rows] = refs[off][...]


def slice_specs(rows, full, count, span):
    start, size = span
    ratio = full // count // size
    base = start // size
    return [
        pl.BlockSpec((rows, size), lambda i, me, off=off: (0, (me[0] ^ off) * ratio + base))
        for off in range(count)
    ]


def slice_weights(me, w, count, span):
    rows, full = w.shape
    shape = jax.ShapeDtypeStruct((2 * rows, span[1]), w.dtype)
    return pl.pallas_call(
        partial(slice_kernel, count=count),
        out_shape=[shape] * (count // 2),
        grid_spec=pltpu.PrefetchScalarGridSpec(
            num_scalar_prefetch=1,
            grid=(1,),
            in_specs=slice_specs(rows, full, count, span),
            out_specs=[whole(shape)] * (count // 2),
        ),
        compiler_params=params(16 * MIB),
        cost_estimate=cost(),
        name=f"slice_{span[0]}",
    )(me, *[w] * count)


def pack_kernel(me_ref, cot_ref, seen_ref, scale_ref, *refs, count):
    *outs, masked_ref = refs[-(count // 2) - 1 :]
    blocks = refs[: -(count // 2) - 1]
    spans = len(blocks) // count
    rows, width = cot_ref.shape
    part, size = blocks[0].shape
    panels = width // size
    tile = 16

    def body(i, carry):
        here = pl.ds(pl.multiple_of(i * tile, tile), tile)
        masked = (cot_ref[here].astype(F32) * seen_ref[here]).astype(BF16)
        masked_ref[here] = masked
        branch = (masked.astype(F32) * scale_ref[...]).astype(BF16)
        for out in outs:
            for p in range(panels):
                there = pl.ds(pl.multiple_of(p * rows + i * tile, tile), tile)
                out[there] = branch[:, p * size : (p + 1) * size]
        return carry

    lax.fori_loop(0, rows // tile, body, 0)
    for off in range(count):
        for k in range(spans):
            low = panels * rows + (off % 2 * spans + k) * part
            outs[off // 2][low : low + part] = blocks[k * count + off][...]


def pack_first(me, cot, seen, scale, w, count, spans):
    rows, width = cot.shape
    part, full = w.shape
    size = spans[0][1]
    shape = jax.ShapeDtypeStruct((width // size * rows + 2 * len(spans) * part, size), BF16)
    *packs, masked = pl.pallas_call(
        partial(pack_kernel, count=count),
        out_shape=[shape] * (count // 2) + [jax.ShapeDtypeStruct(cot.shape, BF16)],
        grid_spec=pltpu.PrefetchScalarGridSpec(
            num_scalar_prefetch=1,
            grid=(1,),
            in_specs=[whole(cot), whole(seen), whole(scale)]
            + [spec for span in spans for spec in slice_specs(part, full, count, span)],
            out_specs=[whole(shape)] * (count // 2) + [whole(cot)],
        ),
        compiler_params=params(24 * MIB),
        cost_estimate=cost(),
        name="pack_first",
    )(me, cot, seen, scale, *[w] * (count * len(spans)))
    return packs, masked


def norm_kernel(me_ref, taps_ref, gain_ref, *refs, count, tile):
    pieces = refs[:count]
    normed_ref, turned_ref, unit_ref, inv_ref, padded = refs[-5:]
    off = pl.program_id(0)
    seqs, steps, width = pieces[0].shape
    taps = taps_ref.shape[0]
    reach = taps // 2
    me = me_ref[0]

    @pl.when(off == 0)
    def _():
        edge = jnp.zeros((seqs, PAD, width), F32)
        padded[:, :PAD] = edge
        padded[:, PAD + count * steps :] = edge
        for other in range(count):
            start = pl.multiple_of((me ^ other) * steps + PAD, 8)
            padded[:, pl.ds(start, steps)] = pieces[other][...].astype(F32)

    def body(i, carry):
        s = i // (steps // tile)
        r = i % (steps // tile)
        base = pl.multiple_of((me ^ off) * steps + r * tile, 8)
        window = padded.at[s, pl.ds(base, tile + 2 * PAD)]
        conv = jnp.zeros((tile, width), F32)
        for j in range(taps):
            low = PAD + j - reach
            conv = conv + taps_ref[j : j + 1] * window[low : low + tile]
        centred = conv - jnp.mean(conv, axis=-1, keepdims=True)
        inv = lax.rsqrt(jnp.mean(centred * centred, axis=-1, keepdims=True) + NORM_EPS)
        unit = centred * inv
        rows = pl.ds(pl.multiple_of(i * tile, tile), tile)
        normed_ref[rows] = (unit * gain_ref[...]).astype(BF16)

        @pl.when(off == 0)
        def _():
            unit_ref[rows] = unit
            inv_ref[rows] = jnp.broadcast_to(inv, (tile, 128))

        return carry

    lax.fori_loop(0, seqs * steps // tile, body, 0)
    turned_ref[...] = normed_ref[...].T


def norm_rows(me, pieces, taps, gain, after):
    count = len(pieces)
    seqs, steps, width = pieces[0].shape
    rows = seqs * steps
    total = count * rows
    return pl.pallas_call(
        partial(norm_kernel, count=count, tile=math.gcd(steps, 64)),
        out_shape=[
            jax.ShapeDtypeStruct((total, width), BF16),
            jax.ShapeDtypeStruct((width, total), BF16),
            jax.ShapeDtypeStruct((rows, width), F32),
            jax.ShapeDtypeStruct((rows, 128), F32),
        ],
        grid_spec=pltpu.PrefetchScalarGridSpec(
            num_scalar_prefetch=1,
            grid=(count,),
            in_specs=[whole(taps), whole(gain)]
            + [whole(p) for p in pieces]
            + [hbm()] * len(after),
            out_specs=[
                pl.BlockSpec((rows, width), lambda i, m: (i, 0)),
                pl.BlockSpec((width, rows), lambda i, m: (0, i)),
                pl.BlockSpec((rows, width), lambda i, m: (0, 0)),
                pl.BlockSpec((rows, 128), lambda i, m: (0, 0)),
            ],
            scratch_shapes=[pltpu.VMEM((seqs, count * steps + 2 * PAD, width), F32)],
        ),
        compiler_params=params(18 * MIB + 14 * total * width // 2),
        cost_estimate=cost(40 * MIB),
        name="norm_rows",
    )(me, taps, gain, *pieces, *after)


def adam(weight, first, second, gradient, inv_one, inv_two):
    first_next = BETA_ONE * first + (1.0 - BETA_ONE) * gradient
    second_next = BETA_TWO * second + (1.0 - BETA_TWO) * gradient * gradient
    weight_f = weight.astype(F32)
    direction = first_next * inv_one / (jnp.sqrt(second_next * inv_two) + ADAM_EPS)
    updated = (weight_f - LEARN_RATE * (direction + DECAY_RATE * weight_f)).astype(BF16)
    return updated, first_next, second_next


def adam_tiles(w_ref, m_ref, v_ref, gradient, corr_ref, updated_ref, first_ref, second_ref, tile):
    def body(i, carry):
        rows = pl.ds(pl.multiple_of(i * tile, tile), tile)
        updated, first, second = adam(
            w_ref[rows], m_ref[rows], v_ref[rows], gradient(rows), corr_ref[0], corr_ref[1]
        )
        updated_ref[rows] = updated
        first_ref[rows] = first
        second_ref[rows] = second
        return carry

    lax.fori_loop(0, w_ref.shape[0] // tile, body, 0)


def join_rows(me, pieces, joined, columns=slice(None)):
    part = pieces[0].shape[0]
    for off, piece in enumerate(pieces):
        start = pl.multiple_of((me ^ off) * part, 16)
        joined[pl.ds(start, part), columns] = piece[...]


def hidden_kernel(
    me_ref, corr_ref, normed_ref, w_ref, m_ref, v_ref, *refs, count, first, splits
):
    wide = refs[:count]
    if first:
        packs = refs[count : 2 * count]
        *outs, first_ref, second_ref, slope_ref, grads_ref = refs[-splits - 7 : -3]
    else:
        grads_ref = refs[count]
        *outs, first_ref, second_ref, slope_ref = refs[-splits - 6 : -3]
    joined, total, updated = refs[-3:]
    join_rows(me_ref[0], wide, joined)
    width = normed_ref.shape[1]
    rows = normed_ref.shape[0] // count
    scale_in = 1.0 / math.sqrt(width)
    if first:
        size = packs[0].shape[1]
        for off in range(count):
            for p in range(width // size):
                grads_ref[off * rows : (off + 1) * rows, p * size : (p + 1) * size] = packs[off][
                    p * rows : (p + 1) * rows
                ]
    total[...] = jnp.zeros(total.shape, F32)

    def body(off):
        part = row_range(off, rows)
        pre = dot(normed_ref[part], joined[...]) * scale_in
        cumul = 0.5 * (1.0 + lax.erf(pre * HALF_ROOT))
        density = jnp.exp(-0.5 * pre * pre) * INV_ROOT_TAU
        hidden = (pre * cumul).astype(BF16)
        slope_ref[part] = (cumul + pre * density).astype(BF16)
        total[...] += dot(hidden, grads_ref[part], (0, 0))

    loop(count, body, True)
    adam_tiles(
        w_ref,
        m_ref,
        v_ref,
        lambda rows: total[rows] * corr_ref[2],
        corr_ref,
        updated if splits > 1 else outs[0],
        first_ref,
        second_ref,
        32,
    )
    for k in range(splits if splits > 1 else 0):

        @pl.when(pl.program_id(0) == k)
        def _():
            outs[k][...] = updated[...]


def hidden_chunk(me, corr, span, normed, grads, w, m, v, wide, low, previous, after):
    count = len(wide)
    total, width = normed.shape
    owned, part = w.shape[0], width // count
    start, size = span
    block = min(BLOCK, size)
    base = start // block
    splits = size // block
    rows = total // count
    row_block = pl.BlockSpec((block, width), lambda f, *_: (base + f, 0))
    arrays = [array for array, _ in wide]
    wide_specs = [
        pl.BlockSpec((part, block), lambda f, *_, lead=lead: (lead, low // block + f))
        for _, lead in wide
    ]
    if grads is None:
        spread = width // size * rows
        more = [pl.BlockSpec((spread, size), lambda f, *_: (0, 0))] * count
        extra = arrays
        out_grads = [jax.ShapeDtypeStruct((total, width), BF16)]
    else:
        more = [whole(grads)]
        extra = [grads]
        out_grads = []
    chained = previous is not None
    last = 6 + count + len(extra)
    return pl.pallas_call(
        partial(hidden_kernel, count=count, first=grads is None, splits=splits),
        out_shape=[jax.ShapeDtypeStruct((block, width), BF16)] * splits
        + [
            jax.ShapeDtypeStruct(m.shape, F32),
            jax.ShapeDtypeStruct(v.shape, F32),
            jax.ShapeDtypeStruct((total, owned), BF16),
        ]
        + out_grads,
        grid_spec=pltpu.PrefetchScalarGridSpec(
            num_scalar_prefetch=2,
            grid=(splits,),
            in_specs=[whole(normed), row_block, row_block, row_block]
            + wide_specs
            + more
            + ([hbm()] * 3 if chained else [])
            + [hbm()] * len(after),
            out_specs=[pl.BlockSpec((block, width), lambda f, *_: (0, 0))] * splits
            + [
                row_block,
                row_block,
                pl.BlockSpec((total, block), lambda f, *_: (0, base + f)),
            ]
            + [whole(g) for g in out_grads],
            scratch_shapes=[
                pltpu.VMEM((width, block), BF16),
                pltpu.VMEM((block, width), F32),
                pltpu.VMEM((block, width), BF16),
            ],
        ),
        input_output_aliases=(
            {last + j: splits + j for j in range(3)} if chained else {}
        ),
        compiler_params=params(20 * MIB + 5 * total * width * 2),
        cost_estimate=cost(),
        name=f"hidden_{start}",
    )(me, corr, normed, w, m, v, *arrays, *extra, *(previous or ()), *after)


def expand_kernel(me_ref, corr_ref, turned_ref, grads_ref, w_ref, slope_ref, *refs, count):
    *outs, pre_ref = refs[-count - 1 :]
    width = turned_ref.shape[0]
    rows = grads_ref.shape[0] // count
    scale_in = 1.0 / math.sqrt(width)

    def body(off):
        part = row_range(off, rows)
        back = dot(grads_ref[part], w_ref[...], (1, 1)) * corr_ref[2]
        pre_ref[part] = (back * slope_ref[part].astype(F32)).astype(BF16)

    loop(count, body, EXPAND_UNROLL)
    piece = width // count
    for off in range(count):
        start = pl.multiple_of((me_ref[0] ^ off) * piece, 16)
        block = dot(turned_ref[pl.ds(start, piece)], pre_ref[...]) * scale_in
        outs[off][...] = block.astype(BF16)


def expand_chunk(me, corr, span, turned, grads, w, slope, count, after):
    width, total = turned.shape
    start, size = span
    block = min(BLOCK, size)
    base = start // block
    piece = width // count
    return pl.pallas_call(
        partial(expand_kernel, count=count),
        out_shape=[jax.ShapeDtypeStruct((piece, size), BF16)] * count
        + [jax.ShapeDtypeStruct((total, size), BF16)],
        grid_spec=pltpu.PrefetchScalarGridSpec(
            num_scalar_prefetch=2,
            grid=(size // block,),
            in_specs=[
                whole(turned),
                whole(grads),
                pl.BlockSpec((block, width), lambda f, *_: (base + f, 0)),
                pl.BlockSpec((total, block), lambda f, *_: (0, base + f)),
            ]
            + [hbm()] * len(after),
            out_specs=[pl.BlockSpec((piece, block), lambda f, *_: (0, f))] * count
            + [pl.BlockSpec((total, block), lambda f, *_: (0, f))],
        ),
        compiler_params=params(20 * MIB + 5 * total * width * 2),
        cost_estimate=cost(),
        name=f"expand_{start}",
    )(me, corr, turned, grads, w, slope, *after)


def update_kernel(me_ref, corr_ref, w_ref, m_ref, v_ref, *refs, count, splits):
    pieces = refs[:count]
    *outs, first_ref, second_ref, held, updated = refs[-splits - 4 :]
    for off in range(count):

        @pl.when(pl.program_id(0) == off)
        def _():
            held[...] = pieces[off][...]

    adam_tiles(
        w_ref,
        m_ref,
        v_ref,
        lambda rows: held[rows].astype(F32),
        corr_ref,
        updated,
        first_ref,
        second_ref,
        48,
    )
    for h in range(splits):

        @pl.when(pl.program_id(0) // (count // splits) == h)
        def _():
            outs[h][0] = updated[...]


def update_chunk(me, corr, span, w, m, v, pieces, splits, previous, after):
    count = len(pieces)
    half = count // splits
    rows, size = pieces[0].shape
    start, _ = span
    ratio = w.shape[1] // count // size
    base = start // size
    column = pl.BlockSpec((rows, size), lambda i, me, *_: (0, (me[0] ^ i) * ratio + base))
    chained = previous is not None
    last = 5 + count
    return pl.pallas_call(
        partial(update_kernel, count=count, splits=splits),
        out_shape=[jax.ShapeDtypeStruct((half, rows, size), BF16)] * splits
        + [jax.ShapeDtypeStruct(m.shape, F32), jax.ShapeDtypeStruct(v.shape, F32)],
        grid_spec=pltpu.PrefetchScalarGridSpec(
            num_scalar_prefetch=2,
            grid=(count,),
            in_specs=[column, column, column]
            + [whole(p) for p in pieces]
            + ([hbm()] * 2 if chained else [])
            + [hbm()] * len(after),
            out_specs=[
                pl.BlockSpec(
                    (1, rows, size),
                    lambda i, *_, h=h: (jnp.clip(i - h * half, 0, half - 1).astype(jnp.int32), 0, 0),
                )
                for h in range(splits)
            ]
            + [column, column],
            scratch_shapes=[pltpu.VMEM((rows, size), BF16)] * 2,
        ),
        input_output_aliases={last: splits, last + 1: splits + 1} if chained else {},
        compiler_params=params(24 * MIB),
        cost_estimate=cost(),
        name=f"update_{start}",
    )(me, corr, w, m, v, *pieces, *(previous or ()), *after)


def mean_tiles(own_ref, other_ref, out_ref):
    rows = out_ref.shape[0]
    tile = math.gcd(rows, 16)

    def body(i, carry):
        part = pl.ds(pl.multiple_of(i * tile, tile), tile)
        value = (own_ref[part].astype(F32) + other_ref[part].astype(F32)) * 0.5
        out_ref[part] = value.astype(BF16)
        return carry

    lax.fori_loop(0, rows // tile, body, 0)


def mean_project_kernel(*refs, parts):
    out_ref = refs[-1]
    for i, (start, size) in enumerate(parts):
        mean_tiles(refs[2 * i], refs[2 * i + 1], out_ref.at[pl.ds(start, size)])


def mean_project(pairs, parts):
    flat = [x for pair in pairs for x in pair]
    shape = jax.ShapeDtypeStruct((sum(p[0].shape[0] for p in pairs), flat[0].shape[1]), BF16)
    return pl.pallas_call(
        partial(mean_project_kernel, parts=parts),
        out_shape=shape,
        grid=(1,),
        in_specs=[whole(x) for x in flat],
        out_specs=whole(shape),
        compiler_params=params(24 * MIB),
        cost_estimate=cost(),
        name="mean_project",
    )(*flat)


def mean_expand_kernel(me_ref, own_ref, other_ref, *refs):
    mean_tiles(own_ref.at[0], other_ref.at[0], refs[-1])


def mean_expand(me, span, lead, own, other, full, owned, previous, after):
    count, rows, size = own.shape
    ratio = owned // size
    base = span[0] // size
    in_spec = pl.BlockSpec((1, rows, size), lambda i, m: (i, 0, 0))
    chained = previous is not None
    return pl.pallas_call(
        mean_expand_kernel,
        out_shape=pltpu.HBM((rows, full), BF16),
        grid_spec=pltpu.PrefetchScalarGridSpec(
            num_scalar_prefetch=1,
            grid=(count,),
            in_specs=[in_spec, in_spec] + [hbm()] * (chained + len(after)),
            out_specs=pl.BlockSpec((rows, size), lambda i, m: (0, (m[0] ^ (i + lead)) * ratio + base)),
        ),
        input_output_aliases={3: 0} if chained else {},
        compiler_params=params(16 * MIB),
        cost_estimate=cost(),
        name=f"mean_expand_{span[0]}_{lead}",
    )(me, own, other, *((previous,) if chained else ()), *after)


def rows_kernel(me_ref, *refs, count, groups, parts):
    pre = refs[:groups]
    wide = refs[groups : groups + len(parts) * count]
    *outs, joined = refs[-count - 1 :]
    width = joined.shape[0]

    @pl.when(pl.program_id(0) == 0)
    def _():
        for i, (start, size) in enumerate(parts):
            pieces = wide[i * count : (i + 1) * count]
            join_rows(me_ref[0], pieces, joined, slice(start, start + size))

    total = None
    low = 0
    for piece in pre:
        size = piece.shape[1]
        term = dot(piece[...], joined[:, low : low + size], (1, 1))
        total = term if total is None else total + term
        low += size
    total = (total * (1.0 / math.sqrt(width))).astype(BF16)
    for off in range(count):

        @pl.when(pl.program_id(0) == off)
        def _():
            outs[off][...] = total


def row_grads(me, pre, wide, parts, width, after):
    count = len(wide[0])
    total = pre[0].shape[0]
    rows = total // count
    owned = sum(p.shape[1] for p in pre)
    flat = [piece for chunk in wide for piece in chunk]
    shapes = [jax.ShapeDtypeStruct((rows, width), BF16)] * count
    return pl.pallas_call(
        partial(rows_kernel, count=count, groups=len(pre), parts=parts),
        out_shape=shapes,
        grid_spec=pltpu.PrefetchScalarGridSpec(
            num_scalar_prefetch=1,
            grid=(count,),
            in_specs=[pl.BlockSpec((rows, p.shape[1]), lambda i, m: (i, 0)) for p in pre]
            + [
                pl.BlockSpec((width // count, x.shape[1]), lambda i, m, lead=lead: (lead, 0))
                for x, lead in flat
            ]
            + [hbm()] * len(after),
            out_specs=[whole(x) for x in shapes],
            scratch_shapes=[pltpu.VMEM((width, owned), BF16)],
        ),
        compiler_params=params(24 * MIB),
        cost_estimate=cost(),
        name="row_grads",
    )(me, *pre, *[x for x, _ in flat], *after)


def norm_back_kernel(gain_ref, unit_ref, inv_ref, *refs, count, steps, tile):
    pieces = refs[:count]
    conv_ref, first_ref, last_ref = refs[-3:]

    def body(i, carry):
        rows = pl.ds(pl.multiple_of(i * tile, tile), tile)
        total = pieces[0][rows].astype(F32)
        for piece in pieces[1:]:
            total = total + piece[rows].astype(F32)
        scaled = total * gain_ref[...]
        unit = unit_ref[rows]
        conv_ref[rows] = inv_ref[rows, :1] * (
            scaled
            - jnp.mean(scaled, axis=-1, keepdims=True)
            - unit * jnp.mean(scaled * unit, axis=-1, keepdims=True)
        )
        return carry

    lax.fori_loop(0, conv_ref.shape[0] // tile, body, 0)
    for s in range(first_ref.shape[0]):
        first_ref[s] = conv_ref[s * steps : s * steps + PAD].astype(BF16)
        last_ref[s] = conv_ref[(s + 1) * steps - PAD : (s + 1) * steps].astype(BF16)


def norm_back(gain, unit, inv, pieces, seqs, steps, after):
    count = len(pieces)
    width = unit.shape[1]
    edge = jax.ShapeDtypeStruct((seqs, PAD, width), BF16)
    full = jax.ShapeDtypeStruct((seqs * steps, width), F32)
    return pl.pallas_call(
        partial(norm_back_kernel, count=count, steps=steps, tile=32),
        out_shape=[full, edge, edge],
        grid=(1,),
        in_specs=[whole(gain), whole(unit), whole(inv)]
        + [whole(p) for p in pieces]
        + [hbm()] * len(after),
        out_specs=[whole(full), whole(edge), whole(edge)],
        compiler_params=params(32 * MIB),
        cost_estimate=cost(),
        name="norm_back",
    )(gain, unit, inv, *pieces, *after)


def conv_back_kernel(taps_ref, grad_ref, low_ref, high_ref, cot_ref, *refs, tile):
    out_ref, padded = refs[-2:]
    seqs, steps, width = out_ref.shape
    taps = taps_ref.shape[0]
    reach = taps // 2
    for s in range(seqs):
        padded[s, :PAD] = low_ref[s].astype(F32)
        padded[s, PAD + steps :] = high_ref[s].astype(F32)

    def fill(i, carry):
        s = i // (steps // tile)
        r = i % (steps // tile)
        rows = pl.ds(pl.multiple_of(i * tile, tile), tile)
        padded[s, pl.ds(pl.multiple_of(r * tile + PAD, 8), tile)] = grad_ref[rows]
        return carry

    def body(i, carry):
        s = i // (steps // tile)
        r = i % (steps // tile)
        rows = pl.ds(pl.multiple_of(r * tile, tile), tile)
        window = padded.at[s, pl.ds(pl.multiple_of(r * tile, 8), tile + 2 * PAD)]
        back = cot_ref[pl.ds(pl.multiple_of(i * tile, tile), tile)].astype(F32)
        for j in range(taps):
            low = PAD + reach - j
            back = back + taps_ref[j : j + 1] * window[low : low + tile]
        out_ref[s, rows] = back.astype(BF16)
        return carry

    lax.fori_loop(0, seqs * steps // tile, fill, 0)
    lax.fori_loop(0, seqs * steps // tile, body, 0)


def conv_back(taps, grad, low, high, cot, seqs, after):
    total, width = cot.shape
    steps = total // seqs
    shape = jax.ShapeDtypeStruct((seqs, steps, width), BF16)
    return pl.pallas_call(
        partial(conv_back_kernel, tile=32),
        out_shape=shape,
        grid=(1,),
        in_specs=[whole(x) for x in (taps, grad, low, high, cot)] + [hbm()] * len(after),
        out_specs=whole(shape),
        scratch_shapes=[pltpu.VMEM((seqs, steps + 2 * PAD, width), F32)],
        compiler_params=params(32 * MIB),
        cost_estimate=cost(),
        name="conv_back",
    )(taps, grad, low, high, cot, *after)


def step(
    series,
    cotangent,
    observed,
    depth_kernel,
    norm_gain,
    layer_scale,
    step_index,
    w_expand,
    w_project,
    first_expand,
    second_expand,
    first_project,
    second_project,
    level,
):
    count = lax.axis_size("fsdp")
    seqs, steps, width = series.shape[1:]
    rows = seqs * steps
    hidden_width = w_expand.shape[2]
    owned = hidden_width // count
    sent, parts, groups = plan(owned)
    me = lax.axis_index("fsdp").astype(jnp.int32).reshape(1)
    gain = norm_gain.reshape(1, width)
    we, wp = w_expand[0], w_project[0]
    me_ax, ve_ax = first_expand[0], second_expand[0]
    mp_ax, vp_ax = first_project[0], second_project[0]

    timestep = (step_index[0] + 1).astype(F32)
    corr = jnp.stack(
        [
            1.0 / (1.0 - jnp.power(F32(BETA_ONE), timestep)),
            1.0 / (1.0 - jnp.power(F32(BETA_TWO), timestep)),
            F32(1.0 / math.sqrt(hidden_width)),
        ]
    )

    part = width // count
    first_spans = [span for span in parts if sum(span) <= sum(sent[0])]
    spans = first_spans + list(sent[1:])
    seen = observed[0].reshape(rows, 1).astype(F32)
    cot = cotangent[0].reshape(rows, width)
    packs, masked = pack_first(
        me, cot, seen, layer_scale.reshape(1, width), we, count, first_spans
    )
    series_pieces = gather_xor(series[0], (packs[0],))
    normed, turned, unit, inv = norm_rows(me, series_pieces, depth_kernel, gain, ())
    base = width // parts[0][1] * rows // part
    held = relay_packs(send_packs(packs), (normed,))
    wide = [pieces_of(held, base, len(first_spans), k) for k in range(len(first_spans))]
    received = [send_packs(slice_weights(me, we, count, span)) for span in sent[1:]]

    project_pairs = []
    expand_pairs = []
    pre = []
    carried = None
    grads = None
    done = 0
    pending = list(groups)
    for i, (start, size) in enumerate(parts):
        if i == 0:
            after = ()
        elif i == 2:
            after = (token([project_pairs[0][1]], "first_arrived"), *pre)
        else:
            after = ()
        if i == len(wide):
            hold = (pre[-1] if pre else updates[0],)
            wide.append(pieces_of(relay_packs(received[i - len(first_spans)], hold), 0, 1, 0))
        at = max(j for j, (low, _) in enumerate(spans) if low <= start)
        low = start - spans[at][0]
        outs = hidden_chunk(
            me, corr, (start, size), normed, grads, wp, mp_ax, vp_ax, wide[at], low, carried, after
        )
        splits = max(1, size // BLOCK)
        updates, carried = outs[:splits], list(outs[splits:])
        if i == 0:
            grads = carried.pop()
        project_pairs += [(updated, swap_gossip(updated, level)) for updated in updates]
        done = start + size
        while pending and sum(pending[0]) <= done:
            after = (project_pairs[1][1], expand_pairs[0][-1]) if len(pre) else ()
            *blocks, pre_g = expand_chunk(
                me, corr, pending.pop(0), turned, grads, wp, carried[2], count, after
            )
            pre.append(pre_g)
            expand_pairs.append(swap_blocks(blocks))
    first_project_next, second_project_next, _ = carried

    moments = None
    for i, span in enumerate(groups):
        last = i + 1 == len(groups)
        if last:
            done = tuple(pairs[0][0] for pairs in expand_pairs[:i])
            back = row_grads(me, pre, wide, spans, width, done)
            after = (project_pairs[-1][1], back[0])
        else:
            after = (project_pairs[2][1],)
        splits = 2 if last else 1
        last_blocks = expand_pairs[i][1:]
        outs = update_chunk(
            me, corr, span, we, me_ax, ve_ax, expand_pairs[i], splits, moments, after
        )
        moments = outs[splits:]
        expand_pairs[i] = [(updated, swap_gossip(updated, level)) for updated in outs[:splits]]
    first_expand_next, second_expand_next = moments

    back = list(back)
    back[1] = lax.optimization_barrier((back[1], expand_pairs[-1][-1][0]))[0]
    back[2:] = lax.optimization_barrier((*back[2:], *last_blocks))[: count - 2]
    back_pieces = swap_blocks(back)

    after = tuple(other for pairs in expand_pairs[:-1] for _, other in pairs)
    grad_conv, first_rows, last_rows = norm_back(
        gain, unit, inv, back_pieces, seqs, steps, after
    )
    forward = [(i, i + 1) for i in range(count - 1)]
    backward = [(target, source) for source, target in forward]
    low = lax.ppermute(last_rows, "fsdp", forward)
    high = lax.ppermute(first_rows, "fsdp", backward)
    shared_project = mean_project(project_pairs, ranges([p[0].shape[0] for p in project_pairs]))
    shared_expand = None
    for span, pairs in zip(groups[:-1], expand_pairs):
        for own, other in pairs:
            shared_expand = mean_expand(
                me, span, 0, own, other, hidden_width, owned, shared_expand, (grad_conv,)
            )
    after = (shared_project,) if shared_expand is None else (shared_project, shared_expand)
    input_grad = conv_back(depth_kernel, grad_conv, low, high, masked, seqs, after)
    lead = 0
    for own, other in expand_pairs[-1]:
        shared_expand = mean_expand(
            me, groups[-1], lead, own, other, hidden_width, owned, shared_expand, (input_grad,)
        )
        lead += own.shape[0]
    return (
        shared_expand[None],
        shared_project[None],
        first_expand_next[None],
        second_expand_next[None],
        first_project_next[None],
        second_project_next[None],
        input_grad[None],
    )


def body(*args):
    step_index = args[6]
    levels = lax.axis_size("gossip").bit_length() - 1
    return lax.switch(
        step_index[0] % levels,
        [lambda *a, level=level: step(*a, level) for level in range(levels)],
        *args,
    )


def solution(mesh):
    rows = P("gossip", "fsdp", None)
    steps = P("gossip", None, "fsdp", None)
    in_specs = (steps, steps, P("gossip", None, "fsdp"), P(), P(), P(), P()) + (rows,) * 6
    out_specs = (rows,) * 6 + (steps,)
    return jax.shard_map(body, mesh=mesh, in_specs=in_specs, out_specs=out_specs, check_vma=False)
```
